32 devices in a mesh: mem: 8 (over z, y), lat: 4 (over x, core).
Axes of the slice: x: 2, y: 2, z: 4, core: 2. Of those that a mesh axis runs over, the one named last changes fastest.
Arguments:
- control: float32 [16, 4, 64, 1024], P('mem', None, 'lat'), may hold values from -6 to 6
- perturbations: bfloat16 [4, 2, 16, 4, 64, 1024], P(None, None, 'mem', None, 'lat'), may hold values from -3 to 3
- obs_weight: float32 [8, 2, 4, 64, 1024], P('mem', None, None, 'lat'), may hold values from 0.2 to 5
- slot_owner: int32 [4], replicated, may hold values from 0 to 7, as said below
- zonal_shift: int32 [64], P('lat'), may hold values from 0 to 1023
- zonal_taps: float32 [64, 17], P('lat'), may hold values from 0.05 to 0.5
- meridional_taps: float32 [64, 17], P('lat'), may hold values from 0.05 to 0.5
- level_mixing: float32 [64, 4, 4], P('lat'), may hold values from -3 to 3
Outputs:
- applied: float32 [16, 4, 64, 1024], P('mem', None, 'lat')
The draws below stay inside these ranges and needn't reach their ends.
Inputs may be any that keep to these rules, and one draw needn't show every extreme that they name: `slot_owner`: the 4 entries are distinct; index 0 and index 8 - 1 of mem are always among them.
All inputs are finite; a program needn't handle non-finite values.
Results may differ from the reference program's by a relative error of at most 0.0003.
Values sent between devices are 32-bit elements; how exact they have to be, the bound alone decides.
No kernel may reach another device: no remote copies, remote signals or barrier semaphores. Data moves between devices by JAX's collectives and lax.ppermute only.
A program may use at most 64 MiB of HBM per device.

```python
import math
import jax
import jax.numpy as jnp
from jax import lax

SLOTS = 4
FIELDS = 2
LEV = 4
LON = 1024
BAND = 17
MEMBERS = 16
NLAT = 64
N_MEM = 8


def draw_slot_owner(key, part):
    middle = jax.random.permutation(jax.random.fold_in(key, 11), N_MEM - 2)[:SLOTS - 2].astype(jnp.int32) + 1
    chosen = jnp.concatenate([jnp.array([0, N_MEM - 1], jnp.int32), middle])
    arrangement = jax.random.permutation(jax.random.fold_in(key, 12), SLOTS)
    return chosen[arrangement].astype(jnp.int32)


def set_ends(values, stream_key, least, top_value):
    extent = values.shape
    place = [jax.random.randint(jax.random.fold_in(stream_key, axis), (), 0, extent[axis]) for axis in range(len(extent))]
    values = values.at[tuple(place)].set(least)
    longest = extent.index(max(extent))
    place[longest] = (place[longest] + 1) % extent[longest]
    return values.at[tuple(place)].set(top_value)


def shard_levels(own_key, extent, cuts, low, largest):
    gain, own = 1.0, jax.random.fold_in(own_key, 6)
    for position, blocks in cuts:
        heights = jnp.exp(jax.random.uniform(jax.random.fold_in(own, position), (blocks,), jnp.float32, low / len(cuts), largest / len(cuts)))
        gain = gain * jnp.repeat(heights, extent[position] // blocks).reshape([-1 if axis == position else 1 for axis in range(len(extent))])
    return gain


def scatter_about(key, extent, width, bound, shards=(), kind=jnp.bfloat16):
    values = width * jax.random.normal(key, extent, jnp.float32)
    if shards:
        values = values * shard_levels(key, extent, shards, -0.22, 0.18)
    return jnp.clip(values, -bound, bound).astype(kind)


def setup_inputs(seed: int = 0) -> dict:
    streams_of = jax.random.split(jax.random.key(seed), 9)
    return {
        "control": scatter_about(streams_of[0], (MEMBERS, LEV, NLAT, LON), 1.0, 6.0, ((0, 8), (2, 4)), jnp.float32),
        "perturbations": scatter_about(streams_of[1], (SLOTS, FIELDS, MEMBERS, LEV, NLAT, LON), (MEMBERS // 4) ** -0.5, 3.0, ((2, 8), (4, 4))),
        "obs_weight": jnp.clip(jnp.exp(math.log(5.0) - 3.218876 * jax.random.uniform(streams_of[2], (N_MEM, FIELDS, LEV, NLAT, LON), jnp.float32) ** shard_levels(streams_of[2], (N_MEM, FIELDS, LEV, NLAT, LON), ((0, 8), (3, 4)), -0.2, 0.2)), 0.2, 5.0),
        "slot_owner": draw_slot_owner(jax.random.fold_in(streams_of[8], 71), 0),
        "zonal_shift": set_ends(jax.random.randint(streams_of[4], (NLAT,), 0, LON), jax.random.fold_in(streams_of[4], 1), 0, LON - 1).astype(jnp.int32),
        "zonal_taps": jnp.clip(jnp.exp(math.log(0.5) - 2.3025851 * jax.random.uniform(streams_of[5], (NLAT, BAND), jnp.float32) ** shard_levels(streams_of[5], (NLAT, BAND), ((0, 4),), -0.2, 0.2)), 0.05, 0.5),
        "meridional_taps": jnp.clip(jnp.exp(math.log(0.5) - 2.3025851 * jax.random.uniform(streams_of[6], (NLAT, BAND), jnp.float32) ** shard_levels(streams_of[6], (NLAT, BAND), ((0, 4),), -0.2, 0.2)), 0.05, 0.5),
        "level_mixing": scatter_about(streams_of[7], (NLAT, LEV, LEV), 0.5, 3.0, ((0, 4),), jnp.float32),
    }


def zonal_apply(field, shifts, taps, direction):
    columns = jnp.arange(LON, dtype=jnp.int32)
    row_number = jnp.arange(field.shape[2], dtype=jnp.int32)[:, None]
    result = jnp.zeros(field.shape, jnp.float32)
    for tap_number in range(BAND):
        moved = (columns[None, :] + direction * (shifts[:, None] + tap_number - BAND // 2)) % LON
        result = result + taps[:, tap_number][:, None] * field[:, :, row_number, moved]
    return result


def meridional_forward(field, taps):
    half_band = BAND // 2
    band_rows = field.shape[2]
    padded = jnp.pad(field, ((0, 0), (0, 0), (half_band, half_band), (0, 0)))
    result = jnp.zeros(field.shape, jnp.float32)
    for tap_number in range(BAND):
        result = result + taps[:, tap_number][:, None] * padded[:, :, tap_number:tap_number + band_rows, :]
    return result


def meridional_adjoint(field, taps):
    half_band = BAND // 2
    band_rows = field.shape[2]
    result = jnp.zeros(field.shape, jnp.float32)
    for tap_number in range(BAND):
        scaled = taps[:, tap_number][:, None] * field
        padded = jnp.pad(scaled, ((0, 0), (0, 0), (half_band, half_band), (0, 0)))
        begin = 2 * half_band - tap_number
        result = result + padded[:, :, begin:begin + band_rows, :]
    return result


def reference(control, perturbations, obs_weight, slot_owner, zonal_shift, zonal_taps, meridional_taps, level_mixing):
    highest_mode = lax.Precision.HIGHEST
    section = zonal_apply(control, zonal_shift, zonal_taps, 1)
    section = meridional_forward(section, meridional_taps)
    localized = jnp.einsum("jab,mbjx->majx", level_mixing, section, precision=highest_mode)
    weighted = jnp.zeros(control.shape, jnp.float32)
    for slot_number in range(SLOTS):
        owner_weight = obs_weight[slot_owner[slot_number]]
        for field_number in range(FIELDS):
            members = perturbations[slot_number, field_number].astype(jnp.float32)
            increment = jnp.sum(members * localized, axis=0)
            gradient = owner_weight[field_number] * increment
            weighted = weighted + members * gradient[None]
    back = jnp.einsum("jab,majx->mbjx", level_mixing, weighted, precision=highest_mode)
    back = meridional_adjoint(back, meridional_taps)
    back = zonal_apply(back, zonal_shift, zonal_taps, -1)
    return control + back
```

```python
import functools

import jax
import jax.numpy as jnp
from jax import lax
from jax.experimental import pallas as pl
from jax.experimental.pallas import tpu as pltpu
from jax.sharding import PartitionSpec as P

SLOTS = 4
BAND = 17
HALF = BAND // 2
LANES = 128
F32 = jnp.float32
BF16 = jnp.bfloat16

VMEM = pl.BlockSpec(memory_space=pltpu.VMEM)
SMEM = pl.BlockSpec(memory_space=pltpu.SMEM)

PARITY, HAS_X, OWN_Y, WEIGHT_FROM, SLOT = 0, 1, 2, 3, 4
TABLE = 8


def call(body, outs, name, cost, *operands, specs, scratch=()):
    return pl.pallas_call(
        body,
        out_shape=outs,
        in_specs=list(specs),
        out_specs=jax.tree.map(lambda _: VMEM, outs),
        scratch_shapes=list(scratch),
        compiler_params=pltpu.CompilerParams(vmem_limit_bytes=48 << 20),
        cost_estimate=pl.CostEstimate(flops=cost, bytes_accessed=cost, transcendentals=0),
        name=name,
    )(*operands)


def shape(*dims, dtype=F32):
    return jax.ShapeDtypeStruct(dims, dtype)


def shifted(columns, amount):
    lane = lax.broadcasted_iota(jnp.int32, columns[0].shape, 1)
    turned = [pltpu.roll(c, amount, 1) for c in columns]
    return [
        jnp.where(lane < amount, turned[i - 1], turned[i]) for i in range(len(columns))
    ]


def circle_filter(columns, amount, tap):
    count = len(columns)
    lane = lax.broadcasted_iota(jnp.int32, columns[0].shape, 1)
    fine = amount & (LANES - 1)
    source = (lane - fine) & (LANES - 1)
    turned = [
        jnp.take_along_axis(c, source, axis=1, mode="promise_in_bounds") for c in columns
    ]
    wraps = lane < fine
    columns = [jnp.where(wraps, turned[i - 1], turned[i]) for i in range(count)]
    step = 1
    while step < count:
        moved = (amount & (step * LANES)) != 0
        columns = [jnp.where(moved, columns[i - step], columns[i]) for i in range(count)]
        step *= 2
    near = [columns]
    for offset in range(1, 4):
        near.append(shifted(columns, offset))
    total = [tap(BAND - 1) * c for c in columns]
    for group in range((BAND - 1) // 4 - 1, -1, -1):
        total = shifted(total, 4)
        for offset in range(4):
            factor = tap(4 * group + offset)
            total = [t + factor * c for t, c in zip(total, near[offset])]
    return total


def row_shifts(shift_ref, first):
    row = lax.broadcasted_iota(jnp.int32, (8, LANES), 0)
    amounts = jnp.zeros((8, LANES), jnp.int32)
    for r in range(8):
        amounts = jnp.where(row == r, shift_ref[first + r], amounts)
    return amounts


def spread_taps(taps_ref, first, tap_ref):
    block = taps_ref[pl.ds(first, 8), :]
    for k in range(BAND):
        tap_ref[k] = jnp.broadcast_to(block[:, k : k + 1], (8, LANES))


def tiles(width):
    return [slice(i * LANES, (i + 1) * LANES) for i in range(width // LANES)]


def zonal_forward(table, shift_ref, taps_ref, control, near_core, near_x, tap_ref):
    members, levels, _, width = control.shape
    for which, out in enumerate((near_core, near_x)):
        first = pl.multiple_of((1 - table[PARITY] if which == 0 else table[PARITY]) * 8, 8)
        amount = (width - HALF - row_shifts(shift_ref, first)) & (width - 1)
        spread_taps(taps_ref, first, tap_ref)

        def step(unit, carry, out=out, first=first, amount=amount):
            m, l = unit // levels, unit % levels
            columns = [control[m, l, pl.ds(first, 8), cut] for cut in tiles(width)]
            result = circle_filter(columns, amount, lambda k: tap_ref[BAND - 1 - k])
            for cut, value in zip(tiles(width), result):
                out[m, l, :, cut] = value
            return carry

        lax.fori_loop(0, members * levels, step, 0)


def zonal_adjoint(
    table, shift_ref, taps_ref, control, own_core, own_x, got_core, got_x, out, tap_ref
):
    members, levels, _, width = control.shape
    for which, (own, got) in enumerate(((own_core, got_core), (own_x, got_x))):
        first = pl.multiple_of((1 - table[PARITY] if which == 0 else table[PARITY]) * 8, 8)
        amount = (row_shifts(shift_ref, first) - HALF) & (width - 1)
        spread_taps(taps_ref, first, tap_ref)

        def step(unit, carry, own=own, got=got, first=first, amount=amount):
            m, l = unit // levels, unit % levels
            columns = [own[m, l, :, cut] + got[m, l, :, cut] for cut in tiles(width)]
            result = circle_filter(columns, amount, lambda k: tap_ref[k])
            for cut, value in zip(tiles(width), result):
                out[m, l, pl.ds(first, 8), cut] = control[m, l, pl.ds(first, 8), cut] + value
            return carry

        lax.fori_loop(0, members * levels, step, 0)


def build_matrix(table, taps_ref, mixing_ref, matrix, transposed):
    band_rows, levels = taps_ref.shape[0], mixing_ref.shape[1]
    rows, columns = matrix.shape
    odd = table[PARITY]
    column = lax.broadcasted_iota(jnp.int32, (band_rows, columns), 1)
    row = lax.broadcasted_iota(jnp.int32, (band_rows, columns), 0)
    block, level, inner = column // (8 * levels), (column // 8) % levels, column % 8
    even_start = jnp.where(block == 0, 16, jnp.where(block == 1, 8, jnp.where(block == 2, 24, 0)))
    odd_start = jnp.where(block == 0, 8, jnp.where(block == 1, 16, jnp.where(block == 2, 0, 24)))
    reach = jnp.where(odd == 1, odd_start, even_start) + inner - row
    band = jnp.zeros((band_rows, columns), F32)
    for k in range(BAND):
        band = jnp.where(reach == k, taps_ref[:, k : k + 1], band)
    band = jnp.where((block == 3) & (table[HAS_X] == 0), 0.0, band)
    for a in range(levels):
        mixing = mixing_ref[a * band_rows : (a + 1) * band_rows, :]
        factor = jnp.zeros((band_rows, columns), F32)
        for b in range(levels):
            factor = jnp.where(level == b, mixing[:, b : b + 1], factor)
        matrix[a * band_rows : (a + 1) * band_rows, :] = factor * band
    transposed[...] = matrix[...].T


def halves(value):
    high = value.astype(BF16)
    return high, (value - high.astype(F32)).astype(BF16)


def product(left, right):
    (lh, ll), (rh, rl) = left, right
    dot = functools.partial(jnp.dot, preferred_element_type=F32)
    return dot(lh, rh) + (dot(lh, rl) + dot(ll, rh))


CHUNK = 256


def localize(matrix, parts, out):
    members, levels, band_rows, width = out.shape
    left = halves(matrix[...])
    for m in range(members):
        for c in range(0, width, CHUNK):
            cut = slice(c, c + CHUNK)
            stack = jnp.concatenate(
                [p[m, l, :, cut] for p in parts for l in range(levels)], axis=0
            )
            result = product(left, halves(stack))
            for l in range(levels):
                out[m, l, :, cut] = result[l * band_rows : (l + 1) * band_rows]


def delocalize(matrix, weighted, parts):
    members, levels, band_rows, width = weighted.shape
    left = halves(matrix[...])
    for m in range(members):
        for c in range(0, width, CHUNK):
            cut = slice(c, c + CHUNK)
            stack = jnp.concatenate([weighted[m, l, :, cut] for l in range(levels)], axis=0)
            result = product(left, halves(stack))
            for p, part in enumerate(parts):
                for l in range(levels):
                    start = (p * levels + l) * 8
                    part[m, l, :, cut] = result[start : start + 8]


def increment(ens, localized, slot, field, l):
    total = None
    for m in range(localized.shape[0]):
        term = ens[slot, field, m, l].astype(F32) * localized[m, l]
        total = term if total is None else total + term
    return total


def first_body(step, table, matrix, a, b, c, d, ens, localized, send):
    localize(matrix, (a, b, c, d), localized)
    for l in range(localized.shape[1]):
        send[l] = increment(ens, localized, table[SLOT + step], 1 - table[OWN_Y], l)


def send_body(steps, table, ens, localized, *sends):
    for step, send in zip(steps, sends):
        for l in range(localized.shape[1]):
            send[l] = increment(ens, localized, table[SLOT + step], 1 - table[OWN_Y], l)


def meet_body(step, table, ens, localized, got, out):
    for l in range(localized.shape[1]):
        out[l] = increment(ens, localized, table[SLOT + step], table[OWN_Y], l) + got[l]


def last_body(table, ens, localized, got_y, got_1, got_2, got_3, own, from_y, from_low, from_high, out):
    for l in range(localized.shape[1]):
        out[l] = (
            increment(ens, localized, table[SLOT], table[OWN_Y], l)
            + got_y[l]
            + (got_1[l] + got_2[l] + got_3[l])
        )
    source = table[WEIGHT_FROM]

    @pl.when(source == 0)
    def _():
        out[...] = out[...] * own[0, table[OWN_Y]]

    for code, weight in ((1, from_y), (2, from_low), (3, from_high)):

        @pl.when(source == code)
        def _(weight=weight):
            out[...] = out[...] * weight[...]


def spread_body(pieces, first, final, table, ens, *refs):
    refs = list(refs)
    grads = [refs.pop(0) for _ in pieces]
    before = None if first else refs.pop(0)
    matrix = refs.pop(0) if final else None
    out = refs[-1] if final else refs[0]
    members, levels = out.shape[:2]
    for m in range(members):
        for l in range(levels):
            total = None if before is None else before[m, l]
            for (step, other), grad in zip(pieces, grads):
                field = 1 - table[OWN_Y] if other else table[OWN_Y]
                term = ens[table[SLOT + step], field, m, l].astype(F32) * grad[l]
                total = term if total is None else total + term
            out[m, l] = total
    if final:
        delocalize(matrix, out, refs[:4])


def all_increments(ens, localized, out):
    for slot in range(out.shape[0]):
        for field in range(out.shape[1]):
            for l in range(out.shape[2]):
                out[slot, field, l] = increment(ens, localized, slot, field, l)


def localize_body(matrix, a, b, c, d, localized):
    localize(matrix, (a, b, c, d), localized)


def all_weighted(ens, grad, matrix, a, b, c, d, out):
    members, levels = out.shape[:2]
    for m in range(members):
        for l in range(levels):
            total = None
            for slot in range(ens.shape[0]):
                for field in range(ens.shape[1]):
                    term = ens[slot, field, m, l].astype(F32) * grad[slot, field, l]
                    total = term if total is None else total + term
            out[m, l] = total
    delocalize(matrix, out, (a, b, c, d))


def per_device(
    z_count,
    control,
    perturbations,
    obs_weight,
    slot_owner,
    zonal_shift,
    zonal_taps,
    meridional_taps,
    level_mixing,
):
    members, levels, band_rows, width = control.shape
    mem_count, lat_count = lax.axis_size("mem"), lax.axis_size("lat")
    lat, mem = lax.axis_index("lat"), lax.axis_index("mem")
    parity = lat % 2
    has_x = jnp.where((lat > 0) & (lat < lat_count - 1), 1, 0)
    direct = z_count > 0
    field_shape = (members, levels, band_rows, width)
    half_shape = (members, levels, 8, width)
    core_pairs = [(i, i ^ 1) for i in range(lat_count)]
    x_pairs = [(i, i + 1) for i in range(1, lat_count - 1, 2)]
    x_pairs += [(j, i) for i, j in x_pairs]
    swap_core = lambda v: lax.ppermute(v, "lat", core_pairs)
    swap_x = lambda v: lax.ppermute(v, "lat", x_pairs)

    z, y = mem // 2, mem % 2
    if direct:
        rank = jnp.sum((slot_owner[None, :] < slot_owner[:, None]).astype(jnp.int32), axis=1)
        place = (z + jnp.arange(SLOTS, dtype=jnp.int32)) % SLOTS
        at_place = (rank[None, :] == place[:, None]).astype(jnp.int32)
        slots = jnp.sum(at_place * jnp.arange(SLOTS, dtype=jnp.int32)[None, :], axis=1)
        owners = jnp.sum(at_place * slot_owner[None, :], axis=1)
        own_z, own_y = owners[0] // 2, owners[0] % 2
        source = jnp.where(
            own_z == z, jnp.where(own_y == y, 0, 1), jnp.where(own_z < z, 2, 3)
        )
    else:
        slots, source = jnp.arange(SLOTS, dtype=jnp.int32), jnp.int32(0)
    table = jnp.concatenate(
        [jnp.stack([parity, has_x, y, source]).astype(jnp.int32), slots]
    )

    if direct:
        y_pairs = [(i, i ^ 1) for i in range(mem_count)]
        swap_y = lambda v: lax.ppermute(v, "mem", y_pairs)
        turn_z = lambda v, s: lax.ppermute(
            v, "mem", [(i, (i + 2 * s) % mem_count) for i in range(mem_count)]
        )
        weight_y = swap_y(lax.dynamic_index_in_dim(obs_weight[0], 1 - y, 0, False))

    near_core, near_x = call(
        zonal_forward, (shape(*half_shape),) * 2, "zonal", 1 << 20,
        table, zonal_shift, zonal_taps, control,
        specs=(SMEM, SMEM, VMEM, VMEM), scratch=[pltpu.VMEM((BAND, 8, LANES), F32)],
    )
    far_core, far_x = swap_core(near_core), swap_x(near_x)
    mixing = jnp.transpose(level_mixing, (1, 0, 2)).reshape(levels * band_rows, levels)
    matrix, transposed = call(
        build_matrix,
        (shape(levels * band_rows, 32 * levels), shape(32 * levels, levels * band_rows)),
        "matrix", 1 << 16, table, meridional_taps, mixing, specs=(SMEM, VMEM, VMEM),
    )
    parts = (near_core, near_x, far_core, far_x)
    piece = shape(levels, band_rows, width)

    if direct:
        order = (2, 1, 3)
        localized, first = call(
            functools.partial(first_body, order[0]), (shape(*field_shape), piece),
            "first", 1 << 20, table, matrix, *parts, perturbations,
            specs=(SMEM,) + (VMEM,) * 6,
        )
        sent = {order[0]: first}
        rest = order[1:] + (0,)
        others = call(
            functools.partial(send_body, rest), (piece,) * len(rest), "send", 1 << 20,
            table, perturbations, localized, specs=(SMEM, VMEM, VMEM),
        )
        sent.update(zip(rest, others))
        got = {s: swap_y(sent[s]) for s in order + (0,)}
        own_weight = lax.dynamic_index_in_dim(obs_weight[0], y, 0, False)
        up = jnp.where(owners[1] % 2 == y, own_weight, weight_y)
        down = jnp.where(owners[3] % 2 == y, own_weight, weight_y)
        ends = z_count - 1
        raised = [(2 * i + j, 2 * i + 2 + j) for i in range(ends - 1) for j in range(2)]
        lowered = [(2 * i + 2 + j, 2 * i + j) for i in range(1, ends) for j in range(2)]
        from_low = lax.ppermute(up, "mem", raised)
        from_high = lax.ppermute(down, "mem", lowered)
        arrived = {}
        for s in order:
            total = call(
                functools.partial(meet_body, s), piece, "meet%d" % s, 1 << 19,
                table, perturbations, localized, got[s], specs=(SMEM,) + (VMEM,) * 3,
            )
            arrived[s] = turn_z(total, s)
        grad = call(
            last_body, piece, "last", 1 << 19, table, perturbations, localized, got[0],
            arrived[1], arrived[2], arrived[3], obs_weight, weight_y, from_low, from_high,
            specs=(SMEM,) + (VMEM,) * 10,
        )
        own = {0: grad}
        for s in order:
            own[s] = turn_z(grad, s)
        other = {s: swap_y(own[s]) for s in (0,) + order}
        back = lambda s: (-s) % SLOTS
        weighted = None
        for group in (((0, 0),), ((0, 1), (2, 0)), ((1, 0), (2, 1)), ((3, 0), (1, 1)), ((3, 1),)):
            final = group == ((3, 1),)
            grads = [other[s] if o else own[s] for s, o in group]
            pieces = tuple((back(s), o) for s, o in group)
            before = () if weighted is None else (weighted,)
            extra = (transposed,) if final else ()
            result = call(
                functools.partial(spread_body, pieces, weighted is None, final),
                (shape(*half_shape),) * 4 + (shape(*field_shape),) if final else shape(*field_shape),
                "spread%d" % group[0][0], 1 << 19,
                table, perturbations, *grads, *before, *extra,
                specs=(SMEM,) + (VMEM,) * (1 + len(grads) + len(before) + len(extra)),
            )
            weighted = result
        own_core, own_x, to_core, to_x = result[:4]
    else:
        localized = call(
            localize_body, shape(*field_shape), "localize", 1 << 20, matrix, *parts,
            specs=(VMEM,) * 5,
        )
        partial = call(
            all_increments, shape(SLOTS, perturbations.shape[1], levels, band_rows, width),
            "increments", 1 << 20, perturbations, localized, specs=(VMEM,) * 2,
        )
        weights = jnp.stack(
            [
                lax.psum(jnp.where(mem == slot_owner[t], obs_weight[0], 0.0), "mem")
                for t in range(SLOTS)
            ]
        )
        share = lax.psum_scatter(
            partial.reshape(-1, width), "mem", scatter_dimension=0, tiled=True
        )
        share_rows = share.shape[0]
        weight_rows = lax.dynamic_slice_in_dim(
            weights.reshape(-1, width), mem * share_rows, share_rows, 0
        )
        gathered = lax.all_gather(weight_rows * share, "mem", axis=0, tiled=True)
        own_core, own_x, to_core, to_x, _ = call(
            all_weighted, (shape(*half_shape),) * 4 + (shape(*field_shape),), "weighted",
            1 << 20, perturbations, gathered.reshape(partial.shape), transposed,
            specs=(VMEM,) * 3,
        )
    got_core, got_x = swap_core(to_core), swap_x(to_x)
    return call(
        zonal_adjoint, shape(*field_shape), "zonal_adjoint", 1 << 20,
        table, zonal_shift, zonal_taps, control, own_core, own_x, got_core, got_x,
        specs=(SMEM, SMEM) + (VMEM,) * 6, scratch=[pltpu.VMEM((BAND, 8, LANES), F32)],
    )


def solution(mesh):
    z_count = SLOTS if mesh.shape["mem"] == 2 * SLOTS else 0
    in_specs = (
        P("mem", None, "lat", None),
        P(None, None, "mem", None, "lat", None),
        P("mem", None, None, "lat", None),
        P(),
        P("lat"),
        P("lat", None),
        P("lat", None),
        P("lat", None, None),
    )
    out_specs = P("mem", None, "lat", None)
    return jax.shard_map(
        functools.partial(per_device, z_count),
        mesh=mesh, in_specs=in_specs, out_specs=out_specs, check_vma=False,
    )
```

```python
import functools

import jax
import jax.numpy as jnp
from jax import lax
from jax.experimental import pallas as pl
from jax.experimental.pallas import tpu as pltpu
from jax.sharding import PartitionSpec as P

SLOTS = 4
BAND = 17
HALF = BAND // 2
LANES = 128
F32 = jnp.float32
BF16 = jnp.bfloat16

VMEM = pl.BlockSpec(memory_space=pltpu.VMEM)
SMEM = pl.BlockSpec(memory_space=pltpu.SMEM)
ANY = pl.BlockSpec(memory_space=pl.ANY)


def call(body, outs, name, cost, *operands, specs, scratch=(), after=()):
    count, extra = len(operands), len(after)

    def kernel(*refs):
        body(*refs[:count], *refs[count + extra :])

    return pl.pallas_call(
        kernel,
        out_shape=outs,
        in_specs=list(specs) + [ANY] * extra,
        out_specs=jax.tree.map(lambda _: VMEM, outs),
        scratch_shapes=list(scratch),
        compiler_params=pltpu.CompilerParams(vmem_limit_bytes=16 << 20),
        cost_estimate=pl.CostEstimate(flops=cost, bytes_accessed=cost, transcendentals=0),
        name=name,
    )(*operands, *after)


def parity():
    return lax.axis_index("lat") & 1


def own_y():
    return lax.axis_index("mem") & 1


def own_z():
    return lax.axis_index("mem") >> 1


def entry_at(owners, step, value):
    place = (own_z() + step) & (SLOTS - 1)
    found = jnp.int32(0)
    for t in range(SLOTS):
        rank = jnp.int32(0)
        for u in range(SLOTS):
            if u != t:
                rank += jnp.where(owners[u] < owners[t], 1, 0)
        found = jnp.where(rank == place, value(t), found)
    return found


def slot_at(owners, step):
    return entry_at(owners, step, lambda t: jnp.int32(t))


def owner_at(owners, step):
    return entry_at(owners, step, lambda t: owners[t])


def shape(*dims, dtype=F32):
    return jax.ShapeDtypeStruct(dims, dtype)


def shifted(columns, amount):
    lane = lax.broadcasted_iota(jnp.int32, columns[0].shape, 1)
    turned = [pltpu.roll(c, amount, 1) for c in columns]
    return [
        jnp.where(lane < amount, turned[i - 1], turned[i]) for i in range(len(columns))
    ]


def circle_filter(columns, amount, tap):
    count = len(columns)
    lane = lax.broadcasted_iota(jnp.int32, columns[0].shape, 1)
    fine = amount & (LANES - 1)
    source = (lane - fine) & (LANES - 1)
    turned = [
        jnp.take_along_axis(c, source, axis=1, mode="promise_in_bounds") for c in columns
    ]
    wraps = lane < fine
    columns = [jnp.where(wraps, turned[i - 1], turned[i]) for i in range(count)]
    step = 1
    while step < count:
        moved = (amount & (step * LANES)) != 0
        columns = [jnp.where(moved, columns[i - step], columns[i]) for i in range(count)]
        step *= 2
    near = [columns]
    for offset in range(1, 4):
        near.append(shifted(columns, offset))
    total = [tap(BAND - 1) * c for c in columns]
    for group in range((BAND - 1) // 4 - 1, -1, -1):
        total = shifted(total, 4)
        for offset in range(4):
            factor = tap(4 * group + offset)
            total = [t + factor * c for t, c in zip(total, near[offset])]
    return total


def row_shifts(shift_ref, first):
    row = lax.broadcasted_iota(jnp.int32, (8, LANES), 0)
    amounts = jnp.zeros((8, LANES), jnp.int32)
    for r in range(8):
        amounts = jnp.where(row == r, shift_ref[first + r], amounts)
    return amounts


def spread_taps(taps_ref, first, tap_ref):
    block = taps_ref[pl.ds(first, 8), :]
    for k in range(BAND):
        tap_ref[k] = jnp.broadcast_to(block[:, k : k + 1], (8, LANES))


def tiles(width):
    return [slice(i * LANES, (i + 1) * LANES) for i in range(width // LANES)]


def half_start(which):
    odd = parity()
    return pl.multiple_of((1 - odd if which == 0 else odd) * 8, 8)


def zonal_forward(which, shift_ref, taps_ref, control, out, tap_ref):
    members, levels, _, width = control.shape
    first = half_start(which)
    amount = (width - HALF - row_shifts(shift_ref, first)) & (width - 1)
    spread_taps(taps_ref, first, tap_ref)

    def step(m, carry):
        for l in range(levels):
            columns = [control[m, l, pl.ds(first, 8), cut] for cut in tiles(width)]
            result = circle_filter(columns, amount, lambda k: tap_ref[BAND - 1 - k])
            for cut, value in zip(tiles(width), result):
                out[m, l, :, cut] = value
        return carry

    lax.fori_loop(0, members, step, 0)


def zonal_adjoint(which, shift_ref, taps_ref, control, own, got, *refs):
    other, out, tap_ref = (None, *refs) if which == 0 else refs
    members, levels, _, width = control.shape
    first = half_start(which)
    amount = (row_shifts(shift_ref, first) - HALF) & (width - 1)
    spread_taps(taps_ref, first, tap_ref)

    def step(m, carry):
        for l in range(levels):
            columns = [own[m, l, :, cut] + got[m, l, :, cut] for cut in tiles(width)]
            result = circle_filter(columns, amount, lambda k: tap_ref[k])
            for cut, value in zip(tiles(width), result):
                total = control[m, l, pl.ds(first, 8), cut] + value
                if which == 0:
                    out[m, l, :, cut] = total
                else:
                    out[m, l, pl.ds(first, 8), cut] = total
                    out[m, l, pl.ds(8 - first, 8), cut] = other[m, l, :, cut]
        return carry

    lax.fori_loop(0, members, step, 0)


def build_matrix(lat_count, taps_ref, mixing_ref, matrix, transposed):
    band_rows, levels = taps_ref.shape[0], mixing_ref.shape[1]
    rows, columns = matrix.shape
    odd, lat = parity(), lax.axis_index("lat")
    alone = (lat == 0) | (lat == lat_count - 1)
    column = lax.broadcasted_iota(jnp.int32, (band_rows, columns), 1)
    row = lax.broadcasted_iota(jnp.int32, (band_rows, columns), 0)
    block, level, inner = column // (8 * levels), (column // 8) % levels, column % 8
    even_start = jnp.where(block == 0, 16, jnp.where(block == 1, 8, jnp.where(block == 2, 24, 0)))
    odd_start = jnp.where(block == 0, 8, jnp.where(block == 1, 16, jnp.where(block == 2, 0, 24)))
    reach = jnp.where(odd == 1, odd_start, even_start) + inner - row
    band = jnp.zeros((band_rows, columns), F32)
    for k in range(BAND):
        band = jnp.where(reach == k, taps_ref[:, k : k + 1], band)
    band = jnp.where((block == 3) & alone, 0.0, band)
    for a in range(levels):
        mixing = mixing_ref[a * band_rows : (a + 1) * band_rows, :]
        factor = jnp.zeros((band_rows, columns), F32)
        for b in range(levels):
            factor = jnp.where(level == b, mixing[:, b : b + 1], factor)
        matrix[a * band_rows : (a + 1) * band_rows, :] = factor * band
    transposed[...] = matrix[...].T


def halves(value):
    high = value.astype(BF16)
    return high, (value - high.astype(F32)).astype(BF16)


def product(left, right):
    (lh, ll), (rh, rl) = left, right
    dot = functools.partial(jnp.dot, preferred_element_type=F32)
    return dot(lh, rh) + (dot(lh, rl) + dot(ll, rh))


CHUNK = 256


def localize(matrix, parts, out):
    members, levels, band_rows, width = out.shape
    left = halves(matrix[...])
    for m in range(members):
        for c in range(0, width, CHUNK):
            cut = slice(c, c + CHUNK)
            stack = jnp.concatenate(
                [p[m, l, :, cut] for p in parts for l in range(levels)], axis=0
            )
            result = product(left, halves(stack))
            for l in range(levels):
                out[m, l, :, cut] = result[l * band_rows : (l + 1) * band_rows]


def delocalize(matrix, weighted, parts):
    members, levels, band_rows, width = weighted.shape
    left = halves(matrix[...])
    for m in range(members):
        for c in range(0, width, CHUNK):
            cut = slice(c, c + CHUNK)
            stack = jnp.concatenate([weighted[m, l, :, cut] for l in range(levels)], axis=0)
            result = product(left, halves(stack))
            for p, part in enumerate(parts):
                for l in range(levels):
                    start = (p * levels + l) * 8
                    part[m, l, :, cut] = result[start : start + 8]


def increment(ens, localized, slot, field, l):
    total = None
    for m in range(localized.shape[0]):
        term = ens[slot, field, m, l].astype(F32) * localized[m, l]
        total = term if total is None else total + term
    return total


def weight_out(obs, out):
    pltpu.sync_copy(obs.at[0, 1 - own_y()], out)


def weight_pick(owners, obs, from_y, mine, up, down):
    for step, out in ((0, mine), (1, up), (SLOTS - 1, down)):
        held = (owner_at(owners, step) & 1) == own_y()

        @pl.when(held)
        def _(out=out):
            pltpu.sync_copy(obs.at[0, own_y()], out)

        @pl.when(jnp.logical_not(held))
        def _(out=out):
            out[...] = from_y[...]


def first_body(step, owners, matrix, a, b, c, d, ens, localized, send):
    localize(matrix, (a, b, c, d), localized)
    slot = slot_at(owners, step)
    for l in range(localized.shape[1]):
        send[l] = increment(ens, localized, slot, 1 - own_y(), l)


def send_body(steps, owners, ens, localized, *sends):
    for step, send in zip(steps, sends):
        slot = slot_at(owners, step)
        for l in range(localized.shape[1]):
            send[l] = increment(ens, localized, slot, 1 - own_y(), l)


def meet_body(step, owners, ens, localized, got, out):
    slot = slot_at(owners, step)
    for l in range(localized.shape[1]):
        out[l] = increment(ens, localized, slot, own_y(), l) + got[l]


def last_body(owners, ens, localized, got_y, got_1, got_2, got_3, mine, from_low, from_high, out):
    slot, place = slot_at(owners, 0), owner_at(owners, 0) >> 1
    for code, weight in enumerate((mine, from_low, from_high)):
        here = (place == own_z(), place < own_z(), place > own_z())[code]

        @pl.when(here)
        def _(weight=weight):
            for l in range(localized.shape[1]):
                out[l] = weight[l] * (
                    increment(ens, localized, slot, own_y(), l)
                    + got_y[l]
                    + (got_1[l] + got_2[l] + got_3[l])
                )


def spread_body(pieces, first, final, owners, ens, *refs):
    refs = list(refs)
    grads = [refs.pop(0) for _ in pieces]
    before = None if first else refs.pop(0)
    matrix = refs.pop(0) if final else None
    out = refs[-1] if final else refs[0]
    members, levels = out.shape[:2]
    places = [
        (slot_at(owners, step), 1 - own_y() if other else own_y()) for step, other in pieces
    ]
    for m in range(members):
        for l in range(levels):
            total = None if before is None else before[m, l]
            for (slot, field), grad in zip(places, grads):
                term = ens[slot, field, m, l].astype(F32) * grad[l]
                total = term if total is None else total + term
            out[m, l] = total
    if final:
        delocalize(matrix, out, refs[:4])


def all_increments(ens, localized, out):
    for slot in range(out.shape[0]):
        for field in range(out.shape[1]):
            for l in range(out.shape[2]):
                out[slot, field, l] = increment(ens, localized, slot, field, l)


def localize_body(matrix, a, b, c, d, localized):
    localize(matrix, (a, b, c, d), localized)


def all_weighted(ens, grad, matrix, a, b, c, d, out):
    members, levels = out.shape[:2]
    for m in range(members):
        for l in range(levels):
            total = None
            for slot in range(ens.shape[0]):
                for field in range(ens.shape[1]):
                    term = ens[slot, field, m, l].astype(F32) * grad[slot, field, l]
                    total = term if total is None else total + term
            out[m, l] = total
    delocalize(matrix, out, (a, b, c, d))


def per_device(
    z_count,
    control,
    perturbations,
    obs_weight,
    slot_owner,
    zonal_shift,
    zonal_taps,
    meridional_taps,
    level_mixing,
):
    members, levels, band_rows, width = control.shape
    mem_count, lat_count = lax.axis_size("mem"), lax.axis_size("lat")
    mem = lax.axis_index("mem")
    direct = z_count > 0
    field_shape = (members, levels, band_rows, width)
    half_shape = (members, levels, 8, width)
    piece = shape(levels, band_rows, width)
    core_pairs = [(i, i ^ 1) for i in range(lat_count)]
    x_pairs = [(i, i + 1) for i in range(1, lat_count - 1, 2)]
    x_pairs += [(j, i) for i, j in x_pairs]
    swap_core = lambda v: lax.ppermute(v, "lat", core_pairs)
    swap_x = lambda v: lax.ppermute(v, "lat", x_pairs)
    tap_room = [pltpu.VMEM((BAND, 8, LANES), F32)]

    ahead = ()
    if direct:
        y_pairs = [(i, i ^ 1) for i in range(mem_count)]
        swap_y = lambda v: lax.ppermute(v, "mem", y_pairs)
        turn_z = lambda v, s: lax.ppermute(
            v, "mem", [(i, (i + 2 * s) % mem_count) for i in range(mem_count)]
        )
        weight_sent = call(weight_out, piece, "weight_out", 1 << 18, obs_weight, specs=(ANY,))
        weight_y = swap_y(weight_sent)
        ahead = (weight_sent,)

    def forward(which, after):
        return call(
            functools.partial(zonal_forward, which), shape(*half_shape), "zonal%d" % which,
            1 << 19, zonal_shift, zonal_taps, control, specs=(SMEM, VMEM, VMEM),
            scratch=tap_room, after=after,
        )

    near_x = forward(1, ahead)
    far_x = swap_x(near_x)
    near_core = forward(0, (near_x,))
    far_core = swap_core(near_core)
    mixing = jnp.transpose(level_mixing, (1, 0, 2)).reshape(levels * band_rows, levels)
    matrix, transposed = call(
        functools.partial(build_matrix, lat_count),
        (shape(levels * band_rows, 32 * levels), shape(32 * levels, levels * band_rows)),
        "matrix", 1 << 16, meridional_taps, mixing, specs=(VMEM, VMEM), after=(near_core,),
    )
    parts = (near_core, near_x, far_core, far_x)

    if direct:
        ends = z_count - 1
        raised = [(2 * i + j, 2 * i + 2 + j) for i in range(ends - 1) for j in range(2)]
        lowered = [(2 * i + 2 + j, 2 * i + j) for i in range(1, ends) for j in range(2)]
        mine, up, down = call(
            weight_pick, (piece,) * 3, "weight_pick", 1 << 18, slot_owner, obs_weight, weight_y,
            specs=(SMEM, ANY, VMEM), after=(matrix,),
        )
        from_low = lax.ppermute(up, "mem", raised)
        from_high = lax.ppermute(down, "mem", lowered)
        order = (2, 1, 3)
        localized, first = call(
            functools.partial(first_body, order[0]), (shape(*field_shape), piece),
            "first", 1 << 20, slot_owner, matrix, *parts, perturbations,
            specs=(SMEM,) + (VMEM,) * 6, after=(up,),
        )
        sent = {order[0]: first}
        rest = order[1:] + (0,)
        others = call(
            functools.partial(send_body, rest), (piece,) * len(rest), "send", 1 << 20,
            slot_owner, perturbations, localized, specs=(SMEM, VMEM, VMEM),
        )
        sent.update(zip(rest, others))
        got = {s: swap_y(sent[s]) for s in order + (0,)}
        arrived, before = {}, ()
        for s in order:
            total = call(
                functools.partial(meet_body, s), piece, "meet%d" % s, 1 << 19,
                slot_owner, perturbations, localized, got[s],
                specs=(SMEM,) + (VMEM,) * 3, after=before,
            )
            arrived[s] = turn_z(total, s)
            before = (total,)
        grad = call(
            last_body, piece, "last", 1 << 19, slot_owner, perturbations, localized, got[0],
            arrived[1], arrived[2], arrived[3], mine, from_low, from_high,
            specs=(SMEM,) + (VMEM,) * 9,
        )
        own = {0: grad}
        for s in order:
            own[s] = turn_z(grad, s)
        other = {s: swap_y(own[s]) for s in (0,) + order}
        back = lambda s: (-s) % SLOTS
        weighted = None
        for group in (((0, 0),), ((0, 1), (2, 0)), ((1, 0), (2, 1)), ((3, 0), (1, 1)), ((3, 1),)):
            final = group == ((3, 1),)
            grads = [other[s] if o else own[s] for s, o in group]
            pieces = tuple((back(s), o) for s, o in group)
            before = () if weighted is None else (weighted,)
            extra = (transposed,) if final else ()
            result = call(
                functools.partial(spread_body, pieces, weighted is None, final),
                (shape(*half_shape),) * 4 + (shape(*field_shape),) if final else shape(*field_shape),
                "spread%d" % group[0][0], 1 << 19,
                slot_owner, perturbations, *grads, *before, *extra,
                specs=(SMEM,) + (VMEM,) * (1 + len(grads) + len(before) + len(extra)),
            )
            weighted = result
        own_core, own_x, to_core, to_x = result[:4]
    else:
        localized = call(
            localize_body, shape(*field_shape), "localize", 1 << 20, matrix, *parts,
            specs=(VMEM,) * 5,
        )
        partial = call(
            all_increments, shape(SLOTS, perturbations.shape[1], levels, band_rows, width),
            "increments", 1 << 20, perturbations, localized, specs=(VMEM,) * 2,
        )
        weights = jnp.stack(
            [
                lax.psum(jnp.where(mem == slot_owner[t], obs_weight[0], 0.0), "mem")
                for t in range(SLOTS)
            ]
        )
        share = lax.psum_scatter(
            partial.reshape(-1, width), "mem", scatter_dimension=0, tiled=True
        )
        share_rows = share.shape[0]
        weight_rows = lax.dynamic_slice_in_dim(
            weights.reshape(-1, width), mem * share_rows, share_rows, 0
        )
        gathered = lax.all_gather(weight_rows * share, "mem", axis=0, tiled=True)
        own_core, own_x, to_core, to_x, _ = call(
            all_weighted, (shape(*half_shape),) * 4 + (shape(*field_shape),), "weighted",
            1 << 20, perturbations, gathered.reshape(partial.shape), transposed,
            specs=(VMEM,) * 3,
        )
    got_x, got_core = swap_x(to_x), swap_core(to_core)
    half = call(
        functools.partial(zonal_adjoint, 0), shape(*half_shape), "adjoint0", 1 << 19,
        zonal_shift, zonal_taps, control, own_core, got_core,
        specs=(SMEM,) + (VMEM,) * 4, scratch=tap_room,
    )
    return call(
        functools.partial(zonal_adjoint, 1), shape(*field_shape), "adjoint1", 1 << 19,
        zonal_shift, zonal_taps, control, own_x, got_x, half,
        specs=(SMEM,) + (VMEM,) * 5, scratch=tap_room,
    )


def solution(mesh):
    z_count = SLOTS if mesh.shape["mem"] == 2 * SLOTS else 0
    in_specs = (
        P("mem", None, "lat", None),
        P(None, None, "mem", None, "lat", None),
        P("mem", None, None, "lat", None),
        P(),
        P("lat"),
        P("lat", None),
        P("lat", None),
        P("lat", None, None),
    )
    out_specs = P("mem", None, "lat", None)
    return jax.shard_map(
        functools.partial(per_device, z_count),
        mesh=mesh, in_specs=in_specs, out_specs=out_specs, check_vma=False,
    )
```

```python
import functools

import jax
import jax.numpy as jnp
from jax import lax
from jax.experimental import pallas as pl
from jax.experimental.pallas import tpu as pltpu
from jax.sharding import PartitionSpec as P

SLOTS = 4
BAND = 17
HALF = BAND // 2
LANES = 128
F32 = jnp.float32
BF16 = jnp.bfloat16

VMEM = pl.BlockSpec(memory_space=pltpu.VMEM)
SMEM = pl.BlockSpec(memory_space=pltpu.SMEM)
ANY = pl.BlockSpec(memory_space=pl.ANY)
HBM = pl.BlockSpec(memory_space=pltpu.HBM)


def call(body, outs, name, cost, *operands, specs, scratch=(), after=()):
    count, extra = len(operands), len(after)

    def kernel(*refs):
        body(*refs[:count], *refs[count + extra :])

    return pl.pallas_call(
        kernel,
        out_shape=outs,
        in_specs=list(specs) + [ANY] * extra,
        out_specs=jax.tree.map(lambda _: VMEM, outs),
        scratch_shapes=list(scratch),
        compiler_params=pltpu.CompilerParams(vmem_limit_bytes=16 << 20),
        cost_estimate=pl.CostEstimate(flops=cost, bytes_accessed=cost, transcendentals=0),
        name=name,
    )(*operands, *after)


def parity():
    return lax.axis_index("lat") & 1


def own_y():
    return lax.axis_index("mem") & 1


def own_z():
    return lax.axis_index("mem") >> 1


def entry_at(owners, step, value):
    place = (own_z() + step) & (SLOTS - 1)
    found = jnp.int32(0)
    for t in range(SLOTS):
        rank = jnp.int32(0)
        for u in range(SLOTS):
            if u != t:
                rank += jnp.where(owners[u] < owners[t], 1, 0)
        found = jnp.where(rank == place, value(t), found)
    return found


def slot_at(owners, step):
    return entry_at(owners, step, lambda t: jnp.int32(t))


def owner_at(owners, step):
    return entry_at(owners, step, lambda t: owners[t])


def shape(*dims, dtype=F32):
    return jax.ShapeDtypeStruct(dims, dtype)


def shifted(columns, amount):
    lane = lax.broadcasted_iota(jnp.int32, columns[0].shape, 1)
    turned = [pltpu.roll(c, amount, 1) for c in columns]
    return [
        jnp.where(lane < amount, turned[i - 1], turned[i]) for i in range(len(columns))
    ]


def circle_filter(columns, amount, tap):
    count = len(columns)
    lane = lax.broadcasted_iota(jnp.int32, columns[0].shape, 1)
    fine = amount & (LANES - 1)
    source = (lane - fine) & (LANES - 1)
    turned = [
        jnp.take_along_axis(c, source, axis=1, mode="promise_in_bounds") for c in columns
    ]
    wraps = lane < fine
    columns = [jnp.where(wraps, turned[i - 1], turned[i]) for i in range(count)]
    step = 1
    while step < count:
        moved = (amount & (step * LANES)) != 0
        columns = [jnp.where(moved, columns[i - step], columns[i]) for i in range(count)]
        step *= 2
    near = [columns]
    for offset in range(1, 4):
        near.append(shifted(columns, offset))
    total = [tap(BAND - 1) * c for c in columns]
    for group in range((BAND - 1) // 4 - 1, -1, -1):
        total = shifted(total, 4)
        for offset in range(4):
            factor = tap(4 * group + offset)
            total = [t + factor * c for t, c in zip(total, near[offset])]
    return total


def row_shifts(shifts, first):
    row = lax.broadcasted_iota(jnp.int32, (8, LANES), 0)
    amounts = jnp.zeros((8, LANES), jnp.int32)
    for r in range(8):
        amounts = jnp.where(row == r, shifts[first + r], amounts)
    return amounts


def spread_taps(taps, first, spread):
    block = taps[pl.ds(first, 8), :]
    for k in range(BAND):
        spread[k] = jnp.broadcast_to(block[:, k : k + 1], (8, LANES))


def tiles(width):
    return [slice(i * LANES, (i + 1) * LANES) for i in range(width // LANES)]


def half_start(which):
    odd = parity()
    return pl.multiple_of((1 - odd if which == 0 else odd) * 8, 8)


def zonal_forward(first, shifts, taps, control, out):
    members, levels, _, width = control.shape
    amount = (width - HALF - shifts[...]) & (width - 1)

    def step(m, carry):
        for l in range(levels):
            columns = [control[m, l, pl.ds(first, 8), cut] for cut in tiles(width)]
            result = circle_filter(columns, amount, lambda k: taps[BAND - 1 - k])
            for cut, value in zip(tiles(width), result):
                out[m, l, :, cut] = value
        return carry

    lax.fori_loop(0, members, step, 0)


def front_body(names, *refs):
    r = dict(zip(names, refs))
    sems = r["sems"]
    first_x, first_core = half_start(1), half_start(0)
    rows_x, rows_core = pl.ds(first_x, 8), pl.ds(first_core, 8)
    moves = [
        (r["shift"], r["shift_s"]),
        (r["taps"], r["taps_v"]),
        (r["control"].at[:, :, rows_x], r["control_v"].at[:, :, rows_x]),
    ]
    moves.append((r["control"].at[:, :, rows_core], r["control_v"].at[:, :, rows_core]))
    moves.append((r["meridional"], r["meridional_v"]))
    if "obs" in r:
        moves.append((r["obs"].at[0], r["obs_v"]))
    moves.append((r["ens"], r["ens_v"]))
    copies = [pltpu.make_async_copy(a, b, sems.at[i]) for i, (a, b) in enumerate(moves)]
    for copy in copies:
        copy.start()
    for copy in copies[:3]:
        copy.wait()
    r["shift_x"][...] = row_shifts(r["shift_s"], first_x)
    r["shift_core"][...] = row_shifts(r["shift_s"], first_core)
    spread_taps(r["taps_v"], first_x, r["taps_x"])
    zonal_forward(first_x, r["shift_x"], r["taps_x"], r["control_v"], r["near_x"])
    for copy in copies[3:]:
        copy.wait()


def core_body(shifts, taps_v, control, out, taps):
    first = half_start(0)
    spread_taps(taps_v, first, taps)
    zonal_forward(first, shifts, taps, control, out)


def zonal_adjoint(which, shifts, taps_v, control, own, got, *refs):
    other, out, taps = (None, *refs) if which == 0 else refs
    members, levels, _, width = control.shape
    first = half_start(which)
    amount = (shifts[...] - HALF) & (width - 1)
    spread_taps(taps_v, first, taps)

    def step(m, carry):
        for l in range(levels):
            columns = [own[m, l, :, cut] + got[m, l, :, cut] for cut in tiles(width)]
            result = circle_filter(columns, amount, lambda k: taps[k])
            for cut, value in zip(tiles(width), result):
                total = control[m, l, pl.ds(first, 8), cut] + value
                if which == 0:
                    out[m, l, :, cut] = total
                else:
                    out[m, l, pl.ds(first, 8), cut] = total
                    out[m, l, pl.ds(8 - first, 8), cut] = other[m, l, :, cut]
        return carry

    lax.fori_loop(0, members, step, 0)


def build_matrix(lat_count, taps_ref, mixing_ref, matrix, transposed):
    band_rows, levels = taps_ref.shape[0], mixing_ref.shape[1]
    rows, columns = matrix.shape
    odd, lat = parity(), lax.axis_index("lat")
    alone = (lat == 0) | (lat == lat_count - 1)
    column = lax.broadcasted_iota(jnp.int32, (band_rows, columns), 1)
    row = lax.broadcasted_iota(jnp.int32, (band_rows, columns), 0)
    block, level, inner = column // (8 * levels), (column // 8) % levels, column % 8
    even_start = jnp.where(block == 0, 16, jnp.where(block == 1, 8, jnp.where(block == 2, 24, 0)))
    odd_start = jnp.where(block == 0, 8, jnp.where(block == 1, 16, jnp.where(block == 2, 0, 24)))
    reach = jnp.where(odd == 1, odd_start, even_start) + inner - row
    band = jnp.zeros((band_rows, columns), F32)
    for k in range(BAND):
        band = jnp.where(reach == k, taps_ref[:, k : k + 1], band)
    band = jnp.where((block == 3) & alone, 0.0, band)
    for a in range(levels):
        mixing = mixing_ref[a * band_rows : (a + 1) * band_rows, :]
        factor = jnp.zeros((band_rows, columns), F32)
        for b in range(levels):
            factor = jnp.where(level == b, mixing[:, b : b + 1], factor)
        matrix[a * band_rows : (a + 1) * band_rows, :] = factor * band
    transposed[...] = matrix[...].T


def halves(value):
    high = value.astype(BF16)
    return high, (value - high.astype(F32)).astype(BF16)


def product(left, right):
    (lh, ll), (rh, rl) = left, right
    dot = functools.partial(jnp.dot, preferred_element_type=F32)
    return dot(lh, rh) + (dot(lh, rl) + dot(ll, rh))


CHUNK = 256


def localize(matrix, parts, out):
    members, levels, band_rows, width = out.shape
    left = halves(matrix[...])
    for m in range(members):
        for c in range(0, width, CHUNK):
            cut = slice(c, c + CHUNK)
            stack = jnp.concatenate(
                [p[m, l, :, cut] for p in parts for l in range(levels)], axis=0
            )
            result = product(left, halves(stack))
            for l in range(levels):
                out[m, l, :, cut] = result[l * band_rows : (l + 1) * band_rows]


def delocalize(matrix, weighted, parts):
    members, levels, band_rows, width = weighted.shape
    left = halves(matrix[...])
    for m in range(members):
        for c in range(0, width, CHUNK):
            cut = slice(c, c + CHUNK)
            stack = jnp.concatenate([weighted[m, l, :, cut] for l in range(levels)], axis=0)
            result = product(left, halves(stack))
            for p, part in enumerate(parts):
                for l in range(levels):
                    start = (p * levels + l) * 8
                    part[m, l, :, cut] = result[start : start + 8]


def increment(ens, localized, slot, field, l):
    total = None
    for m in range(localized.shape[0]):
        term = ens[slot, field, m, l].astype(F32) * localized[m, l]
        total = term if total is None else total + term
    return total


def weight_pick(owners, here, low, high, mine, across):
    place = owner_at(owners, 0) >> 1
    for found, weights in (
        (place == own_z(), here), (place < own_z(), low), (place > own_z(), high)
    ):

        @pl.when(found)
        def _(weights=weights):
            mine[...] = weights[own_y()]
            across[...] = weights[1 - own_y()]


def first_body(step, owners_hbm, matrix, a, b, c, d, ens, localized, send, owners, sem):
    copy = pltpu.make_async_copy(owners_hbm, owners, sem)
    copy.start()
    localize(matrix, (a, b, c, d), localized)
    copy.wait()
    slot = slot_at(owners, step)
    for l in range(localized.shape[1]):
        send[l] = increment(ens, localized, slot, 1 - own_y(), l)


def send_body(owners, ens, localized, pair, single):
    for step, send in ((1, pair.at[0]), (3, pair.at[1]), (0, single)):
        slot = slot_at(owners, step)
        for l in range(localized.shape[1]):
            send[l] = increment(ens, localized, slot, 1 - own_y(), l)


def meet_body(step, owners, ens, localized, got, out):
    slot = slot_at(owners, step)
    for l in range(localized.shape[1]):
        out[l] = increment(ens, localized, slot, own_y(), l) + got[l]


def meet_pair_body(owners, ens, localized, got, *outs):
    for i, (step, out) in enumerate(zip((1, 3), outs)):
        meet_body(step, owners, ens, localized, got.at[i], out)


def last_body(owners, ens, localized, got_y, got_1, got_2, got_3, mine, from_y, out):
    slot = slot_at(owners, 0)
    held = (owner_at(owners, 0) & 1) == own_y()
    for here, weight in ((held, mine), (jnp.logical_not(held), from_y)):

        @pl.when(here)
        def _(weight=weight):
            for l in range(localized.shape[1]):
                out[l] = weight[l] * (
                    increment(ens, localized, slot, own_y(), l)
                    + got_y[l]
                    + (got_1[l] + got_2[l] + got_3[l])
                )


def spread_body(pieces, first, final, owners, ens, *refs):
    refs = list(refs)
    grads = [refs.pop(0) for _ in pieces]
    before = None if first else refs.pop(0)
    matrix = refs.pop(0) if final else None
    out = refs[-1] if final else refs[0]
    members, levels = out.shape[:2]
    places = [
        (slot_at(owners, step), 1 - own_y() if other else own_y()) for step, other in pieces
    ]
    for m in range(members):
        for l in range(levels):
            total = None if before is None else before[m, l]
            for (slot, field), grad in zip(places, grads):
                term = ens[slot, field, m, l].astype(F32) * grad[l]
                total = term if total is None else total + term
            out[m, l] = total
    if final:
        delocalize(matrix, out, refs[:4])


def all_increments(ens, localized, out):
    for slot in range(out.shape[0]):
        for field in range(out.shape[1]):
            for l in range(out.shape[2]):
                out[slot, field, l] = increment(ens, localized, slot, field, l)


def localize_body(matrix, a, b, c, d, localized):
    localize(matrix, (a, b, c, d), localized)


def all_weighted(ens, grad, matrix, a, b, c, d, out):
    members, levels = out.shape[:2]
    for m in range(members):
        for l in range(levels):
            total = None
            for slot in range(ens.shape[0]):
                for field in range(ens.shape[1]):
                    term = ens[slot, field, m, l].astype(F32) * grad[slot, field, l]
                    total = term if total is None else total + term
            out[m, l] = total
    delocalize(matrix, out, (a, b, c, d))


def per_device(
    z_count,
    control,
    perturbations,
    obs_weight,
    slot_owner,
    zonal_shift,
    zonal_taps,
    meridional_taps,
    level_mixing,
):
    members, levels, band_rows, width = control.shape
    mem_count, lat_count = lax.axis_size("mem"), lax.axis_size("lat")
    mem = lax.axis_index("mem")
    direct = z_count > 0
    field_shape = (members, levels, band_rows, width)
    half_shape = (members, levels, 8, width)
    piece = shape(levels, band_rows, width)
    core_pairs = [(i, i ^ 1) for i in range(lat_count)]
    x_pairs = [(i, i + 1) for i in range(1, lat_count - 1, 2)]
    x_pairs += [(j, i) for i, j in x_pairs]
    swap_core = lambda v: lax.ppermute(v, "lat", core_pairs)
    swap_x = lambda v: lax.ppermute(v, "lat", x_pairs)
    tap_room = [pltpu.VMEM((BAND, 8, LANES), F32)]
    ins = {
        "shift": zonal_shift, "taps": zonal_taps, "control": control,
        "meridional": meridional_taps, "ens": perturbations,
    }
    results = {
        "near_x": shape(*half_shape), "control_v": shape(*field_shape),
        "taps_v": shape(*zonal_taps.shape), "meridional_v": shape(*meridional_taps.shape),
        "shift_x": shape(8, LANES, dtype=jnp.int32),
        "shift_core": shape(8, LANES, dtype=jnp.int32),
        "ens_v": shape(*perturbations.shape, dtype=BF16),
    }
    if direct:
        ins["obs"] = obs_weight
        results["obs_v"] = shape(*obs_weight.shape[1:])
    names = (*ins, *results, "taps_x", "shift_s", "sems")
    made = call(
        functools.partial(front_body, names), tuple(results.values()), "front", 1 << 19,
        *(pltpu.with_memory_space_constraint(v, pltpu.HBM) for v in ins.values()),
        specs=(HBM,) * len(ins),
        scratch=[
            *tap_room, pltpu.SMEM(zonal_shift.shape, jnp.int32), pltpu.SemaphoreType.DMA((7,)),
        ],
    )
    made = dict(zip(results, made))
    near_x, control_v, ens = made["near_x"], made["control_v"], made["ens_v"]
    far_x = swap_x(near_x)
    if direct:
        y_pairs = [(i, i ^ 1) for i in range(mem_count)]
        swap_y = lambda v: lax.ppermute(v, "mem", y_pairs)
        turn_z = lambda v, s: lax.ppermute(
            v, "mem", [(i, (i + 2 * s) % mem_count) for i in range(mem_count)]
        )
        ends = z_count - 1
        raised = [(2 * i + j, 2 * i + 2 + j) for i in range(ends - 1) for j in range(2)]
        lowered = [(2 * i + 2 + j, 2 * i + j) for i in range(1, ends) for j in range(2)]
        from_low = lax.ppermute(made["obs_v"], "mem", raised)
        from_high = lax.ppermute(made["obs_v"], "mem", lowered)
    near_core = call(
        core_body, shape(*half_shape), "core", 1 << 19, made["shift_core"], made["taps_v"],
        control_v, specs=(VMEM,) * 3, scratch=tap_room,
    )
    far_core = swap_core(near_core)
    mixing = jnp.transpose(level_mixing, (1, 0, 2)).reshape(levels * band_rows, levels)
    matrix, transposed = call(
        functools.partial(build_matrix, lat_count),
        (shape(levels * band_rows, 32 * levels), shape(32 * levels, levels * band_rows)),
        "matrix", 1 << 16, made["meridional_v"], mixing, specs=(VMEM, VMEM), after=(near_core, far_x),
    )
    parts = (near_core, near_x, far_core, far_x)

    if direct:
        localized, first = call(
            functools.partial(first_body, 2), (shape(*field_shape), piece),
            "first", 1 << 20, slot_owner, matrix, *parts, ens,
            specs=(HBM,) + (VMEM,) * 6,
            scratch=[pltpu.SMEM((SLOTS,), jnp.int32), pltpu.SemaphoreType.DMA],
        )
        got_two = swap_y(first)
        pair, single = call(
            send_body, (shape(2, levels, band_rows, width), piece), "send", 1 << 20,
            slot_owner, ens, localized, specs=(SMEM, VMEM, VMEM), after=(from_low, from_high),
        )
        pair, got_two = lax.optimization_barrier((pair, got_two))
        got_pair = swap_y(pair)
        two = call(
            functools.partial(meet_body, 2), piece, "meet2", 1 << 19,
            slot_owner, ens, localized, got_two, specs=(SMEM,) + (VMEM,) * 3,
        )
        arrived = {2: turn_z(two, 2)}
        mine, across = call(
            weight_pick, (piece,) * 2, "weight_pick", 1 << 18, slot_owner, made["obs_v"],
            from_low, from_high, specs=(SMEM,) + (VMEM,) * 3, after=(two,),
        )
        one, three = call(
            meet_pair_body, (piece,) * 2, "meet13", 1 << 19,
            slot_owner, ens, localized, got_pair, specs=(SMEM,) + (VMEM,) * 3,
            after=(two, across),
        )
        arrived[1], arrived[3] = turn_z(one, 1), turn_z(three, 3)
        single, across, _ = lax.optimization_barrier((single, across, got_pair))
        got_own, from_y = swap_y(single), swap_y(across)
        grad = call(
            last_body, piece, "last", 1 << 19, slot_owner, ens, localized, got_own,
            arrived[1], arrived[2], arrived[3], mine, from_y,
            specs=(SMEM,) + (VMEM,) * 8,
        )
        own = {0: grad, 1: turn_z(grad, 1), 3: turn_z(grad, 3)}
        other = {0: swap_y(grad)}
        later, own[1], own[3], other[0] = lax.optimization_barrier((grad, own[1], own[3], other[0]))
        own[2] = turn_z(later, 2)
        other.update({s: swap_y(own[s]) for s in (1, 3, 2)})
        back = lambda s: (-s) % SLOTS
        weighted = None
        groups = (((0, 0),), ((0, 1), (1, 0), (3, 0)), ((1, 1), (3, 1), (2, 0)), ((2, 1),))
        for group in groups:
            final = group == groups[-1]
            grads = [other[s] if o else own[s] for s, o in group]
            pieces = tuple((back(s), o) for s, o in group)
            before = () if weighted is None else (weighted,)
            extra = (transposed,) if final else ()
            result = call(
                functools.partial(spread_body, pieces, weighted is None, final),
                (shape(*half_shape),) * 4 + (shape(*field_shape),) if final else shape(*field_shape),
                "spread%d" % group[0][0], 1 << 19,
                slot_owner, ens, *grads, *before, *extra,
                specs=(SMEM,) + (VMEM,) * (1 + len(grads) + len(before) + len(extra)),
            )
            weighted = result
        own_core, own_x, to_core, to_x = result[:4]
    else:
        localized = call(
            localize_body, shape(*field_shape), "localize", 1 << 20, matrix, *parts,
            specs=(VMEM,) * 5,
        )
        partial = call(
            all_increments, shape(SLOTS, ens.shape[1], levels, band_rows, width),
            "increments", 1 << 20, ens, localized, specs=(VMEM,) * 2,
        )
        weights = jnp.stack(
            [
                lax.psum(jnp.where(mem == slot_owner[t], obs_weight[0], 0.0), "mem")
                for t in range(SLOTS)
            ]
        )
        share = lax.psum_scatter(
            partial.reshape(-1, width), "mem", scatter_dimension=0, tiled=True
        )
        share_rows = share.shape[0]
        weight_rows = lax.dynamic_slice_in_dim(
            weights.reshape(-1, width), mem * share_rows, share_rows, 0
        )
        gathered = lax.all_gather(weight_rows * share, "mem", axis=0, tiled=True)
        own_core, own_x, to_core, to_x, _ = call(
            all_weighted, (shape(*half_shape),) * 4 + (shape(*field_shape),), "weighted",
            1 << 20, ens, gathered.reshape(partial.shape), transposed,
            specs=(VMEM,) * 3,
        )
    got_x, got_core = swap_x(to_x), swap_core(to_core)
    half = call(
        functools.partial(zonal_adjoint, 0), shape(*half_shape), "adjoint0", 1 << 19,
        made["shift_core"], made["taps_v"], control_v, own_core, got_core,
        specs=(VMEM,) * 5, scratch=tap_room,
    )
    return call(
        functools.partial(zonal_adjoint, 1), shape(*field_shape), "adjoint1", 1 << 19,
        made["shift_x"], made["taps_v"], control_v, own_x, got_x, half,
        specs=(VMEM,) * 6, scratch=tap_room,
    )


def solution(mesh):
    z_count = SLOTS if mesh.shape["mem"] == 2 * SLOTS else 0
    in_specs = (
        P("mem", None, "lat", None),
        P(None, None, "mem", None, "lat", None),
        P("mem", None, None, "lat", None),
        P(),
        P("lat"),
        P("lat", None),
        P("lat", None),
        P("lat", None, None),
    )
    out_specs = P("mem", None, "lat", None)
    return jax.shard_map(
        functools.partial(per_device, z_count),
        mesh=mesh, in_specs=in_specs, out_specs=out_specs, check_vma=False,
    )
```

```python
import functools

import jax
import jax.numpy as jnp
from jax import lax
from jax.experimental import pallas as pl
from jax.experimental.pallas import tpu as pltpu
from jax.sharding import PartitionSpec as P

SLOTS = 4
BAND = 17
HALF = BAND // 2
LANES = 128
F32 = jnp.float32
BF16 = jnp.bfloat16

VMEM = pl.BlockSpec(memory_space=pltpu.VMEM)
SMEM = pl.BlockSpec(memory_space=pltpu.SMEM)
ANY = pl.BlockSpec(memory_space=pl.ANY)
HBM = pl.BlockSpec(memory_space=pltpu.HBM)


def call(body, outs, name, cost, *operands, specs, scratch=(), after=()):
    count, extra = len(operands), len(after)

    def kernel(*refs):
        body(*refs[:count], *refs[count + extra :])

    return pl.pallas_call(
        kernel,
        out_shape=outs,
        in_specs=list(specs) + [ANY] * extra,
        out_specs=jax.tree.map(lambda _: VMEM, outs),
        scratch_shapes=list(scratch),
        compiler_params=pltpu.CompilerParams(vmem_limit_bytes=16 << 20),
        cost_estimate=pl.CostEstimate(flops=cost, bytes_accessed=cost, transcendentals=0),
        name=name,
    )(*operands, *after)


def parity():
    return lax.axis_index("lat") & 1


def own_y():
    return lax.axis_index("mem") & 1


def own_z():
    return lax.axis_index("mem") >> 1


def entry_at(owners, step, value):
    place = own_z() ^ step
    found = jnp.int32(0)
    for t in range(SLOTS):
        rank = jnp.int32(0)
        for u in range(SLOTS):
            if u != t:
                rank += jnp.where(owners[u] < owners[t], 1, 0)
        found = jnp.where(rank == place, value(t), found)
    return found


def slot_at(owners, step):
    return entry_at(owners, step, lambda t: jnp.int32(t))


def owner_at(owners, step):
    return entry_at(owners, step, lambda t: owners[t])


def shape(*dims, dtype=F32):
    return jax.ShapeDtypeStruct(dims, dtype)


def shifted(columns, amount):
    lane = lax.broadcasted_iota(jnp.int32, columns[0].shape, 1)
    turned = [pltpu.roll(c, amount, 1) for c in columns]
    return [
        jnp.where(lane < amount, turned[i - 1], turned[i]) for i in range(len(columns))
    ]


def circle_filter(columns, amount, tap):
    count = len(columns)
    lane = lax.broadcasted_iota(jnp.int32, columns[0].shape, 1)
    fine = amount & (LANES - 1)
    source = (lane - fine) & (LANES - 1)
    turned = [
        jnp.take_along_axis(c, source, axis=1, mode="promise_in_bounds") for c in columns
    ]
    wraps = lane < fine
    columns = [jnp.where(wraps, turned[i - 1], turned[i]) for i in range(count)]
    step = 1
    while step < count:
        moved = (amount & (step * LANES)) != 0
        columns = [jnp.where(moved, columns[i - step], columns[i]) for i in range(count)]
        step *= 2
    near = [columns]
    for offset in range(1, 4):
        near.append(shifted(columns, offset))
    total = [tap(BAND - 1) * c for c in columns]
    for group in range((BAND - 1) // 4 - 1, -1, -1):
        total = shifted(total, 4)
        for offset in range(4):
            factor = tap(4 * group + offset)
            total = [t + factor * c for t, c in zip(total, near[offset])]
    return total


def row_shifts(shifts, first):
    row = lax.broadcasted_iota(jnp.int32, (8, LANES), 0)
    amounts = jnp.zeros((8, LANES), jnp.int32)
    for r in range(8):
        amounts = jnp.where(row == r, shifts[first + r], amounts)
    return amounts


def spread_taps(taps, first, spread):
    block = taps[pl.ds(first, 8), :]
    for k in range(BAND):
        spread[k] = jnp.broadcast_to(block[:, k : k + 1], (8, LANES))


def tiles(width):
    return [slice(i * LANES, (i + 1) * LANES) for i in range(width // LANES)]


def half_start(which):
    odd = parity()
    return pl.multiple_of((1 - odd if which == 0 else odd) * 8, 8)


def zonal_forward(first, shifts, taps, control, out):
    members, levels, _, width = control.shape
    amount = (width - HALF - shifts[...]) & (width - 1)

    def step(m, carry):
        for l in range(levels):
            columns = [control[m, l, pl.ds(first, 8), cut] for cut in tiles(width)]
            result = circle_filter(columns, amount, lambda k: taps[BAND - 1 - k])
            for cut, value in zip(tiles(width), result):
                out[m, l, :, cut] = value
        return carry

    lax.fori_loop(0, members, step, 0)


def front_body(names, *refs):
    r = dict(zip(names, refs))
    sems = r["sems"]
    first_x, first_core = half_start(1), half_start(0)
    rows_x, rows_core = pl.ds(first_x, 8), pl.ds(first_core, 8)
    moves = [
        (r["shift"], r["shift_s"]),
        (r["taps"], r["taps_v"]),
        (r["control"].at[:, :, rows_x], r["control_v"].at[:, :, rows_x]),
    ]
    moves.append((r["control"].at[:, :, rows_core], r["control_v"].at[:, :, rows_core]))
    moves.append((r["meridional"], r["meridional_v"]))
    if "obs" in r:
        moves.append((r["obs"].at[0], r["obs_v"]))
    moves.append((r["ens"], r["ens_v"]))
    copies = [pltpu.make_async_copy(a, b, sems.at[i]) for i, (a, b) in enumerate(moves)]
    for copy in copies:
        copy.start()
    for copy in copies[:3]:
        copy.wait()
    r["shift_x"][...] = row_shifts(r["shift_s"], first_x)
    r["shift_core"][...] = row_shifts(r["shift_s"], first_core)
    spread_taps(r["taps_v"], first_x, r["taps_x"])
    zonal_forward(first_x, r["shift_x"], r["taps_x"], r["control_v"], r["near_x"])
    for copy in copies[3:]:
        copy.wait()


def core_body(shifts, taps_v, control, out, taps):
    first = half_start(0)
    spread_taps(taps_v, first, taps)
    zonal_forward(first, shifts, taps, control, out)


def zonal_adjoint(which, shifts, taps_v, control, own, got, *refs):
    other, out, taps = (None, *refs) if which == 0 else refs
    members, levels, _, width = control.shape
    first = half_start(which)
    amount = (shifts[...] - HALF) & (width - 1)
    spread_taps(taps_v, first, taps)

    def step(m, carry):
        for l in range(levels):
            columns = [own[m, l, :, cut] + got[m, l, :, cut] for cut in tiles(width)]
            result = circle_filter(columns, amount, lambda k: taps[k])
            for cut, value in zip(tiles(width), result):
                total = control[m, l, pl.ds(first, 8), cut] + value
                if which == 0:
                    out[m, l, :, cut] = total
                else:
                    out[m, l, pl.ds(first, 8), cut] = total
                    out[m, l, pl.ds(8 - first, 8), cut] = other[m, l, :, cut]
        return carry

    lax.fori_loop(0, members, step, 0)


def build_matrix(lat_count, taps_ref, mixing_ref, matrix, transposed):
    band_rows, levels = taps_ref.shape[0], mixing_ref.shape[1]
    rows, columns = matrix.shape
    odd, lat = parity(), lax.axis_index("lat")
    alone = (lat == 0) | (lat == lat_count - 1)
    column = lax.broadcasted_iota(jnp.int32, (band_rows, columns), 1)
    row = lax.broadcasted_iota(jnp.int32, (band_rows, columns), 0)
    block, level, inner = column // (8 * levels), (column // 8) % levels, column % 8
    even_start = jnp.where(block == 0, 16, jnp.where(block == 1, 8, jnp.where(block == 2, 24, 0)))
    odd_start = jnp.where(block == 0, 8, jnp.where(block == 1, 16, jnp.where(block == 2, 0, 24)))
    reach = jnp.where(odd == 1, odd_start, even_start) + inner - row
    band = jnp.zeros((band_rows, columns), F32)
    for k in range(BAND):
        band = jnp.where(reach == k, taps_ref[:, k : k + 1], band)
    band = jnp.where((block == 3) & alone, 0.0, band)
    for a in range(levels):
        mixing = mixing_ref[a * band_rows : (a + 1) * band_rows, :]
        factor = jnp.zeros((band_rows, columns), F32)
        for b in range(levels):
            factor = jnp.where(level == b, mixing[:, b : b + 1], factor)
        matrix[a * band_rows : (a + 1) * band_rows, :] = factor * band
    transposed[...] = matrix[...].T


def halves(value):
    high = value.astype(BF16)
    return high, (value - high.astype(F32)).astype(BF16)


def product(left, right):
    (lh, ll), (rh, rl) = left, right
    dot = functools.partial(jnp.dot, preferred_element_type=F32)
    return dot(lh, rh) + (dot(lh, rl) + dot(ll, rh))


CHUNK = 256


def localize(matrix, parts, out):
    members, levels, band_rows, width = out.shape
    left = halves(matrix[...])
    for m in range(members):
        for c in range(0, width, CHUNK):
            cut = slice(c, c + CHUNK)
            stack = jnp.concatenate(
                [p[m, l, :, cut] for p in parts for l in range(levels)], axis=0
            )
            result = product(left, halves(stack))
            for l in range(levels):
                out[m, l, :, cut] = result[l * band_rows : (l + 1) * band_rows]


def delocalize(matrix, weighted, parts):
    members, levels, band_rows, width = weighted.shape
    left = halves(matrix[...])
    for m in range(members):
        for c in range(0, width, CHUNK):
            cut = slice(c, c + CHUNK)
            stack = jnp.concatenate([weighted[m, l, :, cut] for l in range(levels)], axis=0)
            result = product(left, halves(stack))
            for p, part in enumerate(parts):
                for l in range(levels):
                    start = (p * levels + l) * 8
                    part[m, l, :, cut] = result[start : start + 8]


def increment(ens, localized, slot, field, l):
    total = None
    for m in range(localized.shape[0]):
        term = ens[slot, field, m, l].astype(F32) * localized[m, l]
        total = term if total is None else total + term
    return total


def weight_pick(owners, here, side, middle, mine, across):
    place = owner_at(owners, 0) >> 1
    for found, weights in (
        (place == own_z(), here),
        (place == own_z() ^ 1, side),
        (place == own_z() ^ 3, middle),
    ):

        @pl.when(found)
        def _(weights=weights):
            mine[...] = weights[own_y()]
            across[...] = weights[1 - own_y()]


def first_body(step, owners_hbm, matrix, a, b, c, d, ens, localized, send, owners, sem):
    copy = pltpu.make_async_copy(owners_hbm, owners, sem)
    copy.start()
    localize(matrix, (a, b, c, d), localized)
    copy.wait()
    slot = slot_at(owners, step)
    for l in range(localized.shape[1]):
        send[l] = increment(ens, localized, slot, 1 - own_y(), l)


def send_body(owners, ens, localized, pair, single):
    for step, send in ((1, pair.at[0]), (3, pair.at[1]), (0, single)):
        slot = slot_at(owners, step)
        for l in range(localized.shape[1]):
            send[l] = increment(ens, localized, slot, 1 - own_y(), l)


def meet_body(step, owners, ens, localized, got, out):
    slot = slot_at(owners, step)
    for l in range(localized.shape[1]):
        out[l] = increment(ens, localized, slot, own_y(), l) + got[l]


def meet_pair_body(owners, ens, localized, got, *outs):
    for i, (step, out) in enumerate(zip((1, 3), outs)):
        meet_body(step, owners, ens, localized, got.at[i], out)


def last_body(owners, ens, localized, got_y, got_1, got_2, got_3, mine, from_y, out):
    slot = slot_at(owners, 0)
    held = (owner_at(owners, 0) & 1) == own_y()
    for here, weight in ((held, mine), (jnp.logical_not(held), from_y)):

        @pl.when(here)
        def _(weight=weight):
            for l in range(localized.shape[1]):
                out[l] = weight[l] * (
                    increment(ens, localized, slot, own_y(), l)
                    + got_y[l]
                    + (got_1[l] + got_2[l] + got_3[l])
                )


def spread_body(pieces, first, final, owners, ens, *refs):
    refs = list(refs)
    grads = [refs.pop(0) for _ in pieces]
    before = None if first else refs.pop(0)
    matrix = refs.pop(0) if final else None
    out = refs[-1] if final else refs[0]
    members, levels = out.shape[:2]
    places = [
        (slot_at(owners, step), 1 - own_y() if other else own_y()) for step, other in pieces
    ]
    for m in range(members):
        for l in range(levels):
            total = None if before is None else before[m, l]
            for (slot, field), grad in zip(places, grads):
                term = ens[slot, field, m, l].astype(F32) * grad[l]
                total = term if total is None else total + term
            out[m, l] = total
    if final:
        delocalize(matrix, out, refs[:4])


def all_increments(ens, localized, out):
    for slot in range(out.shape[0]):
        for field in range(out.shape[1]):
            for l in range(out.shape[2]):
                out[slot, field, l] = increment(ens, localized, slot, field, l)


def localize_body(matrix, a, b, c, d, localized):
    localize(matrix, (a, b, c, d), localized)


def all_weighted(ens, grad, matrix, a, b, c, d, out):
    members, levels = out.shape[:2]
    for m in range(members):
        for l in range(levels):
            total = None
            for slot in range(ens.shape[0]):
                for field in range(ens.shape[1]):
                    term = ens[slot, field, m, l].astype(F32) * grad[slot, field, l]
                    total = term if total is None else total + term
            out[m, l] = total
    delocalize(matrix, out, (a, b, c, d))


def per_device(
    z_count,
    control,
    perturbations,
    obs_weight,
    slot_owner,
    zonal_shift,
    zonal_taps,
    meridional_taps,
    level_mixing,
):
    members, levels, band_rows, width = control.shape
    mem_count, lat_count = lax.axis_size("mem"), lax.axis_size("lat")
    mem = lax.axis_index("mem")
    direct = z_count > 0
    field_shape = (members, levels, band_rows, width)
    half_shape = (members, levels, 8, width)
    piece = shape(levels, band_rows, width)
    core_pairs = [(i, i ^ 1) for i in range(lat_count)]
    x_pairs = [(i, i + 1) for i in range(1, lat_count - 1, 2)]
    x_pairs += [(j, i) for i, j in x_pairs]
    swap_core = lambda v: lax.ppermute(v, "lat", core_pairs)
    swap_x = lambda v: lax.ppermute(v, "lat", x_pairs)
    tap_room = [pltpu.VMEM((BAND, 8, LANES), F32)]
    ins = {
        "shift": zonal_shift, "taps": zonal_taps, "control": control,
        "meridional": meridional_taps, "ens": perturbations,
    }
    results = {
        "near_x": shape(*half_shape), "control_v": shape(*field_shape),
        "taps_v": shape(*zonal_taps.shape), "meridional_v": shape(*meridional_taps.shape),
        "shift_x": shape(8, LANES, dtype=jnp.int32),
        "shift_core": shape(8, LANES, dtype=jnp.int32),
        "ens_v": shape(*perturbations.shape, dtype=BF16),
    }
    if direct:
        ins["obs"] = obs_weight
        results["obs_v"] = shape(*obs_weight.shape[1:])
    names = (*ins, *results, "taps_x", "shift_s", "sems")
    made = call(
        functools.partial(front_body, names), tuple(results.values()), "front", 1 << 19,
        *(pltpu.with_memory_space_constraint(v, pltpu.HBM) for v in ins.values()),
        specs=(HBM,) * len(ins),
        scratch=[
            *tap_room, pltpu.SMEM(zonal_shift.shape, jnp.int32), pltpu.SemaphoreType.DMA((7,)),
        ],
    )
    made = dict(zip(results, made))
    near_x, control_v, ens = made["near_x"], made["control_v"], made["ens_v"]
    far_x = swap_x(near_x)
    if direct:
        y_pairs = [(i, i ^ 1) for i in range(mem_count)]
        swap_y = lambda v: lax.ppermute(v, "mem", y_pairs)
        turn_z = lambda v, s: lax.ppermute(
            v, "mem", [(i, i ^ 2 * s) for i in range(mem_count)]
        )
        middle = [(i, i ^ 6) for i in range(2, mem_count - 2)]
        from_side = turn_z(made["obs_v"], 1)
        from_middle = lax.ppermute(made["obs_v"], "mem", middle)
    near_core = call(
        core_body, shape(*half_shape), "core", 1 << 19, made["shift_core"], made["taps_v"],
        control_v, specs=(VMEM,) * 3, scratch=tap_room,
    )
    far_core = swap_core(near_core)
    mixing = jnp.transpose(level_mixing, (1, 0, 2)).reshape(levels * band_rows, levels)
    matrix, transposed = call(
        functools.partial(build_matrix, lat_count),
        (shape(levels * band_rows, 32 * levels), shape(32 * levels, levels * band_rows)),
        "matrix", 1 << 16, made["meridional_v"], mixing, specs=(VMEM, VMEM), after=(near_core, far_x),
    )
    parts = (near_core, near_x, far_core, far_x)

    if direct:
        localized, first = call(
            functools.partial(first_body, 2), (shape(*field_shape), piece),
            "first", 1 << 20, slot_owner, matrix, *parts, ens,
            specs=(HBM,) + (VMEM,) * 6,
            scratch=[pltpu.SMEM((SLOTS,), jnp.int32), pltpu.SemaphoreType.DMA],
        )
        got_two = swap_y(first)
        pair, single = call(
            send_body, (shape(2, levels, band_rows, width), piece), "send", 1 << 20,
            slot_owner, ens, localized, specs=(SMEM, VMEM, VMEM), after=(from_side, from_middle),
        )
        pair, got_two = lax.optimization_barrier((pair, got_two))
        got_pair = swap_y(pair)
        two = call(
            functools.partial(meet_body, 2), piece, "meet2", 1 << 19,
            slot_owner, ens, localized, got_two, specs=(SMEM,) + (VMEM,) * 3,
        )
        arrived = {2: turn_z(two, 2)}
        mine, across = call(
            weight_pick, (piece,) * 2, "weight_pick", 1 << 18, slot_owner, made["obs_v"],
            from_side, from_middle, specs=(SMEM,) + (VMEM,) * 3, after=(two,),
        )
        one, three = call(
            meet_pair_body, (piece,) * 2, "meet13", 1 << 19,
            slot_owner, ens, localized, got_pair, specs=(SMEM,) + (VMEM,) * 3,
            after=(two, across),
        )
        arrived[1], arrived[3] = turn_z(one, 1), turn_z(three, 3)
        single, across, _ = lax.optimization_barrier((single, across, got_pair))
        got_own, from_y = swap_y(single), swap_y(across)
        grad = call(
            last_body, piece, "last", 1 << 19, slot_owner, ens, localized, got_own,
            arrived[1], arrived[2], arrived[3], mine, from_y,
            specs=(SMEM,) + (VMEM,) * 8,
        )
        own = {0: grad, 1: turn_z(grad, 1), 3: turn_z(grad, 3)}
        other = {0: swap_y(grad)}
        later, own[1], own[3], other[0] = lax.optimization_barrier((grad, own[1], own[3], other[0]))
        own[2] = turn_z(later, 2)
        other.update({s: swap_y(own[s]) for s in (1, 3, 2)})
        weighted = None
        groups = (((0, 0),), ((0, 1), (1, 0), (3, 0)), ((1, 1), (3, 1), (2, 0)), ((2, 1),))
        for group in groups:
            final = group == groups[-1]
            grads = [other[s] if o else own[s] for s, o in group]
            pieces = tuple(group)
            before = () if weighted is None else (weighted,)
            extra = (transposed,) if final else ()
            result = call(
                functools.partial(spread_body, pieces, weighted is None, final),
                (shape(*half_shape),) * 4 + (shape(*field_shape),) if final else shape(*field_shape),
                "spread%d" % group[0][0], 1 << 19,
                slot_owner, ens, *grads, *before, *extra,
                specs=(SMEM,) + (VMEM,) * (1 + len(grads) + len(before) + len(extra)),
            )
            weighted = result
        own_core, own_x, to_core, to_x = result[:4]
    else:
        localized = call(
            localize_body, shape(*field_shape), "localize", 1 << 20, matrix, *parts,
            specs=(VMEM,) * 5,
        )
        partial = call(
            all_increments, shape(SLOTS, ens.shape[1], levels, band_rows, width),
            "increments", 1 << 20, ens, localized, specs=(VMEM,) * 2,
        )
        weights = jnp.stack(
            [
                lax.psum(jnp.where(mem == slot_owner[t], obs_weight[0], 0.0), "mem")
                for t in range(SLOTS)
            ]
        )
        share = lax.psum_scatter(
            partial.reshape(-1, width), "mem", scatter_dimension=0, tiled=True
        )
        share_rows = share.shape[0]
        weight_rows = lax.dynamic_slice_in_dim(
            weights.reshape(-1, width), mem * share_rows, share_rows, 0
        )
        gathered = lax.all_gather(weight_rows * share, "mem", axis=0, tiled=True)
        own_core, own_x, to_core, to_x, _ = call(
            all_weighted, (shape(*half_shape),) * 4 + (shape(*field_shape),), "weighted",
            1 << 20, ens, gathered.reshape(partial.shape), transposed,
            specs=(VMEM,) * 3,
        )
    got_x, got_core = swap_x(to_x), swap_core(to_core)
    half = call(
        functools.partial(zonal_adjoint, 0), shape(*half_shape), "adjoint0", 1 << 19,
        made["shift_core"], made["taps_v"], control_v, own_core, got_core,
        specs=(VMEM,) * 5, scratch=tap_room,
    )
    return call(
        functools.partial(zonal_adjoint, 1), shape(*field_shape), "adjoint1", 1 << 19,
        made["shift_x"], made["taps_v"], control_v, own_x, got_x, half,
        specs=(VMEM,) * 6, scratch=tap_room,
    )


def solution(mesh):
    z_count = SLOTS if mesh.shape["mem"] == 2 * SLOTS else 0
    in_specs = (
        P("mem", None, "lat", None),
        P(None, None, "mem", None, "lat", None),
        P("mem", None, None, "lat", None),
        P(),
        P("lat"),
        P("lat", None),
        P("lat", None),
        P("lat", None, None),
    )
    out_specs = P("mem", None, "lat", None)
    return jax.shard_map(
        functools.partial(per_device, z_count),
        mesh=mesh, in_specs=in_specs, out_specs=out_specs, check_vma=False,
    )
```

```python
import functools

import jax
import jax.numpy as jnp
from jax import lax
from jax.experimental import pallas as pl
from jax.experimental.pallas import tpu as pltpu
from jax.sharding import PartitionSpec as P

SLOTS = 4
BAND = 17
HALF = BAND // 2
LANES = 128
F32 = jnp.float32
BF16 = jnp.bfloat16

VMEM = pl.BlockSpec(memory_space=pltpu.VMEM)
SMEM = pl.BlockSpec(memory_space=pltpu.SMEM)
ANY = pl.BlockSpec(memory_space=pl.ANY)
HBM = pl.BlockSpec(memory_space=pltpu.HBM)


def call(body, outs, name, cost, *operands, specs, scratch=(), after=()):
    count, extra = len(operands), len(after)

    def kernel(*refs):
        body(*refs[:count], *refs[count + extra :])

    return pl.pallas_call(
        kernel,
        out_shape=outs,
        in_specs=list(specs) + [ANY] * extra,
        out_specs=jax.tree.map(lambda _: VMEM, outs),
        scratch_shapes=list(scratch),
        compiler_params=pltpu.CompilerParams(vmem_limit_bytes=16 << 20),
        cost_estimate=pl.CostEstimate(flops=cost, bytes_accessed=cost, transcendentals=0),
        name=name,
    )(*operands, *after)


def parity():
    return lax.axis_index("lat") & 1


def own_y():
    return lax.axis_index("mem") & 1


def own_z():
    return lax.axis_index("mem") >> 1


def entry_at(owners, step, value):
    place = own_z() ^ step
    found = jnp.int32(0)
    for t in range(SLOTS):
        rank = jnp.int32(0)
        for u in range(SLOTS):
            if u != t:
                rank += jnp.where(owners[u] < owners[t], 1, 0)
        found = jnp.where(rank == place, value(t), found)
    return found


def slot_at(owners, step):
    return entry_at(owners, step, lambda t: jnp.int32(t))


def owner_at(owners, step):
    return entry_at(owners, step, lambda t: owners[t])


def shape(*dims, dtype=F32):
    return jax.ShapeDtypeStruct(dims, dtype)


def shifted(columns, amount):
    lane = lax.broadcasted_iota(jnp.int32, columns[0].shape, 1)
    turned = [pltpu.roll(c, amount, 1) for c in columns]
    return [
        jnp.where(lane < amount, turned[i - 1], turned[i]) for i in range(len(columns))
    ]


def circle_filter(columns, amount, tap):
    count = len(columns)
    lane = lax.broadcasted_iota(jnp.int32, columns[0].shape, 1)
    fine = amount & (LANES - 1)
    source = (lane - fine) & (LANES - 1)
    turned = [
        jnp.take_along_axis(c, source, axis=1, mode="promise_in_bounds") for c in columns
    ]
    wraps = lane < fine
    columns = [jnp.where(wraps, turned[i - 1], turned[i]) for i in range(count)]
    step = 1
    while step < count:
        moved = (amount & (step * LANES)) != 0
        columns = [jnp.where(moved, columns[i - step], columns[i]) for i in range(count)]
        step *= 2
    near = [columns]
    for offset in range(1, 4):
        near.append(shifted(columns, offset))
    total = [tap(BAND - 1) * c for c in columns]
    for group in range((BAND - 1) // 4 - 1, -1, -1):
        total = shifted(total, 4)
        for offset in range(4):
            factor = tap(4 * group + offset)
            total = [t + factor * c for t, c in zip(total, near[offset])]
    return total


def row_shifts(shifts, first):
    row = lax.broadcasted_iota(jnp.int32, (8, LANES), 0)
    amounts = jnp.zeros((8, LANES), jnp.int32)
    for r in range(8):
        amounts = jnp.where(row == r, shifts[first + r], amounts)
    return amounts


def spread_taps(taps, first, spread):
    block = taps[pl.ds(first, 8), :]
    for k in range(BAND):
        spread[k] = jnp.broadcast_to(block[:, k : k + 1], (8, LANES))


def tiles(width):
    return [slice(i * LANES, (i + 1) * LANES) for i in range(width // LANES)]


def half_start(which):
    odd = parity()
    return pl.multiple_of((1 - odd if which == 0 else odd) * 8, 8)


def zonal_forward(first, shifts, taps, control, out):
    members, levels, _, width = control.shape
    amount = (width - HALF - shifts[...]) & (width - 1)

    def step(m, carry):
        for l in range(levels):
            columns = [control[m, l, pl.ds(first, 8), cut] for cut in tiles(width)]
            result = circle_filter(columns, amount, lambda k: taps[BAND - 1 - k])
            for cut, value in zip(tiles(width), result):
                out[m, l, :, cut] = value
        return carry

    lax.fori_loop(0, members, step, 0)


def front_body(names, *refs):
    r = dict(zip(names, refs))
    sems = r["sems"]
    first_x, first_core = half_start(1), half_start(0)
    rows_x, rows_core = pl.ds(first_x, 8), pl.ds(first_core, 8)
    moves = [
        (r["shift"], r["shift_s"]),
        (r["taps"], r["taps_v"]),
        (r["control"].at[:, :, rows_x], r["control_v"].at[:, :, rows_x]),
    ]
    moves.append((r["control"].at[:, :, rows_core], r["control_v"].at[:, :, rows_core]))
    moves.append((r["meridional"], r["meridional_v"]))
    moves.append((r["mixing"], r["mixing_v"]))
    if "obs" in r:
        moves.append((r["obs"].at[0], r["obs_v"]))
    moves.append((r["ens"], r["ens_v"]))
    copies = [pltpu.make_async_copy(a, b, sems.at[i]) for i, (a, b) in enumerate(moves)]
    for copy in copies:
        copy.start()
    for copy in copies[:3]:
        copy.wait()
    r["shift_x"][...] = row_shifts(r["shift_s"], first_x)
    r["shift_core"][...] = row_shifts(r["shift_s"], first_core)
    spread_taps(r["taps_v"], first_x, r["taps_x"])
    zonal_forward(first_x, r["shift_x"], r["taps_x"], r["control_v"], r["near_x"])
    for copy in copies[3:]:
        copy.wait()


def core_body(shifts, taps_v, control, out, taps):
    first = half_start(0)
    spread_taps(taps_v, first, taps)
    zonal_forward(first, shifts, taps, control, out)


def zonal_adjoint(which, shifts, taps_v, control, own, got, *refs):
    other, out, taps = (None, *refs) if which == 0 else refs
    members, levels, _, width = control.shape
    first = half_start(which)
    amount = (shifts[...] - HALF) & (width - 1)
    spread_taps(taps_v, first, taps)

    def step(m, carry):
        for l in range(levels):
            columns = [own[m, l, :, cut] + got[m, l, :, cut] for cut in tiles(width)]
            result = circle_filter(columns, amount, lambda k: taps[k])
            for cut, value in zip(tiles(width), result):
                total = control[m, l, pl.ds(first, 8), cut] + value
                if which == 0:
                    out[m, l, :, cut] = total
                else:
                    out[m, l, pl.ds(first, 8), cut] = total
                    out[m, l, pl.ds(8 - first, 8), cut] = other[m, l, :, cut]
        return carry

    lax.fori_loop(0, members, step, 0)


def build_matrix(lat_count, taps_ref, mixing_ref, matrix, transposed):
    band_rows, levels = taps_ref.shape[0], mixing_ref.shape[1]
    rows, columns = matrix.shape
    odd, lat = parity(), lax.axis_index("lat")
    alone = (lat == 0) | (lat == lat_count - 1)
    column = lax.broadcasted_iota(jnp.int32, (band_rows, columns), 1)
    row = lax.broadcasted_iota(jnp.int32, (band_rows, columns), 0)
    block, level, inner = column // (8 * levels), (column // 8) % levels, column % 8
    even_start = jnp.where(block == 0, 16, jnp.where(block == 1, 8, jnp.where(block == 2, 24, 0)))
    odd_start = jnp.where(block == 0, 8, jnp.where(block == 1, 16, jnp.where(block == 2, 0, 24)))
    reach = jnp.where(odd == 1, odd_start, even_start) + inner - row
    band = jnp.zeros((band_rows, columns), F32)
    for k in range(BAND):
        band = jnp.where(reach == k, taps_ref[:, k : k + 1], band)
    band = jnp.where((block == 3) & alone, 0.0, band)
    same = lax.broadcasted_iota(jnp.int32, (band_rows, band_rows), 0) == (
        lax.broadcasted_iota(jnp.int32, (band_rows, band_rows), 1)
    )
    for a in range(levels):
        mixing = mixing_ref[a]
        factor = jnp.zeros((band_rows, columns), F32)
        for b in range(levels):
            by_lane = jnp.broadcast_to(mixing[b : b + 1, :], (band_rows, band_rows))
            by_row = jnp.sum(jnp.where(same, by_lane, 0.0), axis=1, keepdims=True)
            factor = jnp.where(level == b, by_row, factor)
        matrix[a * band_rows : (a + 1) * band_rows, :] = factor * band
    transposed[...] = matrix[...].T


def halves(value):
    high = value.astype(BF16)
    return high, (value - high.astype(F32)).astype(BF16)


def product(left, right):
    (lh, ll), (rh, rl) = left, right
    dot = functools.partial(jnp.dot, preferred_element_type=F32)
    return dot(lh, rh) + (dot(lh, rl) + dot(ll, rh))


CHUNK = 256


def localize(matrix, parts, out):
    members, levels, band_rows, width = out.shape
    left = halves(matrix[...])
    for m in range(members):
        for c in range(0, width, CHUNK):
            cut = slice(c, c + CHUNK)
            stack = jnp.concatenate(
                [p[m, l, :, cut] for p in parts for l in range(levels)], axis=0
            )
            result = product(left, halves(stack))
            for l in range(levels):
                out[m, l, :, cut] = result[l * band_rows : (l + 1) * band_rows]


def delocalize(matrix, weighted, parts):
    members, levels, band_rows, width = weighted.shape
    left = halves(matrix[...])
    for m in range(members):
        for c in range(0, width, CHUNK):
            cut = slice(c, c + CHUNK)
            stack = jnp.concatenate([weighted[m, l, :, cut] for l in range(levels)], axis=0)
            result = product(left, halves(stack))
            for p, part in enumerate(parts):
                for l in range(levels):
                    start = (p * levels + l) * 8
                    part[m, l, :, cut] = result[start : start + 8]


def increment(ens, localized, slot, field, l):
    total = None
    for m in range(localized.shape[0]):
        term = ens[slot, field, m, l].astype(F32) * localized[m, l]
        total = term if total is None else total + term
    return total


def weight_pick(owners, here, side, middle, mine, across):
    place = owner_at(owners, 0) >> 1
    for found, weights in (
        (place == own_z(), here),
        (place == own_z() ^ 1, side),
        (place == own_z() ^ 3, middle),
    ):

        @pl.when(found)
        def _(weights=weights):
            mine[...] = weights[own_y()]
            across[...] = weights[1 - own_y()]


def first_body(step, owners_hbm, matrix, a, b, c, d, ens, localized, send, owners, sem):
    copy = pltpu.make_async_copy(owners_hbm, owners, sem)
    copy.start()
    localize(matrix, (a, b, c, d), localized)
    copy.wait()
    slot = slot_at(owners, step)
    for l in range(localized.shape[1]):
        send[l] = increment(ens, localized, slot, 1 - own_y(), l)


def send_body(owners, ens, localized, pair, single):
    for step, send in ((1, pair.at[0]), (3, pair.at[1]), (0, single)):
        slot = slot_at(owners, step)
        for l in range(localized.shape[1]):
            send[l] = increment(ens, localized, slot, 1 - own_y(), l)


def meet_body(step, owners, ens, localized, got, out):
    slot = slot_at(owners, step)
    for l in range(localized.shape[1]):
        out[l] = increment(ens, localized, slot, own_y(), l) + got[l]


def meet_pair_body(owners, ens, localized, got, *outs):
    for i, (step, out) in enumerate(zip((1, 3), outs)):
        meet_body(step, owners, ens, localized, got.at[i], out)


def last_body(owners, ens, localized, got_y, got_1, got_2, got_3, mine, from_y, out):
    slot = slot_at(owners, 0)
    held = (owner_at(owners, 0) & 1) == own_y()
    for here, weight in ((held, mine), (jnp.logical_not(held), from_y)):

        @pl.when(here)
        def _(weight=weight):
            for l in range(localized.shape[1]):
                out[l] = weight[l] * (
                    increment(ens, localized, slot, own_y(), l)
                    + got_y[l]
                    + (got_1[l] + got_2[l] + got_3[l])
                )


def spread_body(pieces, first, final, owners, ens, *refs):
    refs = list(refs)
    grads = [refs.pop(0) for _ in pieces]
    before = None if first else refs.pop(0)
    matrix = refs.pop(0) if final else None
    out = refs[-1] if final else refs[0]
    members, levels = out.shape[:2]
    places = [
        (slot_at(owners, step), 1 - own_y() if other else own_y()) for step, other in pieces
    ]
    for m in range(members):
        for l in range(levels):
            total = None if before is None else before[m, l]
            for (slot, field), grad in zip(places, grads):
                term = ens[slot, field, m, l].astype(F32) * grad[l]
                total = term if total is None else total + term
            out[m, l] = total
    if final:
        delocalize(matrix, out, refs[:4])


def all_increments(ens, localized, out):
    for slot in range(out.shape[0]):
        for field in range(out.shape[1]):
            for l in range(out.shape[2]):
                out[slot, field, l] = increment(ens, localized, slot, field, l)


def localize_body(matrix, a, b, c, d, localized):
    localize(matrix, (a, b, c, d), localized)


def all_weighted(ens, grad, matrix, a, b, c, d, out):
    members, levels = out.shape[:2]
    for m in range(members):
        for l in range(levels):
            total = None
            for slot in range(ens.shape[0]):
                for field in range(ens.shape[1]):
                    term = ens[slot, field, m, l].astype(F32) * grad[slot, field, l]
                    total = term if total is None else total + term
            out[m, l] = total
    delocalize(matrix, out, (a, b, c, d))


def per_device(
    z_count,
    control,
    perturbations,
    obs_weight,
    slot_owner,
    zonal_shift,
    zonal_taps,
    meridional_taps,
    level_mixing,
):
    members, levels, band_rows, width = control.shape
    mem_count, lat_count = lax.axis_size("mem"), lax.axis_size("lat")
    mem = lax.axis_index("mem")
    direct = z_count > 0
    field_shape = (members, levels, band_rows, width)
    half_shape = (members, levels, 8, width)
    piece = shape(levels, band_rows, width)
    core_pairs = [(i, i ^ 1) for i in range(lat_count)]
    x_pairs = [(i, i + 1) for i in range(1, lat_count - 1, 2)]
    x_pairs += [(j, i) for i, j in x_pairs]
    swap_core = lambda v: lax.ppermute(v, "lat", core_pairs)
    swap_x = lambda v: lax.ppermute(v, "lat", x_pairs)
    tap_room = [pltpu.VMEM((BAND, 8, LANES), F32)]
    ins = {
        "shift": zonal_shift, "taps": zonal_taps, "control": control,
        "meridional": meridional_taps, "ens": perturbations,
        "mixing": jnp.transpose(level_mixing, (1, 2, 0)),
    }
    results = {
        "near_x": shape(*half_shape), "control_v": shape(*field_shape),
        "taps_v": shape(*zonal_taps.shape), "meridional_v": shape(*meridional_taps.shape),
        "shift_x": shape(8, LANES, dtype=jnp.int32),
        "shift_core": shape(8, LANES, dtype=jnp.int32),
        "ens_v": shape(*perturbations.shape, dtype=BF16),
        "mixing_v": shape(levels, levels, band_rows),
    }
    if direct:
        ins["obs"] = obs_weight
        results["obs_v"] = shape(*obs_weight.shape[1:])
    names = (*ins, *results, "taps_x", "shift_s", "sems")
    made = call(
        functools.partial(front_body, names), tuple(results.values()), "front", 1 << 19,
        *(pltpu.with_memory_space_constraint(v, pltpu.HBM) for v in ins.values()),
        specs=(HBM,) * len(ins),
        scratch=[
            *tap_room, pltpu.SMEM(zonal_shift.shape, jnp.int32), pltpu.SemaphoreType.DMA((8,)),
        ],
    )
    made = dict(zip(results, made))
    near_x, control_v, ens = made["near_x"], made["control_v"], made["ens_v"]
    far_x = swap_x(near_x)
    if direct:
        y_pairs = [(i, i ^ 1) for i in range(mem_count)]
        swap_y = lambda v: lax.ppermute(v, "mem", y_pairs)
        turn_z = lambda v, s: lax.ppermute(
            v, "mem", [(i, i ^ 2 * s) for i in range(mem_count)]
        )
        middle = [(i, i ^ 6) for i in range(2, mem_count - 2)]
        from_side = turn_z(made["obs_v"], 1)
        from_middle = lax.ppermute(made["obs_v"], "mem", middle)
    near_core = call(
        core_body, shape(*half_shape), "core", 1 << 19, made["shift_core"], made["taps_v"],
        control_v, specs=(VMEM,) * 3, scratch=tap_room,
    )
    far_core = swap_core(near_core)
    matrix, transposed = call(
        functools.partial(build_matrix, lat_count),
        (shape(levels * band_rows, 32 * levels), shape(32 * levels, levels * band_rows)),
        "matrix", 1 << 16, made["meridional_v"], made["mixing_v"], specs=(VMEM, VMEM), after=(near_core, far_x),
    )
    parts = (near_core, near_x, far_core, far_x)

    if direct:
        localized, first = call(
            functools.partial(first_body, 2), (shape(*field_shape), piece),
            "first", 1 << 20, slot_owner, matrix, *parts, ens,
            specs=(HBM,) + (VMEM,) * 6,
            scratch=[pltpu.SMEM((SLOTS,), jnp.int32), pltpu.SemaphoreType.DMA],
        )
        got_two = swap_y(first)
        pair, single = call(
            send_body, (shape(2, levels, band_rows, width), piece), "send", 1 << 20,
            slot_owner, ens, localized, specs=(SMEM, VMEM, VMEM), after=(from_side, from_middle),
        )
        pair, got_two = lax.optimization_barrier((pair, got_two))
        got_pair = swap_y(pair)
        two = call(
            functools.partial(meet_body, 2), piece, "meet2", 1 << 19,
            slot_owner, ens, localized, got_two, specs=(SMEM,) + (VMEM,) * 3,
        )
        arrived = {2: turn_z(two, 2)}
        mine, across = call(
            weight_pick, (piece,) * 2, "weight_pick", 1 << 18, slot_owner, made["obs_v"],
            from_side, from_middle, specs=(SMEM,) + (VMEM,) * 3, after=(two,),
        )
        one, three = call(
            meet_pair_body, (piece,) * 2, "meet13", 1 << 19,
            slot_owner, ens, localized, got_pair, specs=(SMEM,) + (VMEM,) * 3,
            after=(two, across),
        )
        arrived[1], arrived[3] = turn_z(one, 1), turn_z(three, 3)
        single, across, _ = lax.optimization_barrier((single, across, got_pair))
        got_own, from_y = swap_y(single), swap_y(across)
        grad = call(
            last_body, piece, "last", 1 << 19, slot_owner, ens, localized, got_own,
            arrived[1], arrived[2], arrived[3], mine, from_y,
            specs=(SMEM,) + (VMEM,) * 8,
        )
        own = {0: grad, 1: turn_z(grad, 1), 3: turn_z(grad, 3)}
        other = {0: swap_y(grad)}
        later, own[1], own[3], other[0] = lax.optimization_barrier((grad, own[1], own[3], other[0]))
        own[2] = turn_z(later, 2)
        other.update({s: swap_y(own[s]) for s in (1, 3, 2)})
        weighted = None
        groups = (((0, 0),), ((0, 1), (1, 0), (3, 0)), ((1, 1), (3, 1), (2, 0)), ((2, 1),))
        for group in groups:
            final = group == groups[-1]
            grads = [other[s] if o else own[s] for s, o in group]
            pieces = tuple(group)
            before = () if weighted is None else (weighted,)
            extra = (transposed,) if final else ()
            result = call(
                functools.partial(spread_body, pieces, weighted is None, final),
                (shape(*half_shape),) * 4 + (shape(*field_shape),) if final else shape(*field_shape),
                "spread%d" % group[0][0], 1 << 19,
                slot_owner, ens, *grads, *before, *extra,
                specs=(SMEM,) + (VMEM,) * (1 + len(grads) + len(before) + len(extra)),
            )
            weighted = result
        own_core, own_x, to_core, to_x = result[:4]
    else:
        localized = call(
            localize_body, shape(*field_shape), "localize", 1 << 20, matrix, *parts,
            specs=(VMEM,) * 5,
        )
        partial = call(
            all_increments, shape(SLOTS, ens.shape[1], levels, band_rows, width),
            "increments", 1 << 20, ens, localized, specs=(VMEM,) * 2,
        )
        weights = jnp.stack(
            [
                lax.psum(jnp.where(mem == slot_owner[t], obs_weight[0], 0.0), "mem")
                for t in range(SLOTS)
            ]
        )
        share = lax.psum_scatter(
            partial.reshape(-1, width), "mem", scatter_dimension=0, tiled=True
        )
        share_rows = share.shape[0]
        weight_rows = lax.dynamic_slice_in_dim(
            weights.reshape(-1, width), mem * share_rows, share_rows, 0
        )
        gathered = lax.all_gather(weight_rows * share, "mem", axis=0, tiled=True)
        own_core, own_x, to_core, to_x, _ = call(
            all_weighted, (shape(*half_shape),) * 4 + (shape(*field_shape),), "weighted",
            1 << 20, ens, gathered.reshape(partial.shape), transposed,
            specs=(VMEM,) * 3,
        )
    got_x, got_core = swap_x(to_x), swap_core(to_core)
    half = call(
        functools.partial(zonal_adjoint, 0), shape(*half_shape), "adjoint0", 1 << 19,
        made["shift_core"], made["taps_v"], control_v, own_core, got_core,
        specs=(VMEM,) * 5, scratch=tap_room,
    )
    return call(
        functools.partial(zonal_adjoint, 1), shape(*field_shape), "adjoint1", 1 << 19,
        made["shift_x"], made["taps_v"], control_v, own_x, got_x, half,
        specs=(VMEM,) * 6, scratch=tap_room,
    )


def solution(mesh):
    z_count = SLOTS if mesh.shape["mem"] == 2 * SLOTS else 0
    in_specs = (
        P("mem", None, "lat", None),
        P(None, None, "mem", None, "lat", None),
        P("mem", None, None, "lat", None),
        P(),
        P("lat"),
        P("lat", None),
        P("lat", None),
        P("lat", None, None),
    )
    out_specs = P("mem", None, "lat", None)
    return jax.shard_map(
        functools.partial(per_device, z_count),
        mesh=mesh, in_specs=in_specs, out_specs=out_specs, check_vma=False,
    )
```

```python
import functools

import jax
import jax.numpy as jnp
from jax import lax
from jax.experimental import pallas as pl
from jax.experimental.pallas import tpu as pltpu
from jax.sharding import PartitionSpec as P

SLOTS = 4
BAND = 17
HALF = BAND // 2
LANES = 128
F32 = jnp.float32
BF16 = jnp.bfloat16

VMEM = pl.BlockSpec(memory_space=pltpu.VMEM)
SMEM = pl.BlockSpec(memory_space=pltpu.SMEM)
ANY = pl.BlockSpec(memory_space=pl.ANY)
HBM = pl.BlockSpec(memory_space=pltpu.HBM)


def call(body, outs, name, cost, *operands, specs, scratch=(), after=()):
    count, extra = len(operands), len(after)

    def kernel(*refs):
        body(*refs[:count], *refs[count + extra :])

    return pl.pallas_call(
        kernel,
        out_shape=outs,
        in_specs=list(specs) + [ANY] * extra,
        out_specs=jax.tree.map(lambda _: VMEM, outs),
        scratch_shapes=list(scratch),
        compiler_params=pltpu.CompilerParams(vmem_limit_bytes=16 << 20),
        cost_estimate=pl.CostEstimate(flops=cost, bytes_accessed=cost, transcendentals=0),
        name=name,
    )(*operands, *after)


def parity():
    return lax.axis_index("lat") & 1


def own_y():
    return lax.axis_index("mem") & 1


def own_z():
    return lax.axis_index("mem") >> 1


def entry_at(owners, step, value):
    place = own_z() ^ step
    found = jnp.int32(0)
    for t in range(SLOTS):
        rank = jnp.int32(0)
        for u in range(SLOTS):
            if u != t:
                rank += jnp.where(owners[u] < owners[t], 1, 0)
        found = jnp.where(rank == place, value(t), found)
    return found


def slot_at(owners, step):
    return entry_at(owners, step, lambda t: jnp.int32(t))


def owner_at(owners, step):
    return entry_at(owners, step, lambda t: owners[t])


def shape(*dims, dtype=F32):
    return jax.ShapeDtypeStruct(dims, dtype)


def shifted(columns, amount):
    lane = lax.broadcasted_iota(jnp.int32, columns[0].shape, 1)
    turned = [pltpu.roll(c, amount, 1) for c in columns]
    return [
        jnp.where(lane < amount, turned[i - 1], turned[i]) for i in range(len(columns))
    ]


def circle_filter(columns, amount, tap):
    count = len(columns)
    lane = lax.broadcasted_iota(jnp.int32, columns[0].shape, 1)
    fine = amount & (LANES - 1)
    source = (lane - fine) & (LANES - 1)
    turned = [
        jnp.take_along_axis(c, source, axis=1, mode="promise_in_bounds") for c in columns
    ]
    wraps = lane < fine
    columns = [jnp.where(wraps, turned[i - 1], turned[i]) for i in range(count)]
    step = 1
    while step < count:
        moved = (amount & (step * LANES)) != 0
        columns = [jnp.where(moved, columns[i - step], columns[i]) for i in range(count)]
        step *= 2
    near = [columns]
    for offset in range(1, 4):
        near.append(shifted(columns, offset))
    total = [tap(BAND - 1) * c for c in columns]
    for group in range((BAND - 1) // 4 - 1, -1, -1):
        total = shifted(total, 4)
        for offset in range(4):
            factor = tap(4 * group + offset)
            total = [t + factor * c for t, c in zip(total, near[offset])]
    return total


def row_shifts(shifts, first):
    row = lax.broadcasted_iota(jnp.int32, (8, LANES), 0)
    amounts = jnp.zeros((8, LANES), jnp.int32)
    for r in range(8):
        amounts = jnp.where(row == r, shifts[first + r], amounts)
    return amounts


def spread_taps(taps, first, spread):
    block = taps[pl.ds(first, 8), :]
    for k in range(BAND):
        spread[k] = jnp.broadcast_to(block[:, k : k + 1], (8, LANES))


def tiles(width):
    return [slice(i * LANES, (i + 1) * LANES) for i in range(width // LANES)]


def half_start(which):
    odd = parity()
    return pl.multiple_of((1 - odd if which == 0 else odd) * 8, 8)


def zonal_forward(first, shifts, taps, control, out):
    members, levels, _, width = control.shape
    amount = (width - HALF - shifts[...]) & (width - 1)

    def step(m, carry):
        for l in range(levels):
            columns = [control[m, l, pl.ds(first, 8), cut] for cut in tiles(width)]
            result = circle_filter(columns, amount, lambda k: taps[BAND - 1 - k])
            for cut, value in zip(tiles(width), result):
                out[m, l, :, cut] = value
        return carry

    lax.fori_loop(0, members, step, 0)


def front_body(names, *refs):
    r = dict(zip(names, refs))
    sems = r["sems"]
    first_x, first_core = half_start(1), half_start(0)
    rows_x, rows_core = pl.ds(first_x, 8), pl.ds(first_core, 8)
    moves = [
        (r["shift"], r["shift_s"]),
        (r["taps"], r["taps_v"]),
        (r["control"].at[:, :, rows_x], r["control_v"].at[:, :, rows_x]),
    ]
    if "obs" in r:
        moves.append((r["obs"].at[0, 1 - own_y()], r["weight_sent"]))
    moves.append((r["control"].at[:, :, rows_core], r["control_v"].at[:, :, rows_core]))
    moves.append((r["meridional"], r["meridional_v"]))
    moves.append((r["mixing"], r["mixing_v"]))
    if "obs" in r:
        moves.append((r["obs"].at[0, own_y()], r["obs_v"]))
    moves.append((r["ens"], r["ens_v"]))
    copies = [pltpu.make_async_copy(a, b, sems.at[i]) for i, (a, b) in enumerate(moves)]
    for copy in copies:
        copy.start()
    for copy in copies[:3]:
        copy.wait()
    r["shift_x"][...] = row_shifts(r["shift_s"], first_x)
    r["shift_core"][...] = row_shifts(r["shift_s"], first_core)
    spread_taps(r["taps_v"], first_x, r["taps_x"])
    zonal_forward(first_x, r["shift_x"], r["taps_x"], r["control_v"], r["near_x"])
    for copy in copies[3:]:
        copy.wait()


def core_body(shifts, taps_v, control, out, taps):
    first = half_start(0)
    spread_taps(taps_v, first, taps)
    zonal_forward(first, shifts, taps, control, out)


def zonal_adjoint(which, shifts, taps_v, control, own, got, *refs):
    other, out, taps = (None, *refs) if which == 0 else refs
    members, levels, _, width = control.shape
    first = half_start(which)
    amount = (shifts[...] - HALF) & (width - 1)
    spread_taps(taps_v, first, taps)

    def step(m, carry):
        for l in range(levels):
            columns = [own[m, l, :, cut] + got[m, l, :, cut] for cut in tiles(width)]
            result = circle_filter(columns, amount, lambda k: taps[k])
            for cut, value in zip(tiles(width), result):
                total = control[m, l, pl.ds(first, 8), cut] + value
                if which == 0:
                    out[m, l, :, cut] = total
                else:
                    out[m, l, pl.ds(first, 8), cut] = total
                    out[m, l, pl.ds(8 - first, 8), cut] = other[m, l, :, cut]
        return carry

    lax.fori_loop(0, members, step, 0)


def build_matrix(lat_count, taps_ref, mixing_ref, matrix, transposed):
    band_rows, levels = taps_ref.shape[0], mixing_ref.shape[1]
    rows, columns = matrix.shape
    odd, lat = parity(), lax.axis_index("lat")
    alone = (lat == 0) | (lat == lat_count - 1)
    column = lax.broadcasted_iota(jnp.int32, (band_rows, columns), 1)
    row = lax.broadcasted_iota(jnp.int32, (band_rows, columns), 0)
    block, level, inner = column // (8 * levels), (column // 8) % levels, column % 8
    even_start = jnp.where(block == 0, 16, jnp.where(block == 1, 8, jnp.where(block == 2, 24, 0)))
    odd_start = jnp.where(block == 0, 8, jnp.where(block == 1, 16, jnp.where(block == 2, 0, 24)))
    reach = jnp.where(odd == 1, odd_start, even_start) + inner - row
    band = jnp.zeros((band_rows, columns), F32)
    for k in range(BAND):
        band = jnp.where(reach == k, taps_ref[:, k : k + 1], band)
    band = jnp.where((block == 3) & alone, 0.0, band)
    same = lax.broadcasted_iota(jnp.int32, (band_rows, band_rows), 0) == (
        lax.broadcasted_iota(jnp.int32, (band_rows, band_rows), 1)
    )
    for a in range(levels):
        mixing = mixing_ref[a]
        factor = jnp.zeros((band_rows, columns), F32)
        for b in range(levels):
            by_lane = jnp.broadcast_to(mixing[b : b + 1, :], (band_rows, band_rows))
            by_row = jnp.sum(jnp.where(same, by_lane, 0.0), axis=1, keepdims=True)
            factor = jnp.where(level == b, by_row, factor)
        matrix[a * band_rows : (a + 1) * band_rows, :] = factor * band
    transposed[...] = matrix[...].T


def halves(value):
    high = value.astype(BF16)
    return high, (value - high.astype(F32)).astype(BF16)


def product(left, right):
    (lh, ll), (rh, rl) = left, right
    dot = functools.partial(jnp.dot, preferred_element_type=F32)
    return dot(lh, rh) + (dot(lh, rl) + dot(ll, rh))


CHUNK = 256


def localize(matrix, parts, out):
    members, levels, band_rows, width = out.shape
    left = halves(matrix[...])
    for m in range(members):
        for c in range(0, width, CHUNK):
            cut = slice(c, c + CHUNK)
            stack = jnp.concatenate(
                [p[m, l, :, cut] for p in parts for l in range(levels)], axis=0
            )
            result = product(left, halves(stack))
            for l in range(levels):
                out[m, l, :, cut] = result[l * band_rows : (l + 1) * band_rows]


def delocalize(matrix, weighted, parts):
    members, levels, band_rows, width = weighted.shape
    left = halves(matrix[...])
    for m in range(members):
        for c in range(0, width, CHUNK):
            cut = slice(c, c + CHUNK)
            stack = jnp.concatenate([weighted[m, l, :, cut] for l in range(levels)], axis=0)
            result = product(left, halves(stack))
            for p, part in enumerate(parts):
                for l in range(levels):
                    start = (p * levels + l) * 8
                    part[m, l, :, cut] = result[start : start + 8]


def increment(ens, localized, slot, field, l):
    total = None
    for m in range(localized.shape[0]):
        term = ens[slot, field, m, l].astype(F32) * localized[m, l]
        total = term if total is None else total + term
    return total


def weight_pick(owners, here, from_y, mine, side, middle):
    for step, out in ((0, mine), (1, side), (3, middle)):
        held = (owner_at(owners, step) & 1) == own_y()

        @pl.when(held)
        def _(out=out):
            out[...] = here[...]

        @pl.when(jnp.logical_not(held))
        def _(out=out):
            out[...] = from_y[...]


def first_body(step, owners_hbm, matrix, a, b, c, d, ens, localized, send, owners, sem):
    copy = pltpu.make_async_copy(owners_hbm, owners, sem)
    copy.start()
    localize(matrix, (a, b, c, d), localized)
    copy.wait()
    slot = slot_at(owners, step)
    for l in range(localized.shape[1]):
        send[l] = increment(ens, localized, slot, 1 - own_y(), l)


def send_body(owners, ens, localized, pair, single):
    for step, send in ((1, pair.at[0]), (3, pair.at[1]), (0, single)):
        slot = slot_at(owners, step)
        for l in range(localized.shape[1]):
            send[l] = increment(ens, localized, slot, 1 - own_y(), l)


def meet_body(step, owners, ens, localized, got, out):
    slot = slot_at(owners, step)
    for l in range(localized.shape[1]):
        out[l] = increment(ens, localized, slot, own_y(), l) + got[l]


def meet_pair_body(owners, ens, localized, got, *outs):
    for i, (step, out) in enumerate(zip((1, 3), outs)):
        meet_body(step, owners, ens, localized, got.at[i], out)


def last_body(
    owners, ens, localized, got_y, got_1, got_2, got_3, mine, side, middle, out
):
    slot, place = slot_at(owners, 0), owner_at(owners, 0) >> 1
    for found, weight in (
        (place == own_z(), mine),
        (place == own_z() ^ 1, side),
        (place == own_z() ^ 3, middle),
    ):

        @pl.when(found)
        def _(weight=weight):
            for l in range(localized.shape[1]):
                out[l] = weight[l] * (
                    increment(ens, localized, slot, own_y(), l)
                    + got_y[l]
                    + (got_1[l] + got_2[l] + got_3[l])
                )


def spread_body(pieces, first, final, owners, ens, *refs):
    refs = list(refs)
    grads = [refs.pop(0) for _ in pieces]
    before = None if first else refs.pop(0)
    matrix = refs.pop(0) if final else None
    out = refs[-1] if final else refs[0]
    members, levels = out.shape[:2]
    places = [
        (slot_at(owners, step), 1 - own_y() if other else own_y()) for step, other in pieces
    ]
    for m in range(members):
        for l in range(levels):
            total = None if before is None else before[m, l]
            for (slot, field), grad in zip(places, grads):
                term = ens[slot, field, m, l].astype(F32) * grad[l]
                total = term if total is None else total + term
            out[m, l] = total
    if final:
        delocalize(matrix, out, refs[:4])


def all_increments(ens, localized, out):
    for slot in range(out.shape[0]):
        for field in range(out.shape[1]):
            for l in range(out.shape[2]):
                out[slot, field, l] = increment(ens, localized, slot, field, l)


def localize_body(matrix, a, b, c, d, localized):
    localize(matrix, (a, b, c, d), localized)


def all_weighted(ens, grad, matrix, a, b, c, d, out):
    members, levels = out.shape[:2]
    for m in range(members):
        for l in range(levels):
            total = None
            for slot in range(ens.shape[0]):
                for field in range(ens.shape[1]):
                    term = ens[slot, field, m, l].astype(F32) * grad[slot, field, l]
                    total = term if total is None else total + term
            out[m, l] = total
    delocalize(matrix, out, (a, b, c, d))


def per_device(
    z_count,
    control,
    perturbations,
    obs_weight,
    slot_owner,
    zonal_shift,
    zonal_taps,
    meridional_taps,
    level_mixing,
):
    members, levels, band_rows, width = control.shape
    mem_count, lat_count = lax.axis_size("mem"), lax.axis_size("lat")
    mem = lax.axis_index("mem")
    direct = z_count > 0
    field_shape = (members, levels, band_rows, width)
    half_shape = (members, levels, 8, width)
    piece = shape(levels, band_rows, width)
    core_pairs = [(i, i ^ 1) for i in range(lat_count)]
    x_pairs = [(i, i + 1) for i in range(1, lat_count - 1, 2)]
    x_pairs += [(j, i) for i, j in x_pairs]
    swap_core = lambda v: lax.ppermute(v, "lat", core_pairs)
    swap_x = lambda v: lax.ppermute(v, "lat", x_pairs)
    tap_room = [pltpu.VMEM((BAND, 8, LANES), F32)]
    ins = {
        "shift": zonal_shift, "taps": zonal_taps, "control": control,
        "meridional": meridional_taps, "ens": perturbations,
        "mixing": jnp.transpose(level_mixing, (1, 2, 0)),
    }
    results = {
        "near_x": shape(*half_shape), "control_v": shape(*field_shape),
        "taps_v": shape(*zonal_taps.shape), "meridional_v": shape(*meridional_taps.shape),
        "shift_x": shape(8, LANES, dtype=jnp.int32),
        "shift_core": shape(8, LANES, dtype=jnp.int32),
        "ens_v": shape(*perturbations.shape, dtype=BF16),
        "mixing_v": shape(levels, levels, band_rows),
    }
    if direct:
        ins["obs"] = obs_weight
        results["weight_sent"] = results["obs_v"] = piece
    names = (*ins, *results, "taps_x", "shift_s", "sems")
    made = call(
        functools.partial(front_body, names), tuple(results.values()), "front", 1 << 19,
        *(pltpu.with_memory_space_constraint(v, pltpu.HBM) for v in ins.values()),
        specs=(HBM,) * len(ins),
        scratch=[
            *tap_room, pltpu.SMEM(zonal_shift.shape, jnp.int32), pltpu.SemaphoreType.DMA((9,)),
        ],
    )
    made = dict(zip(results, made))
    near_x, control_v, ens = made["near_x"], made["control_v"], made["ens_v"]
    far_x = swap_x(near_x)
    if direct:
        y_pairs = [(i, i ^ 1) for i in range(mem_count)]
        swap_y = lambda v: lax.ppermute(v, "mem", y_pairs)
        turn_z = lambda v, s: lax.ppermute(
            v, "mem", [(i, i ^ 2 * s) for i in range(mem_count)]
        )
        from_y = swap_y(made["weight_sent"])
    near_core = call(
        core_body, shape(*half_shape), "core", 1 << 19, made["shift_core"], made["taps_v"],
        control_v, specs=(VMEM,) * 3, scratch=tap_room,
    )
    far_core = swap_core(near_core)
    matrix, transposed = call(
        functools.partial(build_matrix, lat_count),
        (shape(levels * band_rows, 32 * levels), shape(32 * levels, levels * band_rows)),
        "matrix", 1 << 16, made["meridional_v"], made["mixing_v"], specs=(VMEM, VMEM), after=(near_core, far_x),
    )
    parts = (near_core, near_x, far_core, far_x)

    if direct:
        localized, first = call(
            functools.partial(first_body, 2), (shape(*field_shape), piece),
            "first", 1 << 20, slot_owner, matrix, *parts, ens,
            specs=(HBM,) + (VMEM,) * 6, after=(from_y,),
            scratch=[pltpu.SMEM((SLOTS,), jnp.int32), pltpu.SemaphoreType.DMA],
        )
        got_two = swap_y(first)
        mine, side, middle = call(
            weight_pick, (piece,) * 3, "weight_pick", 1 << 18, slot_owner, made["obs_v"],
            from_y, specs=(SMEM,) + (VMEM,) * 2, after=(localized,),
        )
        from_side = turn_z(side, 1)
        pairs = [(i, i ^ 6) for i in range(2, mem_count - 2)]
        from_middle = lax.ppermute(middle, "mem", pairs)
        pair, single = call(
            send_body, (shape(2, levels, band_rows, width), piece), "send", 1 << 20,
            slot_owner, ens, localized, specs=(SMEM, VMEM, VMEM),
        )
        two = call(
            functools.partial(meet_body, 2), piece, "meet2", 1 << 19,
            slot_owner, ens, localized, got_two, specs=(SMEM,) + (VMEM,) * 3,
        )
        arrived = {2: turn_z(two, 2)}
        pair, two, from_side, from_middle = lax.optimization_barrier(
            (pair, two, from_side, from_middle)
        )
        got_pair = swap_y(pair)
        one, three = call(
            meet_pair_body, (piece,) * 2, "meet13", 1 << 19,
            slot_owner, ens, localized, got_pair, specs=(SMEM,) + (VMEM,) * 3,
            after=(two,),
        )
        arrived[1], arrived[3] = turn_z(one, 1), turn_z(three, 3)
        single, _ = lax.optimization_barrier((single, got_pair))
        got_own = swap_y(single)
        grad = call(
            last_body, piece, "last", 1 << 19, slot_owner, ens, localized, got_own,
            arrived[1], arrived[2], arrived[3], mine, from_side, from_middle,
            specs=(SMEM,) + (VMEM,) * 9,
        )
        own = {0: grad, 1: turn_z(grad, 1), 3: turn_z(grad, 3)}
        other = {0: swap_y(grad)}
        later, own[1], own[3], other[0] = lax.optimization_barrier((grad, own[1], own[3], other[0]))
        own[2] = turn_z(later, 2)
        other.update({s: swap_y(own[s]) for s in (1, 3, 2)})
        weighted = None
        groups = (((0, 0),), ((0, 1), (1, 0), (3, 0)), ((1, 1), (3, 1), (2, 0)), ((2, 1),))
        for group in groups:
            final = group == groups[-1]
            grads = [other[s] if o else own[s] for s, o in group]
            pieces = tuple(group)
            before = () if weighted is None else (weighted,)
            extra = (transposed,) if final else ()
            result = call(
                functools.partial(spread_body, pieces, weighted is None, final),
                (shape(*half_shape),) * 4 + (shape(*field_shape),) if final else shape(*field_shape),
                "spread%d" % group[0][0], 1 << 19,
                slot_owner, ens, *grads, *before, *extra,
                specs=(SMEM,) + (VMEM,) * (1 + len(grads) + len(before) + len(extra)),
            )
            weighted = result
        own_core, own_x, to_core, to_x = result[:4]
    else:
        localized = call(
            localize_body, shape(*field_shape), "localize", 1 << 20, matrix, *parts,
            specs=(VMEM,) * 5,
        )
        partial = call(
            all_increments, shape(SLOTS, ens.shape[1], levels, band_rows, width),
            "increments", 1 << 20, ens, localized, specs=(VMEM,) * 2,
        )
        weights = jnp.stack(
            [
                lax.psum(jnp.where(mem == slot_owner[t], obs_weight[0], 0.0), "mem")
                for t in range(SLOTS)
            ]
        )
        share = lax.psum_scatter(
            partial.reshape(-1, width), "mem", scatter_dimension=0, tiled=True
        )
        share_rows = share.shape[0]
        weight_rows = lax.dynamic_slice_in_dim(
            weights.reshape(-1, width), mem * share_rows, share_rows, 0
        )
        gathered = lax.all_gather(weight_rows * share, "mem", axis=0, tiled=True)
        own_core, own_x, to_core, to_x, _ = call(
            all_weighted, (shape(*half_shape),) * 4 + (shape(*field_shape),), "weighted",
            1 << 20, ens, gathered.reshape(partial.shape), transposed,
            specs=(VMEM,) * 3,
        )
    got_x, got_core = swap_x(to_x), swap_core(to_core)
    half = call(
        functools.partial(zonal_adjoint, 0), shape(*half_shape), "adjoint0", 1 << 19,
        made["shift_core"], made["taps_v"], control_v, own_core, got_core,
        specs=(VMEM,) * 5, scratch=tap_room,
    )
    return call(
        functools.partial(zonal_adjoint, 1), shape(*field_shape), "adjoint1", 1 << 19,
        made["shift_x"], made["taps_v"], control_v, own_x, got_x, half,
        specs=(VMEM,) * 6, scratch=tap_room,
    )


def solution(mesh):
    z_count = SLOTS if mesh.shape["mem"] == 2 * SLOTS else 0
    in_specs = (
        P("mem", None, "lat", None),
        P(None, None, "mem", None, "lat", None),
        P("mem", None, None, "lat", None),
        P(),
        P("lat"),
        P("lat", None),
        P("lat", None),
        P("lat", None, None),
    )
    out_specs = P("mem", None, "lat", None)
    return jax.shard_map(
        functools.partial(per_device, z_count),
        mesh=mesh, in_specs=in_specs, out_specs=out_specs, check_vma=False,
    )
```

```python
import functools

import jax
import jax.numpy as jnp
from jax import lax
from jax.experimental import pallas as pl
from jax.experimental.pallas import tpu as pltpu
from jax.sharding import PartitionSpec as P

SLOTS = 4
BAND = 17
HALF = BAND // 2
LANES = 128
F32 = jnp.float32
BF16 = jnp.bfloat16

VMEM = pl.BlockSpec(memory_space=pltpu.VMEM)
SMEM = pl.BlockSpec(memory_space=pltpu.SMEM)
ANY = pl.BlockSpec(memory_space=pl.ANY)
HBM = pl.BlockSpec(memory_space=pltpu.HBM)


def call(body, outs, name, cost, *operands, specs, scratch=(), after=()):
    count, extra = len(operands), len(after)

    def kernel(*refs):
        body(*refs[:count], *refs[count + extra :])

    return pl.pallas_call(
        kernel,
        out_shape=outs,
        in_specs=list(specs) + [ANY] * extra,
        out_specs=jax.tree.map(lambda _: VMEM, outs),
        scratch_shapes=list(scratch),
        compiler_params=pltpu.CompilerParams(vmem_limit_bytes=16 << 20),
        cost_estimate=pl.CostEstimate(flops=cost, bytes_accessed=cost, transcendentals=0),
        name=name,
    )(*operands, *after)


def parity():
    return lax.axis_index("lat") & 1


def own_y():
    return lax.axis_index("mem") & 1


def own_z():
    return lax.axis_index("mem") >> 1


def entry_at(owners, step, value):
    place = own_z() ^ step
    found = jnp.int32(0)
    for t in range(SLOTS):
        rank = jnp.int32(0)
        for u in range(SLOTS):
            if u != t:
                rank += jnp.where(owners[u] < owners[t], 1, 0)
        found = jnp.where(rank == place, value(t), found)
    return found


def slot_at(owners, step):
    return entry_at(owners, step, lambda t: jnp.int32(t))


def owner_at(owners, step):
    return entry_at(owners, step, lambda t: owners[t])


def shape(*dims, dtype=F32):
    return jax.ShapeDtypeStruct(dims, dtype)


def shifted(columns, amount):
    lane = lax.broadcasted_iota(jnp.int32, columns[0].shape, 1)
    turned = [pltpu.roll(c, amount, 1) for c in columns]
    return [
        jnp.where(lane < amount, turned[i - 1], turned[i]) for i in range(len(columns))
    ]


def circle_filter(columns, amount, tap):
    count = len(columns)
    lane = lax.broadcasted_iota(jnp.int32, columns[0].shape, 1)
    fine = amount & (LANES - 1)
    source = (lane - fine) & (LANES - 1)
    turned = [
        jnp.take_along_axis(c, source, axis=1, mode="promise_in_bounds") for c in columns
    ]
    wraps = lane < fine
    columns = [jnp.where(wraps, turned[i - 1], turned[i]) for i in range(count)]
    step = 1
    while step < count:
        moved = (amount & (step * LANES)) != 0
        columns = [jnp.where(moved, columns[i - step], columns[i]) for i in range(count)]
        step *= 2
    near = [columns]
    for offset in range(1, 4):
        near.append(shifted(columns, offset))
    total = [tap(BAND - 1) * c for c in columns]
    for group in range((BAND - 1) // 4 - 1, -1, -1):
        total = shifted(total, 4)
        for offset in range(4):
            factor = tap(4 * group + offset)
            total = [t + factor * c for t, c in zip(total, near[offset])]
    return total


def row_shifts(shifts, first):
    row = lax.broadcasted_iota(jnp.int32, (8, LANES), 0)
    amounts = jnp.zeros((8, LANES), jnp.int32)
    for r in range(8):
        amounts = jnp.where(row == r, shifts[first + r], amounts)
    return amounts


def spread_taps(taps, first, spread):
    block = taps[pl.ds(first, 8), :]
    for k in range(BAND):
        spread[k] = jnp.broadcast_to(block[:, k : k + 1], (8, LANES))


def tiles(width):
    return [slice(i * LANES, (i + 1) * LANES) for i in range(width // LANES)]


def half_start(which):
    odd = parity()
    return pl.multiple_of((1 - odd if which == 0 else odd) * 8, 8)


def zonal_forward(first, shifts, taps, control, out):
    members, levels, _, width = control.shape
    amount = (width - HALF - shifts[...]) & (width - 1)

    def step(m, carry):
        for l in range(levels):
            columns = [control[m, l, pl.ds(first, 8), cut] for cut in tiles(width)]
            result = circle_filter(columns, amount, lambda k: taps[BAND - 1 - k])
            for cut, value in zip(tiles(width), result):
                out[m, l, :, cut] = value
        return carry

    lax.fori_loop(0, members, step, 0)


def front_body(names, *refs):
    r = dict(zip(names, refs))
    sems = r["sems"]
    first_x, first_core = half_start(1), half_start(0)
    rows_x, rows_core = pl.ds(first_x, 8), pl.ds(first_core, 8)
    moves = [
        (r["shift"], r["shift_s"]),
        (r["taps"], r["taps_v"]),
        (r["control"].at[:, :, rows_x], r["control_v"].at[:, :, rows_x]),
    ]
    moves.append((r["control"].at[:, :, rows_core], r["control_v"].at[:, :, rows_core]))
    moves.append((r["meridional"], r["meridional_v"]))
    moves.append((r["mixing"], r["mixing_v"]))
    if "obs" in r:
        moves.append((r["obs"].at[0], r["obs_v"]))
    moves.append((r["ens"], r["ens_v"]))
    copies = [pltpu.make_async_copy(a, b, sems.at[i]) for i, (a, b) in enumerate(moves)]
    for copy in copies:
        copy.start()
    for copy in copies[:3]:
        copy.wait()
    r["shift_x"][...] = row_shifts(r["shift_s"], first_x)
    r["shift_core"][...] = row_shifts(r["shift_s"], first_core)
    spread_taps(r["taps_v"], first_x, r["taps_x"])
    zonal_forward(first_x, r["shift_x"], r["taps_x"], r["control_v"], r["near_x"])
    for copy in copies[3:]:
        copy.wait()


def core_body(shifts, taps_v, control, out, taps):
    first = half_start(0)
    spread_taps(taps_v, first, taps)
    zonal_forward(first, shifts, taps, control, out)


def zonal_adjoint(which, shifts, taps_v, control, own, got, *refs):
    other, out, taps = (None, *refs) if which == 0 else refs
    members, levels, _, width = control.shape
    first = half_start(which)
    amount = (shifts[...] - HALF) & (width - 1)
    spread_taps(taps_v, first, taps)

    def step(m, carry):
        for l in range(levels):
            columns = [own[m, l, :, cut] + got[m, l, :, cut] for cut in tiles(width)]
            result = circle_filter(columns, amount, lambda k: taps[k])
            for cut, value in zip(tiles(width), result):
                total = control[m, l, pl.ds(first, 8), cut] + value
                if which == 0:
                    out[m, l, :, cut] = total
                else:
                    out[m, l, pl.ds(first, 8), cut] = total
                    out[m, l, pl.ds(8 - first, 8), cut] = other[m, l, :, cut]
        return carry

    lax.fori_loop(0, members, step, 0)


def build_matrix(lat_count, taps_ref, mixing_ref, matrix, transposed):
    band_rows, levels = taps_ref.shape[0], mixing_ref.shape[1]
    rows, columns = matrix.shape
    odd, lat = parity(), lax.axis_index("lat")
    alone = (lat == 0) | (lat == lat_count - 1)
    column = lax.broadcasted_iota(jnp.int32, (band_rows, columns), 1)
    row = lax.broadcasted_iota(jnp.int32, (band_rows, columns), 0)
    block, level, inner = column // (8 * levels), (column // 8) % levels, column % 8
    even_start = jnp.where(block == 0, 16, jnp.where(block == 1, 8, jnp.where(block == 2, 24, 0)))
    odd_start = jnp.where(block == 0, 8, jnp.where(block == 1, 16, jnp.where(block == 2, 0, 24)))
    reach = jnp.where(odd == 1, odd_start, even_start) + inner - row
    band = jnp.zeros((band_rows, columns), F32)
    for k in range(BAND):
        band = jnp.where(reach == k, taps_ref[:, k : k + 1], band)
    band = jnp.where((block == 3) & alone, 0.0, band)
    same = lax.broadcasted_iota(jnp.int32, (band_rows, band_rows), 0) == (
        lax.broadcasted_iota(jnp.int32, (band_rows, band_rows), 1)
    )
    for a in range(levels):
        mixing = mixing_ref[a]
        factor = jnp.zeros((band_rows, columns), F32)
        for b in range(levels):
            by_lane = jnp.broadcast_to(mixing[b : b + 1, :], (band_rows, band_rows))
            by_row = jnp.sum(jnp.where(same, by_lane, 0.0), axis=1, keepdims=True)
            factor = jnp.where(level == b, by_row, factor)
        matrix[a * band_rows : (a + 1) * band_rows, :] = factor * band
    transposed[...] = matrix[...].T


def halves(value):
    high = value.astype(BF16)
    return high, (value - high.astype(F32)).astype(BF16)


def product(left, right):
    (lh, ll), (rh, rl) = left, right
    dot = functools.partial(jnp.dot, preferred_element_type=F32)
    return dot(lh, rh) + (dot(lh, rl) + dot(ll, rh))


CHUNK = 256


def localize(matrix, parts, out):
    members, levels, band_rows, width = out.shape
    left = halves(matrix[...])
    for m in range(members):
        for c in range(0, width, CHUNK):
            cut = slice(c, c + CHUNK)
            stack = jnp.concatenate(
                [p[m, l, :, cut] for p in parts for l in range(levels)], axis=0
            )
            result = product(left, halves(stack))
            for l in range(levels):
                out[m, l, :, cut] = result[l * band_rows : (l + 1) * band_rows]


def delocalize(matrix, weighted, parts):
    members, levels, band_rows, width = weighted.shape
    left = halves(matrix[...])
    for m in range(members):
        for c in range(0, width, CHUNK):
            cut = slice(c, c + CHUNK)
            stack = jnp.concatenate([weighted[m, l, :, cut] for l in range(levels)], axis=0)
            result = product(left, halves(stack))
            for p, part in enumerate(parts):
                for l in range(levels):
                    start = (p * levels + l) * 8
                    part[m, l, :, cut] = result[start : start + 8]


def increment(ens, localized, slot, field, l):
    total = None
    for m in range(localized.shape[0]):
        term = ens[slot, field, m, l].astype(F32) * localized[m, l]
        total = term if total is None else total + term
    return total


def weight_pick(owners, here, side, middle, mine, across):
    place = owner_at(owners, 0) >> 1
    for found, weights in (
        (place == own_z(), here),
        (place == own_z() ^ 1, side),
        (place == own_z() ^ 3, middle),
    ):

        @pl.when(found)
        def _(weights=weights):
            mine[...] = weights[own_y()]
            across[...] = weights[1 - own_y()]


def first_body(step, owners_hbm, matrix, a, b, c, d, ens, localized, send, owners, sem):
    copy = pltpu.make_async_copy(owners_hbm, owners, sem)
    copy.start()
    localize(matrix, (a, b, c, d), localized)
    copy.wait()
    slot = slot_at(owners, step)
    for l in range(localized.shape[1]):
        send[l] = increment(ens, localized, slot, 1 - own_y(), l)


def send_body(owners, ens, localized, pair, single):
    for step, send in ((1, pair.at[0]), (3, pair.at[1]), (0, single)):
        slot = slot_at(owners, step)
        for l in range(localized.shape[1]):
            send[l] = increment(ens, localized, slot, 1 - own_y(), l)


def meet_body(step, owners, ens, localized, got, out):
    slot = slot_at(owners, step)
    for l in range(localized.shape[1]):
        out[l] = increment(ens, localized, slot, own_y(), l) + got[l]


def meet_pair_body(owners, ens, localized, got, *outs):
    for i, (step, out) in enumerate(zip((1, 3), outs)):
        meet_body(step, owners, ens, localized, got.at[i], out)


def last_body(owners, ens, localized, got_y, got_1, got_2, got_3, mine, from_y, out):
    slot = slot_at(owners, 0)
    held = (owner_at(owners, 0) & 1) == own_y()
    for here, weight in ((held, mine), (jnp.logical_not(held), from_y)):

        @pl.when(here)
        def _(weight=weight):
            for l in range(localized.shape[1]):
                out[l] = weight[l] * (
                    increment(ens, localized, slot, own_y(), l)
                    + got_y[l]
                    + (got_1[l] + got_2[l] + got_3[l])
                )


def spread_body(pieces, first, final, owners, ens, *refs):
    refs = list(refs)
    grads = [refs.pop(0) for _ in pieces]
    before = None if first else refs.pop(0)
    matrix = refs.pop(0) if final else None
    out = refs[-1] if final else refs[0]
    members, levels = out.shape[:2]
    places = [
        (slot_at(owners, step), 1 - own_y() if other else own_y()) for step, other in pieces
    ]
    for m in range(members):
        for l in range(levels):
            total = None if before is None else before[m, l]
            for (slot, field), grad in zip(places, grads):
                term = ens[slot, field, m, l].astype(F32) * grad[l]
                total = term if total is None else total + term
            out[m, l] = total
    if final:
        delocalize(matrix, out, refs[:4])


def all_increments(ens, localized, out):
    for slot in range(out.shape[0]):
        for field in range(out.shape[1]):
            for l in range(out.shape[2]):
                out[slot, field, l] = increment(ens, localized, slot, field, l)


def localize_body(matrix, a, b, c, d, localized):
    localize(matrix, (a, b, c, d), localized)


def all_weighted(ens, grad, matrix, a, b, c, d, out):
    members, levels = out.shape[:2]
    for m in range(members):
        for l in range(levels):
            total = None
            for slot in range(ens.shape[0]):
                for field in range(ens.shape[1]):
                    term = ens[slot, field, m, l].astype(F32) * grad[slot, field, l]
                    total = term if total is None else total + term
            out[m, l] = total
    delocalize(matrix, out, (a, b, c, d))


def per_device(
    z_count,
    control,
    perturbations,
    obs_weight,
    slot_owner,
    zonal_shift,
    zonal_taps,
    meridional_taps,
    level_mixing,
):
    members, levels, band_rows, width = control.shape
    mem_count, lat_count = lax.axis_size("mem"), lax.axis_size("lat")
    mem = lax.axis_index("mem")
    direct = z_count > 0
    field_shape = (members, levels, band_rows, width)
    half_shape = (members, levels, 8, width)
    piece = shape(levels, band_rows, width)
    core_pairs = [(i, i ^ 1) for i in range(lat_count)]
    x_pairs = [(i, i + 1) for i in range(1, lat_count - 1, 2)]
    x_pairs += [(j, i) for i, j in x_pairs]
    swap_core = lambda v: lax.ppermute(v, "lat", core_pairs)
    swap_x = lambda v: lax.ppermute(v, "lat", x_pairs)
    tap_room = [pltpu.VMEM((BAND, 8, LANES), F32)]
    ins = {
        "shift": zonal_shift, "taps": zonal_taps, "control": control,
        "meridional": meridional_taps, "ens": perturbations,
        "mixing": jnp.transpose(level_mixing, (1, 2, 0)),
    }
    results = {
        "near_x": shape(*half_shape), "control_v": shape(*field_shape),
        "taps_v": shape(*zonal_taps.shape), "meridional_v": shape(*meridional_taps.shape),
        "shift_x": shape(8, LANES, dtype=jnp.int32),
        "shift_core": shape(8, LANES, dtype=jnp.int32),
        "ens_v": shape(*perturbations.shape, dtype=BF16),
        "mixing_v": shape(levels, levels, band_rows),
    }
    if direct:
        ins["obs"] = obs_weight
        results["obs_v"] = shape(*obs_weight.shape[1:])
    names = (*ins, *results, "taps_x", "shift_s", "sems")
    made = call(
        functools.partial(front_body, names), tuple(results.values()), "front", 1 << 19,
        *(pltpu.with_memory_space_constraint(v, pltpu.HBM) for v in ins.values()),
        specs=(HBM,) * len(ins),
        scratch=[
            *tap_room, pltpu.SMEM(zonal_shift.shape, jnp.int32), pltpu.SemaphoreType.DMA((8,)),
        ],
    )
    made = dict(zip(results, made))
    near_x, control_v, ens = made["near_x"], made["control_v"], made["ens_v"]
    far_x = swap_x(near_x)
    if direct:
        y_pairs = [(i, i ^ 1) for i in range(mem_count)]
        swap_y = lambda v: lax.ppermute(v, "mem", y_pairs)
        turn_z = lambda v, s: lax.ppermute(
            v, "mem", [(i, i ^ 2 * s) for i in range(mem_count)]
        )
        middle = [(i, i ^ 6) for i in range(2, mem_count - 2)]
        from_side = turn_z(made["obs_v"], 1)
        from_middle = lax.ppermute(made["obs_v"], "mem", middle)
    near_core = call(
        core_body, shape(*half_shape), "core", 1 << 19, made["shift_core"], made["taps_v"],
        control_v, specs=(VMEM,) * 3, scratch=tap_room,
    )
    far_core = swap_core(near_core)
    matrix, transposed = call(
        functools.partial(build_matrix, lat_count),
        (shape(levels * band_rows, 32 * levels), shape(32 * levels, levels * band_rows)),
        "matrix", 1 << 16, made["meridional_v"], made["mixing_v"], specs=(VMEM, VMEM), after=(near_core, far_x),
    )
    parts = (near_core, near_x, far_core, far_x)

    if direct:
        localized, first = call(
            functools.partial(first_body, 2), (shape(*field_shape), piece),
            "first", 1 << 20, slot_owner, matrix, *parts, ens,
            specs=(HBM,) + (VMEM,) * 6,
            scratch=[pltpu.SMEM((SLOTS,), jnp.int32), pltpu.SemaphoreType.DMA],
        )
        got_two = swap_y(first)
        pair, single = call(
            send_body, (shape(2, levels, band_rows, width), piece), "send", 1 << 20,
            slot_owner, ens, localized, specs=(SMEM, VMEM, VMEM), after=(from_side, from_middle),
        )
        pair, got_two = lax.optimization_barrier((pair, got_two))
        got_pair = swap_y(pair)
        two = call(
            functools.partial(meet_body, 2), piece, "meet2", 1 << 19,
            slot_owner, ens, localized, got_two, specs=(SMEM,) + (VMEM,) * 3,
        )
        arrived = {2: turn_z(two, 2)}
        mine, across = call(
            weight_pick, (piece,) * 2, "weight_pick", 1 << 18, slot_owner, made["obs_v"],
            from_side, from_middle, specs=(SMEM,) + (VMEM,) * 3, after=(two,),
        )
        one, three = call(
            meet_pair_body, (piece,) * 2, "meet13", 1 << 19,
            slot_owner, ens, localized, got_pair, specs=(SMEM,) + (VMEM,) * 3,
            after=(two, across),
        )
        arrived[1], arrived[3] = turn_z(one, 1), turn_z(three, 3)
        single, across, _ = lax.optimization_barrier((single, across, got_pair))
        got_own, from_y = swap_y(single), swap_y(across)
        grad = call(
            last_body, piece, "last", 1 << 19, slot_owner, ens, localized, got_own,
            arrived[1], arrived[2], arrived[3], mine, from_y,
            specs=(SMEM,) + (VMEM,) * 8,
        )
        own = {0: grad, 3: turn_z(grad, 3), 1: turn_z(grad, 1)}
        weighted = call(
            functools.partial(spread_body, ((0, 0),), True, False), shape(*field_shape),
            "spread", 1 << 19, slot_owner, ens, grad, specs=(SMEM,) + (VMEM,) * 2,
        )
        other, weighted = lax.optimization_barrier((grad, weighted))
        other = {0: swap_y(other)}
        later, own[3], other[0] = lax.optimization_barrier((grad, own[3], other[0]))
        own[2] = turn_z(later, 2)
        other.update({s: swap_y(own[s]) for s in (1, 3, 2)})
        groups = (((0, 1), (1, 0), (3, 0)), ((1, 1), (3, 1), (2, 0)), ((2, 1),))
        for group in groups:
            final = group == groups[-1]
            grads = [other[s] if o else own[s] for s, o in group]
            pieces = tuple(group)
            extra = (transposed,) if final else ()
            result = call(
                functools.partial(spread_body, pieces, False, final),
                (shape(*half_shape),) * 4 + (shape(*field_shape),) if final else shape(*field_shape),
                "spread%d" % group[0][0], 1 << 19,
                slot_owner, ens, *grads, weighted, *extra,
                specs=(SMEM,) + (VMEM,) * (2 + len(grads) + len(extra)),
            )
            weighted = result
        own_core, own_x, to_core, to_x = result[:4]
    else:
        localized = call(
            localize_body, shape(*field_shape), "localize", 1 << 20, matrix, *parts,
            specs=(VMEM,) * 5,
        )
        partial = call(
            all_increments, shape(SLOTS, ens.shape[1], levels, band_rows, width),
            "increments", 1 << 20, ens, localized, specs=(VMEM,) * 2,
        )
        weights = jnp.stack(
            [
                lax.psum(jnp.where(mem == slot_owner[t], obs_weight[0], 0.0), "mem")
                for t in range(SLOTS)
            ]
        )
        share = lax.psum_scatter(
            partial.reshape(-1, width), "mem", scatter_dimension=0, tiled=True
        )
        share_rows = share.shape[0]
        weight_rows = lax.dynamic_slice_in_dim(
            weights.reshape(-1, width), mem * share_rows, share_rows, 0
        )
        gathered = lax.all_gather(weight_rows * share, "mem", axis=0, tiled=True)
        own_core, own_x, to_core, to_x, _ = call(
            all_weighted, (shape(*half_shape),) * 4 + (shape(*field_shape),), "weighted",
            1 << 20, ens, gathered.reshape(partial.shape), transposed,
            specs=(VMEM,) * 3,
        )
    got_x, got_core = swap_x(to_x), swap_core(to_core)
    half = call(
        functools.partial(zonal_adjoint, 0), shape(*half_shape), "adjoint0", 1 << 19,
        made["shift_core"], made["taps_v"], control_v, own_core, got_core,
        specs=(VMEM,) * 5, scratch=tap_room,
    )
    return call(
        functools.partial(zonal_adjoint, 1), shape(*field_shape), "adjoint1", 1 << 19,
        made["shift_x"], made["taps_v"], control_v, own_x, got_x, half,
        specs=(VMEM,) * 6, scratch=tap_room,
    )


def solution(mesh):
    z_count = SLOTS if mesh.shape["mem"] == 2 * SLOTS else 0
    in_specs = (
        P("mem", None, "lat", None),
        P(None, None, "mem", None, "lat", None),
        P("mem", None, None, "lat", None),
        P(),
        P("lat"),
        P("lat", None),
        P("lat", None),
        P("lat", None, None),
    )
    out_specs = P("mem", None, "lat", None)
    return jax.shard_map(
        functools.partial(per_device, z_count),
        mesh=mesh, in_specs=in_specs, out_specs=out_specs, check_vma=False,
    )
```

```python
import functools

import jax
import jax.numpy as jnp
from jax import lax
from jax.experimental import pallas as pl
from jax.experimental.pallas import tpu as pltpu
from jax.sharding import PartitionSpec as P

SLOTS = 4
BAND = 17
HALF = BAND // 2
LANES = 128
F32 = jnp.float32
BF16 = jnp.bfloat16

VMEM = pl.BlockSpec(memory_space=pltpu.VMEM)
SMEM = pl.BlockSpec(memory_space=pltpu.SMEM)
ANY = pl.BlockSpec(memory_space=pl.ANY)
HBM = pl.BlockSpec(memory_space=pltpu.HBM)


def call(body, outs, name, cost, *operands, specs, scratch=(), after=()):
    count, extra = len(operands), len(after)

    def kernel(*refs):
        body(*refs[:count], *refs[count + extra :])

    return pl.pallas_call(
        kernel,
        out_shape=outs,
        in_specs=list(specs) + [ANY] * extra,
        out_specs=jax.tree.map(lambda _: VMEM, outs),
        scratch_shapes=list(scratch),
        compiler_params=pltpu.CompilerParams(vmem_limit_bytes=16 << 20),
        cost_estimate=pl.CostEstimate(flops=cost, bytes_accessed=cost, transcendentals=0),
        name=name,
    )(*operands, *after)


def parity():
    return lax.axis_index("lat") & 1


def own_y():
    return lax.axis_index("mem") & 1


def own_z():
    return lax.axis_index("mem") >> 1


def entry_at(owners, step, value):
    place = own_z() ^ step
    found = jnp.int32(0)
    for t in range(SLOTS):
        rank = jnp.int32(0)
        for u in range(SLOTS):
            if u != t:
                rank += jnp.where(owners[u] < owners[t], 1, 0)
        found = jnp.where(rank == place, value(t), found)
    return found


def slot_at(owners, step):
    return entry_at(owners, step, lambda t: jnp.int32(t))


def owner_at(owners, step):
    return entry_at(owners, step, lambda t: owners[t])


def shape(*dims, dtype=F32):
    return jax.ShapeDtypeStruct(dims, dtype)


def shifted(columns, amount):
    lane = lax.broadcasted_iota(jnp.int32, columns[0].shape, 1)
    turned = [pltpu.roll(c, amount, 1) for c in columns]
    return [
        jnp.where(lane < amount, turned[i - 1], turned[i]) for i in range(len(columns))
    ]


def circle_filter(columns, amount, tap):
    count = len(columns)
    lane = lax.broadcasted_iota(jnp.int32, columns[0].shape, 1)
    fine = amount & (LANES - 1)
    source = (lane - fine) & (LANES - 1)
    turned = [
        jnp.take_along_axis(c, source, axis=1, mode="promise_in_bounds") for c in columns
    ]
    wraps = lane < fine
    columns = [jnp.where(wraps, turned[i - 1], turned[i]) for i in range(count)]
    step = 1
    while step < count:
        moved = (amount & (step * LANES)) != 0
        columns = [jnp.where(moved, columns[i - step], columns[i]) for i in range(count)]
        step *= 2
    near = [columns]
    for offset in range(1, 4):
        near.append(shifted(columns, offset))
    total = [tap(BAND - 1) * c for c in columns]
    for group in range((BAND - 1) // 4 - 1, -1, -1):
        total = shifted(total, 4)
        for offset in range(4):
            factor = tap(4 * group + offset)
            total = [t + factor * c for t, c in zip(total, near[offset])]
    return total


def row_shifts(shifts, first):
    row = lax.broadcasted_iota(jnp.int32, (8, LANES), 0)
    amounts = jnp.zeros((8, LANES), jnp.int32)
    for r in range(8):
        amounts = jnp.where(row == r, shifts[first + r], amounts)
    return amounts


def spread_taps(taps, first, spread):
    block = taps[pl.ds(first, 8), :]
    for k in range(BAND):
        spread[k] = jnp.broadcast_to(block[:, k : k + 1], (8, LANES))


def tiles(width):
    return [slice(i * LANES, (i + 1) * LANES) for i in range(width // LANES)]


def half_start(which):
    odd = parity()
    return pl.multiple_of((1 - odd if which == 0 else odd) * 8, 8)


def zonal_forward(first, shifts, taps, control, out):
    members, levels, _, width = control.shape
    amount = (width - HALF - shifts[...]) & (width - 1)

    def step(m, carry):
        for l in range(levels):
            columns = [control[m, l, pl.ds(first, 8), cut] for cut in tiles(width)]
            result = circle_filter(columns, amount, lambda k: taps[BAND - 1 - k])
            for cut, value in zip(tiles(width), result):
                out[m, l, :, cut] = value
        return carry

    lax.fori_loop(0, members, step, 0)


def front_body(names, *refs):
    r = dict(zip(names, refs))
    sems = r["sems"]
    first_x, first_core = half_start(1), half_start(0)
    rows_x, rows_core = pl.ds(first_x, 8), pl.ds(first_core, 8)
    moves = [
        (r["shift"], r["shift_s"]),
        (r["taps"], r["taps_v"]),
        (r["control"].at[:, :, rows_x], r["control_v"].at[:, :, rows_x]),
    ]
    moves.append((r["control"].at[:, :, rows_core], r["control_v"].at[:, :, rows_core]))
    moves.append((r["meridional"], r["meridional_v"]))
    moves.append((r["mixing"], r["mixing_v"]))
    if "obs" in r:
        moves.append((r["obs"].at[0], r["obs_v"]))
    moves.append((r["ens"], r["ens_v"]))
    copies = [pltpu.make_async_copy(a, b, sems.at[i]) for i, (a, b) in enumerate(moves)]
    for copy in copies:
        copy.start()
    for copy in copies[:3]:
        copy.wait()
    r["shift_x"][...] = row_shifts(r["shift_s"], first_x)
    r["shift_core"][...] = row_shifts(r["shift_s"], first_core)
    spread_taps(r["taps_v"], first_x, r["taps_x"])
    zonal_forward(first_x, r["shift_x"], r["taps_x"], r["control_v"], r["near_x"])
    for copy in copies[3:]:
        copy.wait()


def core_body(shifts, taps_v, control, out, taps):
    first = half_start(0)
    spread_taps(taps_v, first, taps)
    zonal_forward(first, shifts, taps, control, out)


def zonal_adjoint(lat_count, which, shifts, taps_v, control, own, got, *refs):
    other, out, taps = (None, *refs) if which == 0 else refs
    members, levels, _, width = control.shape
    first = half_start(which)
    amount = (shifts[...] - HALF) & (width - 1)
    spread_taps(taps_v, first, taps)
    lat = lax.axis_index("lat")
    alone = (which == 1) & ((lat == 0) | (lat == lat_count - 1))

    def step(m, carry):
        for l in range(levels):
            columns = [
                own[m, l, :, cut] + jnp.where(alone, 0.0, got[m, l, :, cut])
                for cut in tiles(width)
            ]
            result = circle_filter(columns, amount, lambda k: taps[k])
            for cut, value in zip(tiles(width), result):
                total = control[m, l, pl.ds(first, 8), cut] + value
                if which == 0:
                    out[m, l, :, cut] = total
                else:
                    out[m, l, pl.ds(first, 8), cut] = total
                    out[m, l, pl.ds(8 - first, 8), cut] = other[m, l, :, cut]
        return carry

    lax.fori_loop(0, members, step, 0)


def build_matrix(lat_count, taps_ref, mixing_ref, matrix, transposed):
    band_rows, levels = taps_ref.shape[0], mixing_ref.shape[1]
    rows, columns = matrix.shape
    odd, lat = parity(), lax.axis_index("lat")
    alone = (lat == 0) | (lat == lat_count - 1)
    column = lax.broadcasted_iota(jnp.int32, (band_rows, columns), 1)
    row = lax.broadcasted_iota(jnp.int32, (band_rows, columns), 0)
    block, level, inner = column // (8 * levels), (column // 8) % levels, column % 8
    even_start = jnp.where(block == 0, 16, jnp.where(block == 1, 8, jnp.where(block == 2, 24, 0)))
    odd_start = jnp.where(block == 0, 8, jnp.where(block == 1, 16, jnp.where(block == 2, 0, 24)))
    reach = jnp.where(odd == 1, odd_start, even_start) + inner - row
    band = jnp.zeros((band_rows, columns), F32)
    for k in range(BAND):
        band = jnp.where(reach == k, taps_ref[:, k : k + 1], band)
    band = jnp.where((block == 3) & alone, 0.0, band)
    same = lax.broadcasted_iota(jnp.int32, (band_rows, band_rows), 0) == (
        lax.broadcasted_iota(jnp.int32, (band_rows, band_rows), 1)
    )
    for a in range(levels):
        mixing = mixing_ref[a]
        factor = jnp.zeros((band_rows, columns), F32)
        for b in range(levels):
            by_lane = jnp.broadcast_to(mixing[b : b + 1, :], (band_rows, band_rows))
            by_row = jnp.sum(jnp.where(same, by_lane, 0.0), axis=1, keepdims=True)
            factor = jnp.where(level == b, by_row, factor)
        matrix[a * band_rows : (a + 1) * band_rows, :] = factor * band
    transposed[...] = matrix[...].T


def halves(value):
    high = value.astype(BF16)
    return high, (value - high.astype(F32)).astype(BF16)


def product(left, right):
    (lh, ll), (rh, rl) = left, right
    dot = functools.partial(jnp.dot, preferred_element_type=F32)
    return dot(lh, rh) + (dot(lh, rl) + dot(ll, rh))


CHUNK = 256


def localize(matrix, parts, out):
    members, levels, band_rows, width = out.shape
    left = halves(matrix[...])
    for m in range(members):
        for c in range(0, width, CHUNK):
            cut = slice(c, c + CHUNK)
            stack = jnp.concatenate(
                [p[m, l, :, cut] for p in parts for l in range(levels)], axis=0
            )
            result = product(left, halves(stack))
            for l in range(levels):
                out[m, l, :, cut] = result[l * band_rows : (l + 1) * band_rows]


def delocalize(matrix, weighted, first, parts):
    members, levels, band_rows, width = weighted.shape
    rows = slice(first * levels * 8, (first + len(parts)) * levels * 8)
    left = halves(matrix[rows, :])
    for m in range(members):
        for c in range(0, width, CHUNK):
            cut = slice(c, c + CHUNK)
            stack = jnp.concatenate([weighted[m, l, :, cut] for l in range(levels)], axis=0)
            result = product(left, halves(stack))
            for p, part in enumerate(parts):
                for l in range(levels):
                    start = (p * levels + l) * 8
                    part[m, l, :, cut] = result[start : start + 8]


def blocks_body(first, matrix, weighted, *parts):
    delocalize(matrix, weighted, first, parts)


def increment(ens, localized, slot, field, l):
    total = None
    for m in range(localized.shape[0]):
        term = ens[slot, field, m, l].astype(F32) * localized[m, l]
        total = term if total is None else total + term
    return total


def weight_pick(owners, here, side, middle, mine, across):
    place = owner_at(owners, 0) >> 1
    for found, weights in (
        (place == own_z(), here),
        (place == own_z() ^ 1, side),
        (place == own_z() ^ 3, middle),
    ):

        @pl.when(found)
        def _(weights=weights):
            mine[...] = weights[own_y()]
            across[...] = weights[1 - own_y()]


def first_body(step, owners_hbm, matrix, a, b, c, d, ens, localized, send, owners, sem):
    copy = pltpu.make_async_copy(owners_hbm, owners, sem)
    copy.start()
    localize(matrix, (a, b, c, d), localized)
    copy.wait()
    slot = slot_at(owners, step)
    for l in range(localized.shape[1]):
        send[l] = increment(ens, localized, slot, 1 - own_y(), l)


def send_body(owners, ens, localized, pair, single):
    for step, send in ((1, pair.at[0]), (3, pair.at[1]), (0, single)):
        slot = slot_at(owners, step)
        for l in range(localized.shape[1]):
            send[l] = increment(ens, localized, slot, 1 - own_y(), l)


def meet_body(step, owners, ens, localized, got, out):
    slot = slot_at(owners, step)
    for l in range(localized.shape[1]):
        out[l] = increment(ens, localized, slot, own_y(), l) + got[l]


def meet_pair_body(owners, ens, localized, got, *outs):
    for i, (step, out) in enumerate(zip((1, 3), outs)):
        meet_body(step, owners, ens, localized, got.at[i], out)


def last_body(owners, ens, localized, got_y, got_1, got_2, got_3, mine, from_y, out):
    slot = slot_at(owners, 0)
    held = (owner_at(owners, 0) & 1) == own_y()
    for here, weight in ((held, mine), (jnp.logical_not(held), from_y)):

        @pl.when(here)
        def _(weight=weight):
            for l in range(localized.shape[1]):
                out[l] = weight[l] * (
                    increment(ens, localized, slot, own_y(), l)
                    + got_y[l]
                    + (got_1[l] + got_2[l] + got_3[l])
                )


def spread_body(pieces, first, final, owners, ens, *refs):
    refs = list(refs)
    grads = [refs.pop(0) for _ in pieces]
    before = None if first else refs.pop(0)
    matrix = refs.pop(0) if final else None
    out = refs[-1] if final else refs[0]
    members, levels = out.shape[:2]
    places = [
        (slot_at(owners, step), 1 - own_y() if other else own_y()) for step, other in pieces
    ]
    for m in range(members):
        for l in range(levels):
            total = None if before is None else before[m, l]
            for (slot, field), grad in zip(places, grads):
                term = ens[slot, field, m, l].astype(F32) * grad[l]
                total = term if total is None else total + term
            out[m, l] = total
    if final:
        delocalize(matrix, out, 3, refs[:1])


def all_increments(ens, localized, out):
    for slot in range(out.shape[0]):
        for field in range(out.shape[1]):
            for l in range(out.shape[2]):
                out[slot, field, l] = increment(ens, localized, slot, field, l)


def localize_body(matrix, a, b, c, d, localized):
    localize(matrix, (a, b, c, d), localized)


def all_weighted(ens, grad, matrix, a, b, c, d, out):
    members, levels = out.shape[:2]
    for m in range(members):
        for l in range(levels):
            total = None
            for slot in range(ens.shape[0]):
                for field in range(ens.shape[1]):
                    term = ens[slot, field, m, l].astype(F32) * grad[slot, field, l]
                    total = term if total is None else total + term
            out[m, l] = total
    delocalize(matrix, out, 0, (a, b, c, d))


def per_device(
    z_count,
    control,
    perturbations,
    obs_weight,
    slot_owner,
    zonal_shift,
    zonal_taps,
    meridional_taps,
    level_mixing,
):
    members, levels, band_rows, width = control.shape
    mem_count, lat_count = lax.axis_size("mem"), lax.axis_size("lat")
    mem = lax.axis_index("mem")
    direct = z_count > 0
    field_shape = (members, levels, band_rows, width)
    half_shape = (members, levels, 8, width)
    piece = shape(levels, band_rows, width)
    core_pairs = [(i, i ^ 1) for i in range(lat_count)]
    x_swaps = [
        (m * lat_count + i, (m ^ 1) * lat_count + i)
        if i in (0, lat_count - 1)
        else (m * lat_count + i, m * lat_count + ((i - 1) ^ 1) + 1)
        for m in range(mem_count)
        for i in range(lat_count)
    ]
    swap_core = lambda v: lax.ppermute(v, "lat", core_pairs)
    swap_x = lambda v: lax.ppermute(v, ("mem", "lat"), x_swaps)
    tap_room = [pltpu.VMEM((BAND, 8, LANES), F32)]
    ins = {
        "shift": zonal_shift, "taps": zonal_taps, "control": control,
        "meridional": meridional_taps, "ens": perturbations,
        "mixing": jnp.transpose(level_mixing, (1, 2, 0)),
    }
    results = {
        "near_x": shape(*half_shape), "control_v": shape(*field_shape),
        "taps_v": shape(*zonal_taps.shape), "meridional_v": shape(*meridional_taps.shape),
        "shift_x": shape(8, LANES, dtype=jnp.int32),
        "shift_core": shape(8, LANES, dtype=jnp.int32),
        "ens_v": shape(*perturbations.shape, dtype=BF16),
        "mixing_v": shape(levels, levels, band_rows),
    }
    if direct:
        ins["obs"] = obs_weight
        results["obs_v"] = shape(*obs_weight.shape[1:])
    names = (*ins, *results, "taps_x", "shift_s", "sems")
    made = call(
        functools.partial(front_body, names), tuple(results.values()), "front", 1 << 19,
        *(pltpu.with_memory_space_constraint(v, pltpu.HBM) for v in ins.values()),
        specs=(HBM,) * len(ins),
        scratch=[
            *tap_room, pltpu.SMEM(zonal_shift.shape, jnp.int32), pltpu.SemaphoreType.DMA((8,)),
        ],
    )
    made = dict(zip(results, made))
    near_x, control_v, ens = made["near_x"], made["control_v"], made["ens_v"]
    far_x = swap_x(near_x)
    if direct:
        y_pairs = [(i, i ^ 1) for i in range(mem_count)]
        swap_y = lambda v: lax.ppermute(v, "mem", y_pairs)
        turn_z = lambda v, s: lax.ppermute(
            v, "mem", [(i, i ^ 2 * s) for i in range(mem_count)]
        )
        middle = [(i, i ^ 6) for i in range(2, mem_count - 2)]
        from_side = turn_z(made["obs_v"], 1)
        from_middle = lax.ppermute(made["obs_v"], "mem", middle)
    near_core = call(
        core_body, shape(*half_shape), "core", 1 << 19, made["shift_core"], made["taps_v"],
        control_v, specs=(VMEM,) * 3, scratch=tap_room,
    )
    far_core = swap_core(near_core)
    matrix, transposed = call(
        functools.partial(build_matrix, lat_count),
        (shape(levels * band_rows, 32 * levels), shape(32 * levels, levels * band_rows)),
        "matrix", 1 << 16, made["meridional_v"], made["mixing_v"], specs=(VMEM, VMEM), after=(near_core, far_x),
    )
    parts = (near_core, near_x, far_core, far_x)

    if direct:
        localized, first = call(
            functools.partial(first_body, 2), (shape(*field_shape), piece),
            "first", 1 << 20, slot_owner, matrix, *parts, ens,
            specs=(HBM,) + (VMEM,) * 6,
            scratch=[pltpu.SMEM((SLOTS,), jnp.int32), pltpu.SemaphoreType.DMA],
        )
        got_two = swap_y(first)
        pair, single = call(
            send_body, (shape(2, levels, band_rows, width), piece), "send", 1 << 20,
            slot_owner, ens, localized, specs=(SMEM, VMEM, VMEM), after=(from_side, from_middle),
        )
        pair, got_two = lax.optimization_barrier((pair, got_two))
        got_pair = swap_y(pair)
        two = call(
            functools.partial(meet_body, 2), piece, "meet2", 1 << 19,
            slot_owner, ens, localized, got_two, specs=(SMEM,) + (VMEM,) * 3,
        )
        arrived = {2: turn_z(two, 2)}
        mine, across = call(
            weight_pick, (piece,) * 2, "weight_pick", 1 << 18, slot_owner, made["obs_v"],
            from_side, from_middle, specs=(SMEM,) + (VMEM,) * 3, after=(two,),
        )
        one, three = call(
            meet_pair_body, (piece,) * 2, "meet13", 1 << 19,
            slot_owner, ens, localized, got_pair, specs=(SMEM,) + (VMEM,) * 3,
            after=(two, across),
        )
        arrived[1], arrived[3] = turn_z(one, 1), turn_z(three, 3)
        single, across, _ = lax.optimization_barrier((single, across, got_pair))
        got_own, from_y = swap_y(single), swap_y(across)
        grad = call(
            last_body, piece, "last", 1 << 19, slot_owner, ens, localized, got_own,
            arrived[1], arrived[2], arrived[3], mine, from_y,
            specs=(SMEM,) + (VMEM,) * 8,
        )
        own = {0: grad, 3: turn_z(grad, 3), 1: turn_z(grad, 1)}
        weighted = call(
            functools.partial(spread_body, ((0, 0),), True, False), shape(*field_shape),
            "spread", 1 << 19, slot_owner, ens, grad, specs=(SMEM,) + (VMEM,) * 2,
        )
        other, weighted = lax.optimization_barrier((grad, weighted))
        other = {0: swap_y(other)}
        later, own[3], other[0] = lax.optimization_barrier((grad, own[3], other[0]))
        own[2] = turn_z(later, 2)
        other.update({s: swap_y(own[s]) for s in (1, 3, 2)})
        groups = (((0, 1), (1, 0), (3, 0)), ((1, 1), (3, 1), (2, 0)), ((2, 1),))
        for group in groups:
            final = group == groups[-1]
            grads = [other[s] if o else own[s] for s, o in group]
            pieces = tuple(group)
            extra = (transposed,) if final else ()
            result = call(
                functools.partial(spread_body, pieces, False, final),
                (shape(*half_shape), shape(*field_shape)) if final else shape(*field_shape),
                "spread%d" % group[0][0], 1 << 19,
                slot_owner, ens, *grads, weighted, *extra,
                specs=(SMEM,) + (VMEM,) * (2 + len(grads) + len(extra)),
            )
            weighted = result
        to_x, weighted = result
        own_core, own_x, to_core = call(
            functools.partial(blocks_body, 0), (shape(*half_shape),) * 3, "blocks", 1 << 19,
            transposed, weighted, specs=(VMEM,) * 2,
        )
    else:
        localized = call(
            localize_body, shape(*field_shape), "localize", 1 << 20, matrix, *parts,
            specs=(VMEM,) * 5,
        )
        partial = call(
            all_increments, shape(SLOTS, ens.shape[1], levels, band_rows, width),
            "increments", 1 << 20, ens, localized, specs=(VMEM,) * 2,
        )
        weights = jnp.stack(
            [
                lax.psum(jnp.where(mem == slot_owner[t], obs_weight[0], 0.0), "mem")
                for t in range(SLOTS)
            ]
        )
        share = lax.psum_scatter(
            partial.reshape(-1, width), "mem", scatter_dimension=0, tiled=True
        )
        share_rows = share.shape[0]
        weight_rows = lax.dynamic_slice_in_dim(
            weights.reshape(-1, width), mem * share_rows, share_rows, 0
        )
        gathered = lax.all_gather(weight_rows * share, "mem", axis=0, tiled=True)
        own_core, own_x, to_core, to_x, _ = call(
            all_weighted, (shape(*half_shape),) * 4 + (shape(*field_shape),), "weighted",
            1 << 20, ens, gathered.reshape(partial.shape), transposed,
            specs=(VMEM,) * 3,
        )
    got_x, got_core = swap_x(to_x), swap_core(to_core)
    half = call(
        functools.partial(zonal_adjoint, lat_count, 0), shape(*half_shape), "adjoint0", 1 << 19,
        made["shift_core"], made["taps_v"], control_v, own_core, got_core,
        specs=(VMEM,) * 5, scratch=tap_room,
    )
    return call(
        functools.partial(zonal_adjoint, lat_count, 1), shape(*field_shape), "adjoint1", 1 << 19,
        made["shift_x"], made["taps_v"], control_v, own_x, got_x, half,
        specs=(VMEM,) * 6, scratch=tap_room,
    )


def solution(mesh):
    z_count = SLOTS if mesh.shape["mem"] == 2 * SLOTS else 0
    in_specs = (
        P("mem", None, "lat", None),
        P(None, None, "mem", None, "lat", None),
        P("mem", None, None, "lat", None),
        P(),
        P("lat"),
        P("lat", None),
        P("lat", None),
        P("lat", None, None),
    )
    out_specs = P("mem", None, "lat", None)
    return jax.shard_map(
        functools.partial(per_device, z_count),
        mesh=mesh, in_specs=in_specs, out_specs=out_specs, check_vma=False,
    )
```

```python
import functools

import jax
import jax.numpy as jnp
from jax import lax
from jax.experimental import pallas as pl
from jax.experimental.pallas import tpu as pltpu
from jax.sharding import PartitionSpec as P

SLOTS = 4
BAND = 17
HALF = BAND // 2
LANES = 128
F32 = jnp.float32
BF16 = jnp.bfloat16

VMEM = pl.BlockSpec(memory_space=pltpu.VMEM)
SMEM = pl.BlockSpec(memory_space=pltpu.SMEM)
ANY = pl.BlockSpec(memory_space=pl.ANY)
HBM = pl.BlockSpec(memory_space=pltpu.HBM)


def call(body, outs, name, cost, *operands, specs, scratch=(), after=()):
    count, extra = len(operands), len(after)

    def kernel(*refs):
        body(*refs[:count], *refs[count + extra :])

    return pl.pallas_call(
        kernel,
        out_shape=outs,
        in_specs=list(specs) + [ANY] * extra,
        out_specs=jax.tree.map(lambda _: VMEM, outs),
        scratch_shapes=list(scratch),
        compiler_params=pltpu.CompilerParams(vmem_limit_bytes=16 << 20),
        cost_estimate=pl.CostEstimate(flops=cost, bytes_accessed=cost, transcendentals=0),
        name=name,
    )(*operands, *after)


def parity():
    return lax.axis_index("lat") & 1


def own_y():
    return lax.axis_index("mem") & 1


def own_z():
    return lax.axis_index("mem") >> 1


def entry_at(owners, step, value):
    place = own_z() ^ step
    found = jnp.int32(0)
    for t in range(SLOTS):
        rank = jnp.int32(0)
        for u in range(SLOTS):
            if u != t:
                rank += jnp.where(owners[u] < owners[t], 1, 0)
        found = jnp.where(rank == place, value(t), found)
    return found


def slot_at(owners, step):
    return entry_at(owners, step, lambda t: jnp.int32(t))


def owner_at(owners, step):
    return entry_at(owners, step, lambda t: owners[t])


def shape(*dims, dtype=F32):
    return jax.ShapeDtypeStruct(dims, dtype)


def shifted(columns, amount):
    lane = lax.broadcasted_iota(jnp.int32, columns[0].shape, 1)
    turned = [pltpu.roll(c, amount, 1) for c in columns]
    return [
        jnp.where(lane < amount, turned[i - 1], turned[i]) for i in range(len(columns))
    ]


def circle_filter(columns, amount, tap):
    count = len(columns)
    lane = lax.broadcasted_iota(jnp.int32, columns[0].shape, 1)
    fine = amount & (LANES - 1)
    source = (lane - fine) & (LANES - 1)
    turned = [
        jnp.take_along_axis(c, source, axis=1, mode="promise_in_bounds") for c in columns
    ]
    wraps = lane < fine
    columns = [jnp.where(wraps, turned[i - 1], turned[i]) for i in range(count)]
    step = 1
    while step < count:
        moved = (amount & (step * LANES)) != 0
        columns = [jnp.where(moved, columns[i - step], columns[i]) for i in range(count)]
        step *= 2
    near = [columns]
    for offset in range(1, 4):
        near.append(shifted(columns, offset))
    total = [tap(BAND - 1) * c for c in columns]
    for group in range((BAND - 1) // 4 - 1, -1, -1):
        total = shifted(total, 4)
        for offset in range(4):
            factor = tap(4 * group + offset)
            total = [t + factor * c for t, c in zip(total, near[offset])]
    return total


def row_shifts(shifts, first):
    row = lax.broadcasted_iota(jnp.int32, (8, LANES), 0)
    amounts = jnp.zeros((8, LANES), jnp.int32)
    for r in range(8):
        amounts = jnp.where(row == r, shifts[first + r], amounts)
    return amounts


def spread_taps(taps, first, spread):
    block = taps[pl.ds(first, 8), :]
    for k in range(BAND):
        spread[k] = jnp.broadcast_to(block[:, k : k + 1], (8, LANES))


def tiles(width):
    return [slice(i * LANES, (i + 1) * LANES) for i in range(width // LANES)]


def half_start(which):
    odd = parity()
    return pl.multiple_of((1 - odd if which == 0 else odd) * 8, 8)


def zonal_forward(first, shifts, taps, control, out):
    members, levels, _, width = control.shape
    amount = (width - HALF - shifts[...]) & (width - 1)

    def step(m, carry):
        for l in range(levels):
            columns = [control[m, l, pl.ds(first, 8), cut] for cut in tiles(width)]
            result = circle_filter(columns, amount, lambda k: taps[BAND - 1 - k])
            for cut, value in zip(tiles(width), result):
                out[m, l, :, cut] = value
        return carry

    lax.fori_loop(0, members, step, 0)


def front_body(names, *refs):
    r = dict(zip(names, refs))
    sems = r["sems"]
    first_x, first_core = half_start(1), half_start(0)
    rows_x, rows_core = pl.ds(first_x, 8), pl.ds(first_core, 8)
    moves = [
        (r["shift"], r["shift_s"]),
        (r["taps"], r["taps_v"]),
        (r["control"].at[:, :, rows_x], r["control_v"].at[:, :, rows_x]),
    ]
    moves.append((r["control"].at[:, :, rows_core], r["control_v"].at[:, :, rows_core]))
    moves.append((r["meridional"], r["meridional_v"]))
    moves.append((r["mixing"], r["mixing_v"]))
    if "obs" in r:
        moves.append((r["obs"].at[0], r["obs_v"]))
    moves.append((r["ens"], r["ens_v"]))
    copies = [pltpu.make_async_copy(a, b, sems.at[i]) for i, (a, b) in enumerate(moves)]
    for copy in copies:
        copy.start()
    for copy in copies[:3]:
        copy.wait()
    r["shift_x"][...] = row_shifts(r["shift_s"], first_x)
    r["shift_core"][...] = row_shifts(r["shift_s"], first_core)
    spread_taps(r["taps_v"], first_x, r["taps_x"])
    zonal_forward(first_x, r["shift_x"], r["taps_x"], r["control_v"], r["near_x"])
    for copy in copies[3:]:
        copy.wait()


def core_body(shifts, taps_v, control, out, taps):
    first = half_start(0)
    spread_taps(taps_v, first, taps)
    zonal_forward(first, shifts, taps, control, out)


def zonal_adjoint(lat_count, which, shifts, taps_v, control, own, got, *refs):
    other, out, taps = (None, *refs) if which == 0 else refs
    members, levels, _, width = control.shape
    first = half_start(which)
    amount = (shifts[...] - HALF) & (width - 1)
    spread_taps(taps_v, first, taps)
    lat = lax.axis_index("lat")
    alone = (which == 1) & ((lat == 0) | (lat == lat_count - 1))

    def step(m, carry):
        for l in range(levels):
            columns = [
                own[m, l, :, cut] + jnp.where(alone, 0.0, got[m, l, :, cut])
                for cut in tiles(width)
            ]
            result = circle_filter(columns, amount, lambda k: taps[k])
            for cut, value in zip(tiles(width), result):
                total = control[m, l, pl.ds(first, 8), cut] + value
                if which == 0:
                    out[m, l, :, cut] = total
                else:
                    out[m, l, pl.ds(first, 8), cut] = total
                    out[m, l, pl.ds(8 - first, 8), cut] = other[m, l, :, cut]
        return carry

    lax.fori_loop(0, members, step, 0)


def build_matrix(lat_count, taps_ref, mixing_ref, matrix, transposed):
    band_rows, levels = taps_ref.shape[0], mixing_ref.shape[1]
    rows, columns = matrix.shape
    odd, lat = parity(), lax.axis_index("lat")
    alone = (lat == 0) | (lat == lat_count - 1)
    column = lax.broadcasted_iota(jnp.int32, (band_rows, columns), 1)
    row = lax.broadcasted_iota(jnp.int32, (band_rows, columns), 0)
    block, level, inner = column // (8 * levels), (column // 8) % levels, column % 8
    even_start = jnp.where(block == 0, 16, jnp.where(block == 1, 8, jnp.where(block == 2, 24, 0)))
    odd_start = jnp.where(block == 0, 8, jnp.where(block == 1, 16, jnp.where(block == 2, 0, 24)))
    reach = jnp.where(odd == 1, odd_start, even_start) + inner - row
    band = jnp.zeros((band_rows, columns), F32)
    for k in range(BAND):
        band = jnp.where(reach == k, taps_ref[:, k : k + 1], band)
    band = jnp.where((block == 3) & alone, 0.0, band)
    same = lax.broadcasted_iota(jnp.int32, (band_rows, band_rows), 0) == (
        lax.broadcasted_iota(jnp.int32, (band_rows, band_rows), 1)
    )
    for a in range(levels):
        mixing = mixing_ref[a]
        factor = jnp.zeros((band_rows, columns), F32)
        for b in range(levels):
            by_lane = jnp.broadcast_to(mixing[b : b + 1, :], (band_rows, band_rows))
            by_row = jnp.sum(jnp.where(same, by_lane, 0.0), axis=1, keepdims=True)
            factor = jnp.where(level == b, by_row, factor)
        matrix[a * band_rows : (a + 1) * band_rows, :] = factor * band
    transposed[...] = matrix[...].T


def halves(value):
    high = value.astype(BF16)
    return high, (value - high.astype(F32)).astype(BF16)


def product(left, right):
    (lh, ll), (rh, rl) = left, right
    dot = functools.partial(jnp.dot, preferred_element_type=F32)
    return dot(lh, rh) + (dot(lh, rl) + dot(ll, rh))


CHUNK = 256


def localize(matrix, parts, out):
    members, levels, band_rows, width = out.shape
    left = halves(matrix[...])
    for m in range(members):
        for c in range(0, width, CHUNK):
            cut = slice(c, c + CHUNK)
            stack = jnp.concatenate(
                [p[m, l, :, cut] for p in parts for l in range(levels)], axis=0
            )
            result = product(left, halves(stack))
            for l in range(levels):
                out[m, l, :, cut] = result[l * band_rows : (l + 1) * band_rows]


def delocalize(matrix, weighted, first, parts):
    members, levels, band_rows, width = weighted.shape
    rows = slice(first * levels * 8, (first + len(parts)) * levels * 8)
    left = halves(matrix[rows, :])
    for m in range(members):
        for c in range(0, width, CHUNK):
            cut = slice(c, c + CHUNK)
            stack = jnp.concatenate([weighted[m, l, :, cut] for l in range(levels)], axis=0)
            result = product(left, halves(stack))
            for p, part in enumerate(parts):
                for l in range(levels):
                    start = (p * levels + l) * 8
                    part[m, l, :, cut] = result[start : start + 8]


def blocks_body(first, matrix, weighted, *parts):
    delocalize(matrix, weighted, first, parts)


def increment(ens, localized, slot, field, l):
    total = None
    for m in range(localized.shape[0]):
        term = ens[slot, field, m, l].astype(F32) * localized[m, l]
        total = term if total is None else total + term
    return total


def weight_pick(owners, here, side, middle, mine, across):
    place = owner_at(owners, 0) >> 1
    for found, weights in (
        (place == own_z(), here),
        (place == own_z() ^ 1, side),
        (place == own_z() ^ 3, middle),
    ):

        @pl.when(found)
        def _(weights=weights):
            mine[...] = weights[own_y()]
            across[...] = weights[1 - own_y()]


def first_body(step, owners_hbm, matrix, a, b, c, d, ens, localized, send, owners, sem):
    copy = pltpu.make_async_copy(owners_hbm, owners, sem)
    copy.start()
    localize(matrix, (a, b, c, d), localized)
    copy.wait()
    slot = slot_at(owners, step)
    for l in range(localized.shape[1]):
        send[l] = increment(ens, localized, slot, 1 - own_y(), l)


def send_body(owners, ens, localized, three, one):
    for step, field, send in (
        (3, 1 - own_y(), three), (1, own_y(), one.at[0]), (1, 1 - own_y(), one.at[1])
    ):
        slot = slot_at(owners, step)
        for l in range(localized.shape[1]):
            send[l] = increment(ens, localized, slot, field, l)


def cross_body(owners, ens, localized, got, out):
    slot = slot_at(owners, 0)
    for l in range(localized.shape[1]):
        out[l] = increment(ens, localized, slot, 1 - own_y(), l) + got[1, l]


def meet_body(step, owners, ens, localized, got, out):
    slot = slot_at(owners, step)
    for l in range(localized.shape[1]):
        out[l] = increment(ens, localized, slot, own_y(), l) + got[l]


def last_body(owners, ens, localized, got_y, got_1, got_2, got_3, mine, from_y, out):
    slot = slot_at(owners, 0)
    held = (owner_at(owners, 0) & 1) == own_y()
    for here, weight in ((held, mine), (jnp.logical_not(held), from_y)):

        @pl.when(here)
        def _(weight=weight):
            for l in range(localized.shape[1]):
                out[l] = weight[l] * (
                    increment(ens, localized, slot, own_y(), l)
                    + got_y[l]
                    + (got_1[0, l] + got_2[l] + got_3[l])
                )


def spread_body(pieces, first, final, owners, ens, *refs):
    refs = list(refs)
    grads = [refs.pop(0) for _ in pieces]
    before = None if first else refs.pop(0)
    matrix = refs.pop(0) if final else None
    out = refs[-1] if final else refs[0]
    members, levels = out.shape[:2]
    places = [
        (slot_at(owners, step), 1 - own_y() if other else own_y()) for step, other in pieces
    ]
    for m in range(members):
        for l in range(levels):
            total = None if before is None else before[m, l]
            for (slot, field), grad in zip(places, grads):
                term = ens[slot, field, m, l].astype(F32) * grad[l]
                total = term if total is None else total + term
            out[m, l] = total
    if final:
        delocalize(matrix, out, 3, refs[:1])


def all_increments(ens, localized, out):
    for slot in range(out.shape[0]):
        for field in range(out.shape[1]):
            for l in range(out.shape[2]):
                out[slot, field, l] = increment(ens, localized, slot, field, l)


def localize_body(matrix, a, b, c, d, localized):
    localize(matrix, (a, b, c, d), localized)


def all_weighted(ens, grad, matrix, a, b, c, d, out):
    members, levels = out.shape[:2]
    for m in range(members):
        for l in range(levels):
            total = None
            for slot in range(ens.shape[0]):
                for field in range(ens.shape[1]):
                    term = ens[slot, field, m, l].astype(F32) * grad[slot, field, l]
                    total = term if total is None else total + term
            out[m, l] = total
    delocalize(matrix, out, 0, (a, b, c, d))


def per_device(
    z_count,
    control,
    perturbations,
    obs_weight,
    slot_owner,
    zonal_shift,
    zonal_taps,
    meridional_taps,
    level_mixing,
):
    members, levels, band_rows, width = control.shape
    mem_count, lat_count = lax.axis_size("mem"), lax.axis_size("lat")
    mem = lax.axis_index("mem")
    direct = z_count > 0
    field_shape = (members, levels, band_rows, width)
    half_shape = (members, levels, 8, width)
    piece = shape(levels, band_rows, width)
    core_pairs = [(i, i ^ 1) for i in range(lat_count)]
    x_swaps = [
        (m * lat_count + i, (m ^ 1) * lat_count + i)
        if i in (0, lat_count - 1)
        else (m * lat_count + i, m * lat_count + ((i - 1) ^ 1) + 1)
        for m in range(mem_count)
        for i in range(lat_count)
    ]
    swap_core = lambda v: lax.ppermute(v, "lat", core_pairs)
    swap_x = lambda v: lax.ppermute(v, ("mem", "lat"), x_swaps)
    tap_room = [pltpu.VMEM((BAND, 8, LANES), F32)]
    ins = {
        "shift": zonal_shift, "taps": zonal_taps, "control": control,
        "meridional": meridional_taps, "ens": perturbations,
        "mixing": jnp.transpose(level_mixing, (1, 2, 0)),
    }
    results = {
        "near_x": shape(*half_shape), "control_v": shape(*field_shape),
        "taps_v": shape(*zonal_taps.shape), "meridional_v": shape(*meridional_taps.shape),
        "shift_x": shape(8, LANES, dtype=jnp.int32),
        "shift_core": shape(8, LANES, dtype=jnp.int32),
        "ens_v": shape(*perturbations.shape, dtype=BF16),
        "mixing_v": shape(levels, levels, band_rows),
    }
    if direct:
        ins["obs"] = obs_weight
        results["obs_v"] = shape(*obs_weight.shape[1:])
    names = (*ins, *results, "taps_x", "shift_s", "sems")
    made = call(
        functools.partial(front_body, names), tuple(results.values()), "front", 1 << 19,
        *(pltpu.with_memory_space_constraint(v, pltpu.HBM) for v in ins.values()),
        specs=(HBM,) * len(ins),
        scratch=[
            *tap_room, pltpu.SMEM(zonal_shift.shape, jnp.int32), pltpu.SemaphoreType.DMA((8,)),
        ],
    )
    made = dict(zip(results, made))
    near_x, control_v, ens = made["near_x"], made["control_v"], made["ens_v"]
    far_x = swap_x(near_x)
    if direct:
        y_pairs = [(i, i ^ 1) for i in range(mem_count)]
        swap_y = lambda v: lax.ppermute(v, "mem", y_pairs)
        turn_z = lambda v, s: lax.ppermute(
            v, "mem", [(i, i ^ 2 * s) for i in range(mem_count)]
        )
        middle = [(i, i ^ 6) for i in range(2, mem_count - 2)]
        from_side = turn_z(made["obs_v"], 1)
        from_middle = lax.ppermute(made["obs_v"], "mem", middle)
    near_core = call(
        core_body, shape(*half_shape), "core", 1 << 19, made["shift_core"], made["taps_v"],
        control_v, specs=(VMEM,) * 3, scratch=tap_room,
    )
    far_core = swap_core(near_core)
    matrix, transposed = call(
        functools.partial(build_matrix, lat_count),
        (shape(levels * band_rows, 32 * levels), shape(32 * levels, levels * band_rows)),
        "matrix", 1 << 16, made["meridional_v"], made["mixing_v"], specs=(VMEM, VMEM), after=(near_core, far_x),
    )
    parts = (near_core, near_x, far_core, far_x)

    if direct:
        localized, first = call(
            functools.partial(first_body, 2), (shape(*field_shape), piece),
            "first", 1 << 20, slot_owner, matrix, *parts, ens,
            specs=(HBM,) + (VMEM,) * 6,
            scratch=[pltpu.SMEM((SLOTS,), jnp.int32), pltpu.SemaphoreType.DMA],
        )
        got_two = swap_y(first)
        three, one = call(
            send_body, (piece, shape(2, levels, band_rows, width)), "send", 1 << 20,
            slot_owner, ens, localized, specs=(SMEM, VMEM, VMEM), after=(from_side, from_middle),
        )

        def meet(s, got, after):
            return call(
                functools.partial(meet_body, s), piece, "meet%d" % s, 1 << 19,
                slot_owner, ens, localized, got, specs=(SMEM,) + (VMEM,) * 3, after=after,
            )

        three, got_two = lax.optimization_barrier((three, got_two))
        got_three = swap_y(three)
        two = meet(2, got_two, ())
        arrived = {2: turn_z(two, 2), 1: turn_z(one, 1)}
        mine, across = call(
            weight_pick, (piece,) * 2, "weight_pick", 1 << 18, slot_owner, made["obs_v"],
            from_side, from_middle, specs=(SMEM,) + (VMEM,) * 3, after=(two,),
        )
        three = meet(3, got_three, (two, across))
        arrived[3] = turn_z(three, 3)
        across, _ = lax.optimization_barrier((across, got_three))
        from_y = swap_y(across)
        cross = call(
            cross_body, piece, "cross", 1 << 19, slot_owner, ens, localized, arrived[1],
            specs=(SMEM,) + (VMEM,) * 3, after=(three,),
        )
        got_own = swap_y(cross)
        grad = call(
            last_body, piece, "last", 1 << 19, slot_owner, ens, localized, got_own,
            arrived[1], arrived[2], arrived[3], mine, from_y,
            specs=(SMEM,) + (VMEM,) * 8,
        )
        own = {0: grad, 3: turn_z(grad, 3), 1: turn_z(grad, 1)}
        weighted = call(
            functools.partial(spread_body, ((0, 0),), True, False), shape(*field_shape),
            "spread", 1 << 19, slot_owner, ens, grad, specs=(SMEM,) + (VMEM,) * 2,
        )
        other, weighted = lax.optimization_barrier((grad, weighted))
        other = {0: swap_y(other)}
        later, own[3], other[0] = lax.optimization_barrier((grad, own[3], other[0]))
        own[2] = turn_z(later, 2)
        along, own[1] = lax.optimization_barrier((other[0], own[1]))
        other[1] = turn_z(along, 1)
        other.update({s: swap_y(own[s]) for s in (3, 2)})
        groups = (((0, 1), (1, 0), (3, 0)), ((1, 1), (3, 1), (2, 0)), ((2, 1),))
        for group in groups:
            final = group == groups[-1]
            grads = [other[s] if o else own[s] for s, o in group]
            pieces = tuple(group)
            extra = (transposed,) if final else ()
            result = call(
                functools.partial(spread_body, pieces, False, final),
                (shape(*half_shape), shape(*field_shape)) if final else shape(*field_shape),
                "spread%d" % group[0][0], 1 << 19,
                slot_owner, ens, *grads, weighted, *extra,
                specs=(SMEM,) + (VMEM,) * (2 + len(grads) + len(extra)),
            )
            weighted = result
        to_x, weighted = result
        own_core, own_x, to_core = call(
            functools.partial(blocks_body, 0), (shape(*half_shape),) * 3, "blocks", 1 << 19,
            transposed, weighted, specs=(VMEM,) * 2,
        )
    else:
        localized = call(
            localize_body, shape(*field_shape), "localize", 1 << 20, matrix, *parts,
            specs=(VMEM,) * 5,
        )
        partial = call(
            all_increments, shape(SLOTS, ens.shape[1], levels, band_rows, width),
            "increments", 1 << 20, ens, localized, specs=(VMEM,) * 2,
        )
        weights = jnp.stack(
            [
                lax.psum(jnp.where(mem == slot_owner[t], obs_weight[0], 0.0), "mem")
                for t in range(SLOTS)
            ]
        )
        share = lax.psum_scatter(
            partial.reshape(-1, width), "mem", scatter_dimension=0, tiled=True
        )
        share_rows = share.shape[0]
        weight_rows = lax.dynamic_slice_in_dim(
            weights.reshape(-1, width), mem * share_rows, share_rows, 0
        )
        gathered = lax.all_gather(weight_rows * share, "mem", axis=0, tiled=True)
        own_core, own_x, to_core, to_x, _ = call(
            all_weighted, (shape(*half_shape),) * 4 + (shape(*field_shape),), "weighted",
            1 << 20, ens, gathered.reshape(partial.shape), transposed,
            specs=(VMEM,) * 3,
        )
    got_x, got_core = swap_x(to_x), swap_core(to_core)
    half = call(
        functools.partial(zonal_adjoint, lat_count, 0), shape(*half_shape), "adjoint0", 1 << 19,
        made["shift_core"], made["taps_v"], control_v, own_core, got_core,
        specs=(VMEM,) * 5, scratch=tap_room,
    )
    return call(
        functools.partial(zonal_adjoint, lat_count, 1), shape(*field_shape), "adjoint1", 1 << 19,
        made["shift_x"], made["taps_v"], control_v, own_x, got_x, half,
        specs=(VMEM,) * 6, scratch=tap_room,
    )


def solution(mesh):
    z_count = SLOTS if mesh.shape["mem"] == 2 * SLOTS else 0
    in_specs = (
        P("mem", None, "lat", None),
        P(None, None, "mem", None, "lat", None),
        P("mem", None, None, "lat", None),
        P(),
        P("lat"),
        P("lat", None),
        P("lat", None),
        P("lat", None, None),
    )
    out_specs = P("mem", None, "lat", None)
    return jax.shard_map(
        functools.partial(per_device, z_count),
        mesh=mesh, in_specs=in_specs, out_specs=out_specs, check_vma=False,
    )
```

```python
import functools

import jax
import jax.numpy as jnp
from jax import lax
from jax.experimental import pallas as pl
from jax.experimental.pallas import tpu as pltpu
from jax.sharding import PartitionSpec as P

SLOTS = 4
BAND = 17
HALF = BAND // 2
LANES = 128
F32 = jnp.float32
BF16 = jnp.bfloat16

VMEM = pl.BlockSpec(memory_space=pltpu.VMEM)
SMEM = pl.BlockSpec(memory_space=pltpu.SMEM)
ANY = pl.BlockSpec(memory_space=pl.ANY)
HBM = pl.BlockSpec(memory_space=pltpu.HBM)


def call(body, outs, name, cost, *operands, specs, scratch=(), after=()):
    count, extra = len(operands), len(after)

    def kernel(*refs):
        body(*refs[:count], *refs[count + extra :])

    return pl.pallas_call(
        kernel,
        out_shape=outs,
        in_specs=list(specs) + [ANY] * extra,
        out_specs=jax.tree.map(lambda _: VMEM, outs),
        scratch_shapes=list(scratch),
        compiler_params=pltpu.CompilerParams(vmem_limit_bytes=16 << 20),
        cost_estimate=pl.CostEstimate(flops=cost, bytes_accessed=cost, transcendentals=0),
        name=name,
    )(*operands, *after)


def parity():
    return lax.axis_index("lat") & 1


def own_y():
    return lax.axis_index("mem") & 1


def own_z():
    return lax.axis_index("mem") >> 1


def entry_at(owners, step, value):
    place = own_z() ^ step
    found = jnp.int32(0)
    for t in range(SLOTS):
        rank = jnp.int32(0)
        for u in range(SLOTS):
            if u != t:
                rank += jnp.where(owners[u] < owners[t], 1, 0)
        found = jnp.where(rank == place, value(t), found)
    return found


def slot_at(owners, step):
    return entry_at(owners, step, lambda t: jnp.int32(t))


def owner_at(owners, step):
    return entry_at(owners, step, lambda t: owners[t])


def shape(*dims, dtype=F32):
    return jax.ShapeDtypeStruct(dims, dtype)


def shifted(columns, amount):
    lane = lax.broadcasted_iota(jnp.int32, columns[0].shape, 1)
    turned = [pltpu.roll(c, amount, 1) for c in columns]
    return [
        jnp.where(lane < amount, turned[i - 1], turned[i]) for i in range(len(columns))
    ]


def circle_filter(columns, amount, tap):
    count = len(columns)
    lane = lax.broadcasted_iota(jnp.int32, columns[0].shape, 1)
    fine = amount & (LANES - 1)
    source = (lane - fine) & (LANES - 1)
    turned = [
        jnp.take_along_axis(c, source, axis=1, mode="promise_in_bounds") for c in columns
    ]
    wraps = lane < fine
    columns = [jnp.where(wraps, turned[i - 1], turned[i]) for i in range(count)]
    step = 1
    while step < count:
        moved = (amount & (step * LANES)) != 0
        columns = [jnp.where(moved, columns[i - step], columns[i]) for i in range(count)]
        step *= 2
    near = [columns]
    for offset in range(1, 4):
        near.append(shifted(columns, offset))
    total = [tap(BAND - 1) * c for c in columns]
    for group in range((BAND - 1) // 4 - 1, -1, -1):
        total = shifted(total, 4)
        for offset in range(4):
            factor = tap(4 * group + offset)
            total = [t + factor * c for t, c in zip(total, near[offset])]
    return total


def row_shifts(shifts, first):
    row = lax.broadcasted_iota(jnp.int32, (8, LANES), 0)
    amounts = jnp.zeros((8, LANES), jnp.int32)
    for r in range(8):
        amounts = jnp.where(row == r, shifts[first + r], amounts)
    return amounts


def spread_taps(taps, first, spread):
    block = taps[pl.ds(first, 8), :]
    for k in range(BAND):
        spread[k] = jnp.broadcast_to(block[:, k : k + 1], (8, LANES))


def tiles(width):
    return [slice(i * LANES, (i + 1) * LANES) for i in range(width // LANES)]


def half_start(which):
    odd = parity()
    return pl.multiple_of((1 - odd if which == 0 else odd) * 8, 8)


def zonal_forward(first, shifts, taps, control, out):
    members, levels, _, width = control.shape
    amount = (width - HALF - shifts[...]) & (width - 1)

    def step(m, carry):
        for l in range(levels):
            columns = [control[m, l, pl.ds(first, 8), cut] for cut in tiles(width)]
            result = circle_filter(columns, amount, lambda k: taps[BAND - 1 - k])
            for cut, value in zip(tiles(width), result):
                out[m, l, :, cut] = value
        return carry

    lax.fori_loop(0, members, step, 0)


def front_body(names, *refs):
    r = dict(zip(names, refs))
    sems = r["sems"]
    first_x, first_core = half_start(1), half_start(0)
    rows_x, rows_core = pl.ds(first_x, 8), pl.ds(first_core, 8)
    moves = [
        (r["shift"], r["shift_s"]),
        (r["taps"], r["taps_v"]),
        (r["control"].at[:, :, rows_x], r["control_v"].at[:, :, rows_x]),
    ]
    moves.append((r["control"].at[:, :, rows_core], r["control_v"].at[:, :, rows_core]))
    moves.append((r["meridional"], r["meridional_v"]))
    moves.append((r["mixing"], r["mixing_v"]))
    if "obs" in r:
        moves.append((r["obs"].at[0], r["obs_v"]))
    moves.append((r["ens"], r["ens_v"]))
    copies = [pltpu.make_async_copy(a, b, sems.at[i]) for i, (a, b) in enumerate(moves)]
    for copy in copies:
        copy.start()
    for copy in copies[:3]:
        copy.wait()
    r["shift_x"][...] = row_shifts(r["shift_s"], first_x)
    r["shift_core"][...] = row_shifts(r["shift_s"], first_core)
    spread_taps(r["taps_v"], first_x, r["taps_x"])
    zonal_forward(first_x, r["shift_x"], r["taps_x"], r["control_v"], r["near_x"])
    for copy in copies[3:]:
        copy.wait()


def core_body(shifts, taps_v, control, out, taps):
    first = half_start(0)
    spread_taps(taps_v, first, taps)
    zonal_forward(first, shifts, taps, control, out)


def zonal_adjoint(lat_count, which, shifts, taps_v, control, own, got, *refs):
    other, out, taps = (None, *refs) if which == 0 else refs
    members, levels, _, width = control.shape
    first = half_start(which)
    amount = (shifts[...] - HALF) & (width - 1)
    spread_taps(taps_v, first, taps)
    lat = lax.axis_index("lat")
    alone = (which == 1) & ((lat == 0) | (lat == lat_count - 1))

    def step(m, carry):
        for l in range(levels):
            columns = [
                own[m, l, :, cut] + jnp.where(alone, 0.0, got[m, l, :, cut])
                for cut in tiles(width)
            ]
            result = circle_filter(columns, amount, lambda k: taps[k])
            for cut, value in zip(tiles(width), result):
                total = control[m, l, pl.ds(first, 8), cut] + value
                if which == 0:
                    out[m, l, :, cut] = total
                else:
                    out[m, l, pl.ds(first, 8), cut] = total
                    out[m, l, pl.ds(8 - first, 8), cut] = other[m, l, :, cut]
        return carry

    lax.fori_loop(0, members, step, 0)


def build_matrix(lat_count, taps_ref, mixing_ref, matrix, transposed):
    band_rows, levels = taps_ref.shape[0], mixing_ref.shape[1]
    rows, columns = matrix.shape
    odd, lat = parity(), lax.axis_index("lat")
    alone = (lat == 0) | (lat == lat_count - 1)
    column = lax.broadcasted_iota(jnp.int32, (band_rows, columns), 1)
    row = lax.broadcasted_iota(jnp.int32, (band_rows, columns), 0)
    block, level, inner = column // (8 * levels), (column // 8) % levels, column % 8
    even_start = jnp.where(block == 0, 16, jnp.where(block == 1, 8, jnp.where(block == 2, 24, 0)))
    odd_start = jnp.where(block == 0, 8, jnp.where(block == 1, 16, jnp.where(block == 2, 0, 24)))
    reach = jnp.where(odd == 1, odd_start, even_start) + inner - row
    band = jnp.zeros((band_rows, columns), F32)
    for k in range(BAND):
        band = jnp.where(reach == k, taps_ref[:, k : k + 1], band)
    band = jnp.where((block == 3) & alone, 0.0, band)
    same = lax.broadcasted_iota(jnp.int32, (band_rows, band_rows), 0) == (
        lax.broadcasted_iota(jnp.int32, (band_rows, band_rows), 1)
    )
    for a in range(levels):
        mixing = mixing_ref[a]
        factor = jnp.zeros((band_rows, columns), F32)
        for b in range(levels):
            by_lane = jnp.broadcast_to(mixing[b : b + 1, :], (band_rows, band_rows))
            by_row = jnp.sum(jnp.where(same, by_lane, 0.0), axis=1, keepdims=True)
            factor = jnp.where(level == b, by_row, factor)
        matrix[a * band_rows : (a + 1) * band_rows, :] = factor * band
    transposed[...] = matrix[...].T


def halves(value):
    high = value.astype(BF16)
    return high, (value - high.astype(F32)).astype(BF16)


def product(left, right):
    (lh, ll), (rh, rl) = left, right
    dot = functools.partial(jnp.dot, preferred_element_type=F32)
    return dot(lh, rh) + (dot(lh, rl) + dot(ll, rh))


CHUNK = 256


def localize(matrix, parts, out):
    members, levels, band_rows, width = out.shape
    left = halves(matrix[...])
    for m in range(members):
        for c in range(0, width, CHUNK):
            cut = slice(c, c + CHUNK)
            stack = jnp.concatenate(
                [p[m, l, :, cut] for p in parts for l in range(levels)], axis=0
            )
            result = product(left, halves(stack))
            for l in range(levels):
                out[m, l, :, cut] = result[l * band_rows : (l + 1) * band_rows]


def delocalize(matrix, weighted, first, parts):
    members, levels, band_rows, width = weighted.shape
    rows = slice(first * levels * 8, (first + len(parts)) * levels * 8)
    left = halves(matrix[rows, :])
    for m in range(members):
        for c in range(0, width, CHUNK):
            cut = slice(c, c + CHUNK)
            stack = jnp.concatenate([weighted[m, l, :, cut] for l in range(levels)], axis=0)
            result = product(left, halves(stack))
            for p, part in enumerate(parts):
                for l in range(levels):
                    start = (p * levels + l) * 8
                    part[m, l, :, cut] = result[start : start + 8]


def blocks_body(first, matrix, weighted, *parts):
    delocalize(matrix, weighted, first, parts)


def increment(ens, localized, slot, field, l):
    total = None
    for m in range(localized.shape[0]):
        term = ens[slot, field, m, l].astype(F32) * localized[m, l]
        total = term if total is None else total + term
    return total


def weight_pick(owners, here, side, middle, mine, across):
    place = owner_at(owners, 0) >> 1
    for found, weights in (
        (place == own_z(), here),
        (place == own_z() ^ 1, side),
        (place == own_z() ^ 3, middle),
    ):

        @pl.when(found)
        def _(weights=weights):
            mine[...] = weights[own_y()]
            across[...] = weights[1 - own_y()]


def first_body(step, owners_hbm, matrix, a, b, c, d, ens, localized, send, owners, sem):
    copy = pltpu.make_async_copy(owners_hbm, owners, sem)
    copy.start()
    localize(matrix, (a, b, c, d), localized)
    copy.wait()
    slot = slot_at(owners, step)
    for l in range(localized.shape[1]):
        send[l] = increment(ens, localized, slot, 1 - own_y(), l)


def send_body(owners, ens, localized, three, one):
    for step, field, send in (
        (3, 1 - own_y(), three), (1, own_y(), one.at[0]), (1, 1 - own_y(), one.at[1])
    ):
        slot = slot_at(owners, step)
        for l in range(localized.shape[1]):
            send[l] = increment(ens, localized, slot, field, l)


def cross_body(owners, ens, localized, got, out):
    slot = slot_at(owners, 0)
    for l in range(localized.shape[1]):
        out[l] = increment(ens, localized, slot, 1 - own_y(), l) + got[1, l]


def meet_body(step, owners, ens, localized, got, out):
    slot = slot_at(owners, step)
    for l in range(localized.shape[1]):
        out[l] = increment(ens, localized, slot, own_y(), l) + got[l]


def last_body(owners, ens, localized, got_y, got_1, got_2, got_3, mine, from_y, out):
    slot = slot_at(owners, 0)
    held = (owner_at(owners, 0) & 1) == own_y()
    for here, weight in ((held, mine), (jnp.logical_not(held), from_y)):

        @pl.when(here)
        def _(weight=weight):
            for l in range(localized.shape[1]):
                out[l] = weight[l] * (
                    increment(ens, localized, slot, own_y(), l)
                    + got_y[l]
                    + (got_1[0, l] + got_2[l] + got_3[l])
                )


def spread_body(pieces, first, final, owners, ens, *refs):
    refs = list(refs)
    grads = [refs.pop(0) for _ in pieces]
    before = None if first else refs.pop(0)
    matrix = refs.pop(0) if final else None
    out = refs[-1] if final else refs[0]
    members, levels = out.shape[:2]
    places = [
        (slot_at(owners, step), 1 - own_y() if other else own_y()) for step, other in pieces
    ]
    for m in range(members):
        for l in range(levels):
            total = None if before is None else before[m, l]
            for (slot, field), grad in zip(places, grads):
                term = ens[slot, field, m, l].astype(F32) * grad[l]
                total = term if total is None else total + term
            out[m, l] = total
    if final:
        delocalize(matrix, out, 3, refs[:1])


def all_increments(ens, localized, out):
    for slot in range(out.shape[0]):
        for field in range(out.shape[1]):
            for l in range(out.shape[2]):
                out[slot, field, l] = increment(ens, localized, slot, field, l)


def localize_body(matrix, a, b, c, d, localized):
    localize(matrix, (a, b, c, d), localized)


def all_weighted(ens, grad, matrix, a, b, c, d, out):
    members, levels = out.shape[:2]
    for m in range(members):
        for l in range(levels):
            total = None
            for slot in range(ens.shape[0]):
                for field in range(ens.shape[1]):
                    term = ens[slot, field, m, l].astype(F32) * grad[slot, field, l]
                    total = term if total is None else total + term
            out[m, l] = total
    delocalize(matrix, out, 0, (a, b, c, d))


def per_device(
    z_count,
    control,
    perturbations,
    obs_weight,
    slot_owner,
    zonal_shift,
    zonal_taps,
    meridional_taps,
    level_mixing,
):
    members, levels, band_rows, width = control.shape
    mem_count, lat_count = lax.axis_size("mem"), lax.axis_size("lat")
    mem = lax.axis_index("mem")
    direct = z_count > 0
    field_shape = (members, levels, band_rows, width)
    half_shape = (members, levels, 8, width)
    piece = shape(levels, band_rows, width)
    core_pairs = [(i, i ^ 1) for i in range(lat_count)]
    x_swaps = [
        (m * lat_count + i, (m ^ 1) * lat_count + i)
        if i in (0, lat_count - 1)
        else (m * lat_count + i, m * lat_count + ((i - 1) ^ 1) + 1)
        for m in range(mem_count)
        for i in range(lat_count)
    ]
    swap_core = lambda v: lax.ppermute(v, "lat", core_pairs)
    swap_x = lambda v: lax.ppermute(v, ("mem", "lat"), x_swaps)
    tap_room = [pltpu.VMEM((BAND, 8, LANES), F32)]
    ins = {
        "shift": zonal_shift, "taps": zonal_taps, "control": control,
        "meridional": meridional_taps, "ens": perturbations,
        "mixing": jnp.transpose(level_mixing, (1, 2, 0)),
    }
    results = {
        "near_x": shape(*half_shape), "control_v": shape(*field_shape),
        "taps_v": shape(*zonal_taps.shape), "meridional_v": shape(*meridional_taps.shape),
        "shift_x": shape(8, LANES, dtype=jnp.int32),
        "shift_core": shape(8, LANES, dtype=jnp.int32),
        "ens_v": shape(*perturbations.shape, dtype=BF16),
        "mixing_v": shape(levels, levels, band_rows),
    }
    if direct:
        ins["obs"] = obs_weight
        results["obs_v"] = shape(*obs_weight.shape[1:])
    names = (*ins, *results, "taps_x", "shift_s", "sems")
    made = call(
        functools.partial(front_body, names), tuple(results.values()), "front", 1 << 19,
        *(pltpu.with_memory_space_constraint(v, pltpu.HBM) for v in ins.values()),
        specs=(HBM,) * len(ins),
        scratch=[
            *tap_room, pltpu.SMEM(zonal_shift.shape, jnp.int32), pltpu.SemaphoreType.DMA((8,)),
        ],
    )
    made = dict(zip(results, made))
    near_x, control_v, ens = made["near_x"], made["control_v"], made["ens_v"]
    far_x = swap_x(near_x)
    if direct:
        y_pairs = [(i, i ^ 1) for i in range(mem_count)]
        swap_y = lambda v: lax.ppermute(v, "mem", y_pairs)
        turn_z = lambda v, s: lax.ppermute(
            v, "mem", [(i, i ^ 2 * s) for i in range(mem_count)]
        )
        middle = [(i, i ^ 6) for i in range(2, mem_count - 2)]
        from_side = turn_z(made["obs_v"], 1)
        from_middle = lax.ppermute(made["obs_v"], "mem", middle)
    near_core = call(
        core_body, shape(*half_shape), "core", 1 << 19, made["shift_core"], made["taps_v"],
        control_v, specs=(VMEM,) * 3, scratch=tap_room,
    )
    far_core = swap_core(near_core)
    matrix, transposed = call(
        functools.partial(build_matrix, lat_count),
        (shape(levels * band_rows, 32 * levels), shape(32 * levels, levels * band_rows)),
        "matrix", 1 << 16, made["meridional_v"], made["mixing_v"], specs=(VMEM, VMEM), after=(near_core, far_x),
    )
    parts = (near_core, near_x, far_core, far_x)

    if direct:
        localized, first = call(
            functools.partial(first_body, 2), (shape(*field_shape), piece),
            "first", 1 << 20, slot_owner, matrix, *parts, ens,
            specs=(HBM,) + (VMEM,) * 6,
            scratch=[pltpu.SMEM((SLOTS,), jnp.int32), pltpu.SemaphoreType.DMA],
        )
        got_two = swap_y(first)
        three, one = call(
            send_body, (piece, shape(2, levels, band_rows, width)), "send", 1 << 20,
            slot_owner, ens, localized, specs=(SMEM, VMEM, VMEM), after=(from_side, from_middle),
        )

        def meet(s, got, after):
            return call(
                functools.partial(meet_body, s), piece, "meet%d" % s, 1 << 19,
                slot_owner, ens, localized, got, specs=(SMEM,) + (VMEM,) * 3, after=after,
            )

        three, got_two = lax.optimization_barrier((three, got_two))
        got_three = swap_y(three)
        two = meet(2, got_two, ())
        arrived = {2: turn_z(two, 2), 1: turn_z(one, 1)}
        mine, across = call(
            weight_pick, (piece,) * 2, "weight_pick", 1 << 18, slot_owner, made["obs_v"],
            from_side, from_middle, specs=(SMEM,) + (VMEM,) * 3, after=(two,),
        )
        three = meet(3, got_three, (two, across))
        arrived[3] = turn_z(three, 3)
        across, _ = lax.optimization_barrier((across, got_three))
        from_y = swap_y(across)
        cross = call(
            cross_body, piece, "cross", 1 << 19, slot_owner, ens, localized, arrived[1],
            specs=(SMEM,) + (VMEM,) * 3, after=(three,),
        )
        got_own = swap_y(cross)
        grad = call(
            last_body, piece, "last", 1 << 19, slot_owner, ens, localized, got_own,
            arrived[1], arrived[2], arrived[3], mine, from_y,
            specs=(SMEM,) + (VMEM,) * 8,
        )
        own = {0: grad, 3: turn_z(grad, 3)}
        weighted = call(
            functools.partial(spread_body, ((0, 0),), True, False), shape(*field_shape),
            "spread", 1 << 19, slot_owner, ens, grad, specs=(SMEM,) + (VMEM,) * 2,
        )
        other, weighted = lax.optimization_barrier((grad, weighted))
        other = {0: swap_y(other)}
        later, own[3], other[0] = lax.optimization_barrier((grad, own[3], other[0]))
        own[2] = turn_z(later, 2)
        along, near = lax.optimization_barrier((other[0], grad))
        own[1], other[1] = turn_z(near, 1), turn_z(along, 1)
        other.update({s: swap_y(own[s]) for s in (3, 2)})
        groups = (((0, 1), (1, 0), (3, 0)), ((1, 1), (3, 1), (2, 0)), ((2, 1),))
        for group in groups:
            final = group == groups[-1]
            grads = [other[s] if o else own[s] for s, o in group]
            pieces = tuple(group)
            extra = (transposed,) if final else ()
            result = call(
                functools.partial(spread_body, pieces, False, final),
                (shape(*half_shape), shape(*field_shape)) if final else shape(*field_shape),
                "spread%d" % group[0][0], 1 << 19,
                slot_owner, ens, *grads, weighted, *extra,
                specs=(SMEM,) + (VMEM,) * (2 + len(grads) + len(extra)),
            )
            weighted = result
        to_x, weighted = result
        own_core, own_x, to_core = call(
            functools.partial(blocks_body, 0), (shape(*half_shape),) * 3, "blocks", 1 << 19,
            transposed, weighted, specs=(VMEM,) * 2,
        )
    else:
        localized = call(
            localize_body, shape(*field_shape), "localize", 1 << 20, matrix, *parts,
            specs=(VMEM,) * 5,
        )
        partial = call(
            all_increments, shape(SLOTS, ens.shape[1], levels, band_rows, width),
            "increments", 1 << 20, ens, localized, specs=(VMEM,) * 2,
        )
        weights = jnp.stack(
            [
                lax.psum(jnp.where(mem == slot_owner[t], obs_weight[0], 0.0), "mem")
                for t in range(SLOTS)
            ]
        )
        share = lax.psum_scatter(
            partial.reshape(-1, width), "mem", scatter_dimension=0, tiled=True
        )
        share_rows = share.shape[0]
        weight_rows = lax.dynamic_slice_in_dim(
            weights.reshape(-1, width), mem * share_rows, share_rows, 0
        )
        gathered = lax.all_gather(weight_rows * share, "mem", axis=0, tiled=True)
        own_core, own_x, to_core, to_x, _ = call(
            all_weighted, (shape(*half_shape),) * 4 + (shape(*field_shape),), "weighted",
            1 << 20, ens, gathered.reshape(partial.shape), transposed,
            specs=(VMEM,) * 3,
        )
    got_x, got_core = swap_x(to_x), swap_core(to_core)
    half = call(
        functools.partial(zonal_adjoint, lat_count, 0), shape(*half_shape), "adjoint0", 1 << 19,
        made["shift_core"], made["taps_v"], control_v, own_core, got_core,
        specs=(VMEM,) * 5, scratch=tap_room,
    )
    return call(
        functools.partial(zonal_adjoint, lat_count, 1), shape(*field_shape), "adjoint1", 1 << 19,
        made["shift_x"], made["taps_v"], control_v, own_x, got_x, half,
        specs=(VMEM,) * 6, scratch=tap_room,
    )


def solution(mesh):
    z_count = SLOTS if mesh.shape["mem"] == 2 * SLOTS else 0
    in_specs = (
        P("mem", None, "lat", None),
        P(None, None, "mem", None, "lat", None),
        P("mem", None, None, "lat", None),
        P(),
        P("lat"),
        P("lat", None),
        P("lat", None),
        P("lat", None, None),
    )
    out_specs = P("mem", None, "lat", None)
    return jax.shard_map(
        functools.partial(per_device, z_count),
        mesh=mesh, in_specs=in_specs, out_specs=out_specs, check_vma=False,
    )
```

```python
import functools

import jax
import jax.numpy as jnp
from jax import lax
from jax.experimental import pallas as pl
from jax.experimental.pallas import tpu as pltpu
from jax.sharding import PartitionSpec as P

SLOTS = 4
BAND = 17
HALF = BAND // 2
LANES = 128
F32 = jnp.float32
BF16 = jnp.bfloat16

VMEM = pl.BlockSpec(memory_space=pltpu.VMEM)
SMEM = pl.BlockSpec(memory_space=pltpu.SMEM)
ANY = pl.BlockSpec(memory_space=pl.ANY)
HBM = pl.BlockSpec(memory_space=pltpu.HBM)


def call(body, outs, name, cost, *operands, specs, scratch=(), after=()):
    count, extra = len(operands), len(after)

    def kernel(*refs):
        body(*refs[:count], *refs[count + extra :])

    return pl.pallas_call(
        kernel,
        out_shape=outs,
        in_specs=list(specs) + [ANY] * extra,
        out_specs=jax.tree.map(lambda _: VMEM, outs),
        scratch_shapes=list(scratch),
        compiler_params=pltpu.CompilerParams(vmem_limit_bytes=16 << 20),
        cost_estimate=pl.CostEstimate(flops=cost, bytes_accessed=cost, transcendentals=0),
        name=name,
    )(*operands, *after)


def parity():
    return lax.axis_index("lat") & 1


def own_y():
    return lax.axis_index("mem") & 1


def own_z():
    return lax.axis_index("mem") >> 1


def entry_at(owners, step, value):
    place = own_z() ^ step
    found = jnp.int32(0)
    for t in range(SLOTS):
        rank = jnp.int32(0)
        for u in range(SLOTS):
            if u != t:
                rank += jnp.where(owners[u] < owners[t], 1, 0)
        found = jnp.where(rank == place, value(t), found)
    return found


def slot_at(owners, step):
    return entry_at(owners, step, lambda t: jnp.int32(t))


def owner_at(owners, step):
    return entry_at(owners, step, lambda t: owners[t])


def shape(*dims, dtype=F32):
    return jax.ShapeDtypeStruct(dims, dtype)


def shifted(columns, amount):
    lane = lax.broadcasted_iota(jnp.int32, columns[0].shape, 1)
    turned = [pltpu.roll(c, amount, 1) for c in columns]
    return [
        jnp.where(lane < amount, turned[i - 1], turned[i]) for i in range(len(columns))
    ]


def circle_filter(columns, amount, tap):
    count = len(columns)
    lane = lax.broadcasted_iota(jnp.int32, columns[0].shape, 1)
    fine = amount & (LANES - 1)
    source = (lane - fine) & (LANES - 1)
    turned = [
        jnp.take_along_axis(c, source, axis=1, mode="promise_in_bounds") for c in columns
    ]
    wraps = lane < fine
    columns = [jnp.where(wraps, turned[i - 1], turned[i]) for i in range(count)]
    step = 1
    while step < count:
        moved = (amount & (step * LANES)) != 0
        columns = [jnp.where(moved, columns[i - step], columns[i]) for i in range(count)]
        step *= 2
    near = [columns]
    for offset in range(1, 4):
        near.append(shifted(columns, offset))
    total = [tap(BAND - 1) * c for c in columns]
    for group in range((BAND - 1) // 4 - 1, -1, -1):
        total = shifted(total, 4)
        for offset in range(4):
            factor = tap(4 * group + offset)
            total = [t + factor * c for t, c in zip(total, near[offset])]
    return total


def row_shifts(shifts, first):
    row = lax.broadcasted_iota(jnp.int32, (8, LANES), 0)
    amounts = jnp.zeros((8, LANES), jnp.int32)
    for r in range(8):
        amounts = jnp.where(row == r, shifts[first + r], amounts)
    return amounts


def spread_taps(taps, first, spread):
    block = taps[pl.ds(first, 8), :]
    for k in range(BAND):
        spread[k] = jnp.broadcast_to(block[:, k : k + 1], (8, LANES))


def tiles(width):
    return [slice(i * LANES, (i + 1) * LANES) for i in range(width // LANES)]


def half_start(which):
    odd = parity()
    return pl.multiple_of((1 - odd if which == 0 else odd) * 8, 8)


def zonal_forward(first, shifts, taps, control, out):
    members, levels, _, width = control.shape
    amount = (width - HALF - shifts[...]) & (width - 1)

    def step(m, carry):
        for l in range(levels):
            columns = [control[m, l, pl.ds(first, 8), cut] for cut in tiles(width)]
            result = circle_filter(columns, amount, lambda k: taps[BAND - 1 - k])
            for cut, value in zip(tiles(width), result):
                out[m, l, :, cut] = value
        return carry

    lax.fori_loop(0, members, step, 0)


def front_body(names, *refs):
    r = dict(zip(names, refs))
    sems = r["sems"]
    first_x, first_core = half_start(1), half_start(0)
    rows_x, rows_core = pl.ds(first_x, 8), pl.ds(first_core, 8)
    moves = [
        (r["shift"], r["shift_s"]),
        (r["taps"], r["taps_v"]),
        (r["control"].at[:, :, rows_x], r["control_v"].at[:, :, rows_x]),
    ]
    moves.append((r["control"].at[:, :, rows_core], r["control_v"].at[:, :, rows_core]))
    moves.append((r["meridional"], r["meridional_v"]))
    moves.append((r["mixing"], r["mixing_v"]))
    if "obs" in r:
        moves.append((r["obs"].at[0], r["obs_v"]))
    moves.append((r["ens"], r["ens_v"]))
    copies = [pltpu.make_async_copy(a, b, sems.at[i]) for i, (a, b) in enumerate(moves)]
    for copy in copies:
        copy.start()
    for copy in copies[:3]:
        copy.wait()
    r["shift_x"][...] = row_shifts(r["shift_s"], first_x)
    r["shift_core"][...] = row_shifts(r["shift_s"], first_core)
    spread_taps(r["taps_v"], first_x, r["taps_x"])
    zonal_forward(first_x, r["shift_x"], r["taps_x"], r["control_v"], r["near_x"])
    for copy in copies[3:]:
        copy.wait()


def core_body(shifts, taps_v, control, out, taps):
    first = half_start(0)
    spread_taps(taps_v, first, taps)
    zonal_forward(first, shifts, taps, control, out)


def zonal_adjoint(lat_count, which, shifts, taps_v, control, own, got, *refs):
    other, out, taps = (None, *refs) if which == 0 else refs
    members, levels, _, width = control.shape
    first = half_start(which)
    amount = (shifts[...] - HALF) & (width - 1)
    spread_taps(taps_v, first, taps)
    lat = lax.axis_index("lat")
    alone = (which == 1) & ((lat == 0) | (lat == lat_count - 1))

    def step(m, carry):
        for l in range(levels):
            columns = [
                own[m, l, :, cut] + jnp.where(alone, 0.0, got[m, l, :, cut])
                for cut in tiles(width)
            ]
            result = circle_filter(columns, amount, lambda k: taps[k])
            for cut, value in zip(tiles(width), result):
                total = control[m, l, pl.ds(first, 8), cut] + value
                if which == 0:
                    out[m, l, :, cut] = total
                else:
                    out[m, l, pl.ds(first, 8), cut] = total
                    out[m, l, pl.ds(8 - first, 8), cut] = other[m, l, :, cut]
        return carry

    lax.fori_loop(0, members, step, 0)


def build_matrix(lat_count, taps_ref, mixing_ref, matrix, transposed):
    band_rows, levels = taps_ref.shape[0], mixing_ref.shape[1]
    rows, columns = matrix.shape
    odd, lat = parity(), lax.axis_index("lat")
    alone = (lat == 0) | (lat == lat_count - 1)
    column = lax.broadcasted_iota(jnp.int32, (band_rows, columns), 1)
    row = lax.broadcasted_iota(jnp.int32, (band_rows, columns), 0)
    block, level, inner = column // (8 * levels), (column // 8) % levels, column % 8
    even_start = jnp.where(block == 0, 16, jnp.where(block == 1, 8, jnp.where(block == 2, 24, 0)))
    odd_start = jnp.where(block == 0, 8, jnp.where(block == 1, 16, jnp.where(block == 2, 0, 24)))
    reach = jnp.where(odd == 1, odd_start, even_start) + inner - row
    band = jnp.zeros((band_rows, columns), F32)
    for k in range(BAND):
        band = jnp.where(reach == k, taps_ref[:, k : k + 1], band)
    band = jnp.where((block == 3) & alone, 0.0, band)
    same = lax.broadcasted_iota(jnp.int32, (band_rows, band_rows), 0) == (
        lax.broadcasted_iota(jnp.int32, (band_rows, band_rows), 1)
    )
    for a in range(levels):
        mixing = mixing_ref[a]
        factor = jnp.zeros((band_rows, columns), F32)
        for b in range(levels):
            by_lane = jnp.broadcast_to(mixing[b : b + 1, :], (band_rows, band_rows))
            by_row = jnp.sum(jnp.where(same, by_lane, 0.0), axis=1, keepdims=True)
            factor = jnp.where(level == b, by_row, factor)
        matrix[a * band_rows : (a + 1) * band_rows, :] = factor * band
    transposed[...] = matrix[...].T


def halves(value):
    high = value.astype(BF16)
    return high, (value - high.astype(F32)).astype(BF16)


def product(left, right):
    (lh, ll), (rh, rl) = left, right
    dot = functools.partial(jnp.dot, preferred_element_type=F32)
    return dot(lh, rh) + (dot(lh, rl) + dot(ll, rh))


CHUNK = 512


def localize(matrix, parts, out):
    members, levels, band_rows, width = out.shape
    left = halves(matrix[...])
    for m in range(members):
        for c in range(0, width, CHUNK):
            cut = slice(c, c + CHUNK)
            stack = jnp.concatenate(
                [p[m, l, :, cut] for p in parts for l in range(levels)], axis=0
            )
            result = product(left, halves(stack))
            for l in range(levels):
                out[m, l, :, cut] = result[l * band_rows : (l + 1) * band_rows]


def delocalize(matrix, weighted, first, parts):
    members, levels, band_rows, width = weighted.shape
    rows = slice(first * levels * 8, (first + len(parts)) * levels * 8)
    left = halves(matrix[rows, :])
    for m in range(members):
        for c in range(0, width, CHUNK):
            cut = slice(c, c + CHUNK)
            stack = jnp.concatenate([weighted[m, l, :, cut] for l in range(levels)], axis=0)
            result = product(left, halves(stack))
            for p, part in enumerate(parts):
                for l in range(levels):
                    start = (p * levels + l) * 8
                    part[m, l, :, cut] = result[start : start + 8]


def blocks_body(first, matrix, weighted, *parts):
    delocalize(matrix, weighted, first, parts)


def increment(ens, localized, slot, field, l):
    total = None
    for m in range(localized.shape[0]):
        term = ens[slot, field, m, l].astype(F32) * localized[m, l]
        total = term if total is None else total + term
    return total


def weight_pick(owners, here, side, middle, mine, across):
    place = owner_at(owners, 0) >> 1
    for found, weights in (
        (place == own_z(), here),
        (place == own_z() ^ 1, side),
        (place == own_z() ^ 3, middle),
    ):

        @pl.when(found)
        def _(weights=weights):
            mine[...] = weights[own_y()]
            across[...] = weights[1 - own_y()]


def first_body(step, owners_hbm, matrix, a, b, c, d, ens, localized, send, owners, sem):
    copy = pltpu.make_async_copy(owners_hbm, owners, sem)
    copy.start()
    localize(matrix, (a, b, c, d), localized)
    copy.wait()
    slot = slot_at(owners, step)
    for l in range(localized.shape[1]):
        send[l] = increment(ens, localized, slot, 1 - own_y(), l)


def send_body(owners, ens, localized, three, one):
    for step, field, send in (
        (3, 1 - own_y(), three), (1, own_y(), one.at[0]), (1, 1 - own_y(), one.at[1])
    ):
        slot = slot_at(owners, step)
        for l in range(localized.shape[1]):
            send[l] = increment(ens, localized, slot, field, l)


def cross_body(owners, ens, localized, got, out):
    slot = slot_at(owners, 0)
    for l in range(localized.shape[1]):
        out[l] = increment(ens, localized, slot, 1 - own_y(), l) + got[1, l]


def meet_body(step, owners, ens, localized, got, out):
    slot = slot_at(owners, step)
    for l in range(localized.shape[1]):
        out[l] = increment(ens, localized, slot, own_y(), l) + got[l]


def last_body(owners, ens, localized, got_y, got_1, got_2, got_3, mine, from_y, out):
    slot = slot_at(owners, 0)
    held = (owner_at(owners, 0) & 1) == own_y()
    for here, weight in ((held, mine), (jnp.logical_not(held), from_y)):

        @pl.when(here)
        def _(weight=weight):
            for l in range(localized.shape[1]):
                out[l] = weight[l] * (
                    increment(ens, localized, slot, own_y(), l)
                    + got_y[l]
                    + (got_1[0, l] + got_2[l] + got_3[l])
                )


def spread_body(pieces, first, final, owners, ens, *refs):
    refs = list(refs)
    grads = [refs.pop(0) for _ in pieces]
    before = None if first else refs.pop(0)
    matrix = refs.pop(0) if final else None
    out = refs[-1] if final else refs[0]
    members, levels = out.shape[:2]
    places = [
        (slot_at(owners, step), 1 - own_y() if other else own_y()) for step, other in pieces
    ]
    for m in range(members):
        for l in range(levels):
            total = None if before is None else before[m, l]
            for (slot, field), grad in zip(places, grads):
                term = ens[slot, field, m, l].astype(F32) * grad[l]
                total = term if total is None else total + term
            out[m, l] = total
    if final:
        delocalize(matrix, out, 3, refs[:1])


def all_increments(ens, localized, out):
    for slot in range(out.shape[0]):
        for field in range(out.shape[1]):
            for l in range(out.shape[2]):
                out[slot, field, l] = increment(ens, localized, slot, field, l)


def localize_body(matrix, a, b, c, d, localized):
    localize(matrix, (a, b, c, d), localized)


def all_weighted(ens, grad, matrix, a, b, c, d, out):
    members, levels = out.shape[:2]
    for m in range(members):
        for l in range(levels):
            total = None
            for slot in range(ens.shape[0]):
                for field in range(ens.shape[1]):
                    term = ens[slot, field, m, l].astype(F32) * grad[slot, field, l]
                    total = term if total is None else total + term
            out[m, l] = total
    delocalize(matrix, out, 0, (a, b, c, d))


def per_device(
    z_count,
    control,
    perturbations,
    obs_weight,
    slot_owner,
    zonal_shift,
    zonal_taps,
    meridional_taps,
    level_mixing,
):
    members, levels, band_rows, width = control.shape
    mem_count, lat_count = lax.axis_size("mem"), lax.axis_size("lat")
    mem = lax.axis_index("mem")
    direct = z_count > 0
    field_shape = (members, levels, band_rows, width)
    half_shape = (members, levels, 8, width)
    piece = shape(levels, band_rows, width)
    core_pairs = [(i, i ^ 1) for i in range(lat_count)]
    x_swaps = [
        (m * lat_count + i, (m ^ 1) * lat_count + i)
        if i in (0, lat_count - 1)
        else (m * lat_count + i, m * lat_count + ((i - 1) ^ 1) + 1)
        for m in range(mem_count)
        for i in range(lat_count)
    ]
    swap_core = lambda v: lax.ppermute(v, "lat", core_pairs)
    swap_x = lambda v: lax.ppermute(v, ("mem", "lat"), x_swaps)
    tap_room = [pltpu.VMEM((BAND, 8, LANES), F32)]
    ins = {
        "shift": zonal_shift, "taps": zonal_taps, "control": control,
        "meridional": meridional_taps, "ens": perturbations,
        "mixing": jnp.transpose(level_mixing, (1, 2, 0)),
    }
    results = {
        "near_x": shape(*half_shape), "control_v": shape(*field_shape),
        "taps_v": shape(*zonal_taps.shape), "meridional_v": shape(*meridional_taps.shape),
        "shift_x": shape(8, LANES, dtype=jnp.int32),
        "shift_core": shape(8, LANES, dtype=jnp.int32),
        "ens_v": shape(*perturbations.shape, dtype=BF16),
        "mixing_v": shape(levels, levels, band_rows),
    }
    if direct:
        ins["obs"] = obs_weight
        results["obs_v"] = shape(*obs_weight.shape[1:])
    names = (*ins, *results, "taps_x", "shift_s", "sems")
    made = call(
        functools.partial(front_body, names), tuple(results.values()), "front", 1 << 19,
        *(pltpu.with_memory_space_constraint(v, pltpu.HBM) for v in ins.values()),
        specs=(HBM,) * len(ins),
        scratch=[
            *tap_room, pltpu.SMEM(zonal_shift.shape, jnp.int32), pltpu.SemaphoreType.DMA((8,)),
        ],
    )
    made = dict(zip(results, made))
    near_x, control_v, ens = made["near_x"], made["control_v"], made["ens_v"]
    far_x = swap_x(near_x)
    if direct:
        y_pairs = [(i, i ^ 1) for i in range(mem_count)]
        swap_y = lambda v: lax.ppermute(v, "mem", y_pairs)
        turn_z = lambda v, s: lax.ppermute(
            v, "mem", [(i, i ^ 2 * s) for i in range(mem_count)]
        )
        middle = [(i, i ^ 6) for i in range(2, mem_count - 2)]
        from_side = turn_z(made["obs_v"], 1)
        from_middle = lax.ppermute(made["obs_v"], "mem", middle)
    near_core = call(
        core_body, shape(*half_shape), "core", 1 << 19, made["shift_core"], made["taps_v"],
        control_v, specs=(VMEM,) * 3, scratch=tap_room,
    )
    far_core = swap_core(near_core)
    matrix, transposed = call(
        functools.partial(build_matrix, lat_count),
        (shape(levels * band_rows, 32 * levels), shape(32 * levels, levels * band_rows)),
        "matrix", 1 << 16, made["meridional_v"], made["mixing_v"], specs=(VMEM, VMEM), after=(near_core, far_x),
    )
    parts = (near_core, near_x, far_core, far_x)

    if direct:
        localized, first = call(
            functools.partial(first_body, 2), (shape(*field_shape), piece),
            "first", 1 << 20, slot_owner, matrix, *parts, ens,
            specs=(HBM,) + (VMEM,) * 6,
            scratch=[pltpu.SMEM((SLOTS,), jnp.int32), pltpu.SemaphoreType.DMA],
        )
        got_two = swap_y(first)
        three, one = call(
            send_body, (piece, shape(2, levels, band_rows, width)), "send", 1 << 20,
            slot_owner, ens, localized, specs=(SMEM, VMEM, VMEM), after=(from_side, from_middle),
        )

        def meet(s, got, after):
            return call(
                functools.partial(meet_body, s), piece, "meet%d" % s, 1 << 19,
                slot_owner, ens, localized, got, specs=(SMEM,) + (VMEM,) * 3, after=after,
            )

        three, got_two = lax.optimization_barrier((three, got_two))
        got_three = swap_y(three)
        two = meet(2, got_two, ())
        arrived = {2: turn_z(two, 2), 1: turn_z(one, 1)}
        mine, across = call(
            weight_pick, (piece,) * 2, "weight_pick", 1 << 18, slot_owner, made["obs_v"],
            from_side, from_middle, specs=(SMEM,) + (VMEM,) * 3, after=(two,),
        )
        three = meet(3, got_three, (two, across))
        arrived[3] = turn_z(three, 3)
        across, _ = lax.optimization_barrier((across, got_three))
        from_y = swap_y(across)
        cross = call(
            cross_body, piece, "cross", 1 << 19, slot_owner, ens, localized, arrived[1],
            specs=(SMEM,) + (VMEM,) * 3,
        )
        got_own = swap_y(cross)
        grad = call(
            last_body, piece, "last", 1 << 19, slot_owner, ens, localized, got_own,
            arrived[1], arrived[2], arrived[3], mine, from_y,
            specs=(SMEM,) + (VMEM,) * 8,
        )
        own = {0: grad, 3: turn_z(grad, 3)}
        weighted = call(
            functools.partial(spread_body, ((0, 0),), True, False), shape(*field_shape),
            "spread", 1 << 19, slot_owner, ens, grad, specs=(SMEM,) + (VMEM,) * 2,
        )
        other, weighted = lax.optimization_barrier((grad, weighted))
        other = {0: swap_y(other)}
        later, own[3], other[0], weighted = lax.optimization_barrier((grad, own[3], other[0], weighted))
        own[2] = turn_z(later, 2)
        along, near = lax.optimization_barrier((other[0], grad))
        own[1], other[1] = turn_z(near, 1), turn_z(along, 1)
        other.update({s: swap_y(own[s]) for s in (3, 2)})
        groups = (((0, 1), (1, 0), (3, 0)), ((1, 1), (3, 1), (2, 0)), ((2, 1),))
        for group in groups:
            final = group == groups[-1]
            grads = [other[s] if o else own[s] for s, o in group]
            pieces = tuple(group)
            extra = (transposed,) if final else ()
            result = call(
                functools.partial(spread_body, pieces, False, final),
                (shape(*half_shape), shape(*field_shape)) if final else shape(*field_shape),
                "spread%d" % group[0][0], 1 << 19,
                slot_owner, ens, *grads, weighted, *extra,
                specs=(SMEM,) + (VMEM,) * (2 + len(grads) + len(extra)),
            )
            weighted = result
        to_x, weighted = result
        own_core, own_x, to_core = call(
            functools.partial(blocks_body, 0), (shape(*half_shape),) * 3, "blocks", 1 << 19,
            transposed, weighted, specs=(VMEM,) * 2,
        )
    else:
        localized = call(
            localize_body, shape(*field_shape), "localize", 1 << 20, matrix, *parts,
            specs=(VMEM,) * 5,
        )
        partial = call(
            all_increments, shape(SLOTS, ens.shape[1], levels, band_rows, width),
            "increments", 1 << 20, ens, localized, specs=(VMEM,) * 2,
        )
        weights = jnp.stack(
            [
                lax.psum(jnp.where(mem == slot_owner[t], obs_weight[0], 0.0), "mem")
                for t in range(SLOTS)
            ]
        )
        share = lax.psum_scatter(
            partial.reshape(-1, width), "mem", scatter_dimension=0, tiled=True
        )
        share_rows = share.shape[0]
        weight_rows = lax.dynamic_slice_in_dim(
            weights.reshape(-1, width), mem * share_rows, share_rows, 0
        )
        gathered = lax.all_gather(weight_rows * share, "mem", axis=0, tiled=True)
        own_core, own_x, to_core, to_x, _ = call(
            all_weighted, (shape(*half_shape),) * 4 + (shape(*field_shape),), "weighted",
            1 << 20, ens, gathered.reshape(partial.shape), transposed,
            specs=(VMEM,) * 3,
        )
    got_x, got_core = swap_x(to_x), swap_core(to_core)
    half = call(
        functools.partial(zonal_adjoint, lat_count, 0), shape(*half_shape), "adjoint0", 1 << 19,
        made["shift_core"], made["taps_v"], control_v, own_core, got_core,
        specs=(VMEM,) * 5, scratch=tap_room,
    )
    return call(
        functools.partial(zonal_adjoint, lat_count, 1), shape(*field_shape), "adjoint1", 1 << 19,
        made["shift_x"], made["taps_v"], control_v, own_x, got_x, half,
        specs=(VMEM,) * 6, scratch=tap_room,
    )


def solution(mesh):
    z_count = SLOTS if mesh.shape["mem"] == 2 * SLOTS else 0
    in_specs = (
        P("mem", None, "lat", None),
        P(None, None, "mem", None, "lat", None),
        P("mem", None, None, "lat", None),
        P(),
        P("lat"),
        P("lat", None),
        P("lat", None),
        P("lat", None, None),
    )
    out_specs = P("mem", None, "lat", None)
    return jax.shard_map(
        functools.partial(per_device, z_count),
        mesh=mesh, in_specs=in_specs, out_specs=out_specs, check_vma=False,
    )
```
